32 devices in a mesh: row: 4 (over x, core), col: 8 (over z, y).
Axes of the slice: x: 2, y: 2, z: 4, core: 2. Of those that a mesh axis runs over, the one named last changes fastest.
Arguments:
- orbitals: float32 [128, 32, 1024], P(('row', 'col')), may hold values from -6 to 6
- gradient: float32 [128, 32, 1024], P(('row', 'col')), may hold values from -4 to 4
- offsets: int32 [128, 3], replicated, may hold values from 0 to 3
- pairs: int32 [32, 4, 2], P('row'), may hold values from 0 to 127, as said below
- counts: int32 [32], P('row'), may hold values from 1 to 4, as said below
Outputs:
- updated: float32 [128, 32, 1024], P(('row', 'col'))
- energies: float32 [2], replicated
The draws below stay inside these ranges and needn't reach their ends.
Inputs may be any that keep to these rules, and one draw needn't show every extreme that they name: `pairs`: both orbitals of a slot of pair owner p belong to p's group, ids g * 32 to (g + 1) * 32 - 1 with g = p // 8 (device d owns ids d * 4 onward). Among the live slots of one pair owner at most 2 distinct orbitals come from any one device, and every owner reaches 2 from some device. `counts`: every group of 8 pair owners has one owner with 4 live slots.
All inputs are finite; a program needn't handle non-finite values.
Results may differ from the reference program's by a relative error of at most 0.0082.
Values may be sent and summed in bfloat16 or wider, within the bound.
No kernel may reach another device: no remote copies, remote signals or barrier semaphores. Data moves between devices by JAX's collectives and lax.ppermute only.
A program may use at most 64 MiB of HBM per device.

```python
import jax
import jax.numpy as jnp
from jax import lax

BOX = 32
ORB_DEV = 4
PAIR_DEV = 4
CAP = 2
SHIFT = 4
SWEEPS = 12
ROUNDS = 2
GROUP_ORB = 32
NORB = 128
OWNERS = 32
N_ROW = 4
N_COL = 8


def draw_pairs(key, part):
    columns = GROUP_ORB // ORB_DEV
    pick_key = jax.random.fold_in(key, 11)
    slot_key = jax.random.fold_in(key, 12)
    source_key = jax.random.fold_in(key, 13)
    scores = jax.random.randint(pick_key, (OWNERS, columns, ORB_DEV), 0, 1 << 20) * ORB_DEV + jnp.arange(ORB_DEV)
    chosen = jnp.argsort(scores, axis=-1)[..., :CAP]
    candidates = (jnp.arange(columns)[None, :, None] * ORB_DEV + chosen).reshape(OWNERS, columns * CAP)
    picks = jax.random.randint(slot_key, (OWNERS, PAIR_DEV, 2), 0, columns * CAP)
    anchor = jax.random.randint(source_key, (OWNERS,), 0, columns) * CAP
    picks = picks.at[:, 0, 0].set(anchor).at[:, 0, 1].set(anchor + 1)
    local = jnp.take_along_axis(candidates, picks.reshape(OWNERS, PAIR_DEV * 2), axis=1).reshape(OWNERS, PAIR_DEV, 2)
    group_base = jnp.arange(OWNERS) // columns * GROUP_ORB
    return (local + group_base[:, None, None]).astype(jnp.int32)


def draw_counts(key, part):
    columns = GROUP_ORB // ORB_DEV
    groups = NORB // GROUP_ORB
    base_key = jax.random.fold_in(key, 21)
    full_key = jax.random.fold_in(key, 22)
    drawn = jax.random.randint(base_key, (OWNERS,), 1, PAIR_DEV // 2 + 1)
    busiest = jnp.arange(groups) * columns + jax.random.randint(full_key, (groups,), 0, columns)
    return drawn.at[busiest].set(PAIR_DEV).astype(jnp.int32)


def with_ends(values, own_key, least, high):
    shape = values.shape
    index_at = [jax.random.randint(jax.random.fold_in(own_key, axis), (), 0, shape[axis]) for axis in range(len(shape))]
    values = values.at[tuple(index_at)].set(least)
    longest = shape.index(max(shape))
    index_at[longest] = (index_at[longest] + 1) % shape[longest]
    return values.at[tuple(index_at)].set(high)


def shard_levels(own_key, dims, pieces, low, largest):
    factor_of, own = 1.0, jax.random.fold_in(own_key, 6)
    for dim, shards_of in pieces:
        draws = jnp.exp(jax.random.uniform(jax.random.fold_in(own, dim), (shards_of,), jnp.float32, low / len(pieces), largest / len(pieces)))
        factor_of = factor_of * jnp.repeat(draws, dims[dim] // shards_of).reshape([-1 if axis == dim else 1 for axis in range(len(dims))])
    return factor_of


def centred(rng, dims, width, most, split=(), kind=jnp.bfloat16):
    values = jax.random.normal(rng, dims, jnp.float32) * width
    if len(split) > 0:
        values = shard_levels(rng, dims, split, -0.22, 0.18) * values
    return jnp.clip(values, min=-most, max=most).astype(kind)


def setup_inputs(seed: int = 0) -> dict:
    splits = jax.random.split(jax.random.key(seed), 6)
    orbitals = centred(splits[0], (NORB, BOX, BOX * BOX), 1.0, 6.0, ((0, 32),), jnp.float32)
    gradient = centred(splits[1], (NORB, BOX, BOX * BOX), 0.5, 4.0, ((0, 32),), jnp.float32)
    offsets = with_ends(jax.random.randint(splits[2], (NORB, 3), 0, SHIFT), jax.random.fold_in(splits[2], 1), 0, SHIFT - 1).astype(jnp.int32)
    pairs = draw_pairs(jax.random.fold_in(splits[5], 71), 0)
    counts = draw_counts(jax.random.fold_in(splits[5], 71), 0)
    return dict(orbitals=orbitals, gradient=gradient, offsets=offsets, pairs=pairs, counts=counts)


screen_mu = 0.1
damping = 0.5


def sweep_table(sweeps):
    center_val = 6.0 + screen_mu
    half_width = 6.0
    ratio_val = center_val / half_width
    prev_coef = 1.0 / ratio_val
    keep_list = []
    mix_list = []
    for sweep_idx in range(sweeps):
        next_coef = 1.0 / (2.0 * ratio_val - prev_coef)
        keep_list.append(next_coef * prev_coef)
        mix_list.append(2.0 * next_coef / half_width)
        prev_coef = next_coef
    return jnp.array(keep_list, jnp.float32), jnp.array(mix_list, jnp.float32), 1.0 / center_val


def apply_operator(field):
    edge = field.shape[0]
    plane = field.shape[1]
    zero_row = jnp.zeros_like(field[:1])
    along_x = jnp.concatenate([field[1:], zero_row], 0) + jnp.concatenate([zero_row, field[:-1]], 0)
    zero_band = jnp.zeros_like(field[:, :edge])
    along_y = jnp.concatenate([field[:, edge:], zero_band], 1) + jnp.concatenate([zero_band, field[:, :-edge]], 1)
    zero_col = jnp.zeros_like(field[:, :1])
    depth = jnp.arange(plane) % edge
    upper = jnp.where(depth < edge - 1, jnp.concatenate([field[:, 1:], zero_col], 1), 0.0)
    lower = jnp.where(depth > 0, jnp.concatenate([zero_col, field[:, :-1]], 1), 0.0)
    return (6.0 + screen_mu) * field - (along_x + along_y + upper + lower)


def screened_solve(source, tables):
    keep_coef, mix_coef, first_coef = tables

    def sweep(index, state):
        solution, remainder, direction = state
        solution = solution + direction
        remainder = remainder - apply_operator(direction)
        direction = keep_coef[index] * direction + mix_coef[index] * remainder
        return solution, remainder, direction

    state = (jnp.zeros_like(source), source, source * first_coef)
    return lax.fori_loop(0, keep_coef.shape[0], sweep, state)[0]


def displaced(box, shift):
    edge = box.shape[0]
    reach = SHIFT - 1
    cube = jnp.pad(box.reshape(edge, edge, edge), reach)
    start = (shift + reach).astype(jnp.int32)
    moved = lax.dynamic_slice(cube, (start[0], start[1], start[2]), (edge, edge, edge))
    return moved.reshape(edge, edge * edge)


def run_pairs(boxes, source_of, slot_of, mine, mine_count, group_offsets, tables, slots):
    edge = boxes.shape[1]
    plane = boxes.shape[2]
    collected = jnp.zeros((slots, edge, plane), jnp.float32)

    def one_pair(index, state):
        gathered, energy = state
        first = mine[index, 0]
        second = mine[index, 1]
        shift = group_offsets[first] - group_offsets[second]
        box_i = lax.dynamic_index_in_dim(boxes, source_of[first], 0, False).astype(jnp.float32)
        box_j = displaced(lax.dynamic_index_in_dim(boxes, source_of[second], 0, False), shift).astype(jnp.float32)
        density = box_i * box_j
        potential = screened_solve(density, tables)
        term = potential * box_j
        target = slot_of[first]
        current = lax.dynamic_index_in_dim(gathered, target, 0, False)
        gathered = lax.dynamic_update_index_in_dim(gathered, current + term, target, 0)
        return gathered, energy + jnp.sum(density * potential)

    return lax.fori_loop(0, mine_count, one_pair, (collected, jnp.zeros((), jnp.float32)))


def reference(orbitals, gradient, offsets, pairs, counts):
    tables = sweep_table(SWEEPS)
    group = N_COL * ORB_DEV
    owners = N_ROW * N_COL
    orbit_ids = jnp.arange(group, dtype=jnp.int32)
    current = orbitals
    totals = []
    for round_idx in range(ROUNDS):
        boxes_all = current.astype(jnp.bfloat16)

        def per_owner(state, owner):
            field, energy = state
            base = ((owner // N_COL) * group).astype(jnp.int32)
            boxes = lax.dynamic_slice_in_dim(boxes_all, base, group, 0)
            group_offsets = lax.dynamic_slice_in_dim(offsets, base, group, 0)
            mine = (pairs[owner] - base).astype(jnp.int32)
            gathered, pair_energy = run_pairs(boxes, orbit_ids, orbit_ids, mine, counts[owner], group_offsets, tables, group)
            rounded = lax.optimization_barrier(gathered.astype(jnp.bfloat16)).astype(jnp.float32)
            previous = lax.dynamic_slice_in_dim(field, base, group, 0)
            field = lax.dynamic_update_slice_in_dim(field, previous + rounded, base, 0)
            return (field, energy + pair_energy), None

        start_state = (jnp.zeros_like(current), jnp.zeros((), jnp.float32))
        (field, energy), unused = lax.scan(per_owner, start_state, jnp.arange(owners, dtype=jnp.int32))
        totals.append(energy)
        current = current - damping * (gradient + field)
    energies = jnp.stack(totals) / (BOX * BOX * BOX * owners)
    return current, energies
```

```python
import functools

import jax
import jax.numpy as jnp
import numpy as np
from jax import lax
from jax.experimental import pallas as pl
from jax.experimental.pallas import tpu as pltpu
from jax.sharding import PartitionSpec as P

SWEEPS = 12
ROUNDS = 2
BATCH = 4
FIELDS = 8

screen_mu = 0.1
damping = 0.5

SMEM = pl.BlockSpec(memory_space=pltpu.SMEM)
VMEM = pl.BlockSpec(memory_space=pltpu.VMEM)


def split(values):
    high = values.astype(jnp.bfloat16)
    return high, (values - high.astype(jnp.float32)).astype(jnp.bfloat16)


def sine_basis(edge):
    index = np.arange(1, edge + 1)
    return np.sqrt(2.0 / (edge + 1)) * np.sin(np.pi * np.outer(index, index) / (edge + 1))


def solve_gain(edge):
    cosines = 2.0 * np.cos(np.pi * np.arange(1, edge + 1) / (edge + 1))
    eigen = 6.0 + screen_mu - (cosines[:, None, None] + cosines[None, :, None] + cosines[None, None, :])
    center, half = 6.0 + screen_mu, 6.0
    ratio = center / half
    prev = 1.0 / ratio
    gain, rest = np.zeros_like(eigen), np.ones_like(eigen)
    step = rest / center
    for _ in range(SWEEPS):
        gain = gain + step
        rest = rest - eigen * step
        coef = 1.0 / (2.0 * ratio - prev)
        step = coef * prev * step + (2.0 * coef / half) * rest
        prev = coef
    return gain.reshape(edge, edge * edge)


def dot(a, b):
    return jnp.dot(a, b, preferred_element_type=jnp.float32)


def capacity(mask, columns):
    return 2 if mask < columns // 2 else 1


def plan_kernel(dims, pairs, counts, offsets, phi, plist, meta, send_tab, boxes, *rest):
    columns, own, slots = dims
    sends, (seen, sent) = rest[: columns - 1], rest[columns - 1 :]
    group = columns * own
    owners = pairs.shape[0]
    me = lax.axis_index("col")
    base = lax.axis_index("row") * group
    for b in range(own):
        boxes[b] = phi[b].astype(jnp.bfloat16)

    def clear_seen(at, carry):
        for lane in range(8):
            seen[at * 8 + lane] = 0
        return carry

    lax.fori_loop(0, columns * group // 8, clear_seen, 0)

    def clear_sent(at, carry):
        sent[at] = 0
        return carry

    lax.fori_loop(0, columns * columns, clear_sent, 0)
    meta[0] = 0
    meta[1] = 1

    def owner_step(p, carry):
        def slot_step(k, carry):
            first = pairs[p, k, 0] - base
            second = pairs[p, k, 1] - base
            home = lax.div(first, own)
            source = lax.div(second, own)
            mask = home ^ source
            key = home * group + second

            @pl.when((mask != 0) & (seen[key] == 0))
            def _():
                rank = sent[home * columns + source] + 1
                sent[home * columns + source] = rank
                seen[key] = rank

            limit = jnp.where(mask < columns // 2, 2, 1)
            rank = jnp.maximum(seen[key] - 1, 0)
            chunk = lax.div(rank, limit)
            meta[1] = jnp.maximum(meta[1], chunk + 1)

            @pl.when(home == me)
            def _():
                at = meta[0] * FIELDS
                meta[0] = meta[0] + 1
                plist[at] = first - me * own
                plist[at + 1] = mask
                plist[at + 2] = jnp.where(mask == 0, second - me * own, rank - chunk * limit)
                plist[at + 3] = chunk
                for axis in range(3):
                    plist[at + 4 + axis] = offsets[first + base, axis] - offsets[second + base, axis]

            return carry

        return lax.fori_loop(0, jnp.minimum(counts[p], slots), slot_step, carry)

    lax.fori_loop(0, owners, owner_step, 0)
    for mask in range(1, columns):
        for b in range(own):
            send_tab[mask * own + b] = seen[(me ^ mask) * group + me * own + b]
    fill_sends(columns, own, 0, send_tab, boxes, sends)


def fill_sends(columns, own, chunk, send_tab, boxes, sends):
    for mask in range(1, columns):
        limit = capacity(mask, columns)
        for b in range(own):
            rank = send_tab[mask * own + b] - 1 - chunk * limit

            @pl.when((rank >= 0) & (rank < limit))
            def _():
                sends[mask - 1][rank] = boxes[b]


def pack_kernel(dims, step, send_tab, phi, boxes, *sends):
    columns, own = dims
    for b in range(own):
        boxes[b] = phi[b].astype(jnp.bfloat16)
    fill_sends(columns, own, step[0], send_tab, boxes, sends)


def shifted(box, move):
    edge, plane = box.shape
    along_x, along_y, along_z = move
    flat = along_y * edge + along_z
    out = pltpu.roll(box, lax.rem(edge - along_x, edge), 0)
    out = pltpu.roll(out, lax.rem(plane - flat, plane), 1)
    row = lax.broadcasted_iota(jnp.int32, (edge, plane), 0) + along_x
    lane = lax.broadcasted_iota(jnp.int32, (edge, plane), 1)
    depth = (lane & (edge - 1)) + along_z
    lane = lane + (along_y * edge)
    keep = (row >= 0) & (row < edge) & (lane >= 0) & (lane < plane) & (depth >= 0) & (depth < edge)
    return jnp.where(keep, out, 0.0)


def pair_kernel(dims, with_gradient, step, plist, meta, boxes, base, gradient, basis_hi, basis_lo, left_hi, left_lo, gain, *rest):
    columns, own = dims
    recvs, (out, energy, partner, density, source, total) = rest[: columns - 1], rest[columns - 1 :]
    edge, plane = gain.shape
    for b in range(own):
        out[b] = base[b] - damping * gradient[b] if with_gradient else base[b]
    total[...] = jnp.zeros_like(total)
    count = meta[0]
    chunk = step[0]

    def along_left(values):
        high, low = split(values)
        return dot(left_hi[...], high) + (dot(left_hi[...], low) + dot(left_lo[...], high))

    def along_right(values):
        high, low = split(values)
        both = dot(jnp.concatenate([high, low], 0), basis_hi[...])
        rows = values.shape[0]
        return both[:rows] + (both[rows:] + dot(high, basis_lo[...]))

    def batch_step(index, carry):
        for s in range(BATCH):
            pair = index * BATCH + s
            at = jnp.minimum(pair, count - 1) * FIELDS
            live = (pair < count) & (plist[at + 3] == chunk)
            rows = pl.ds(s * edge, edge)

            @pl.when(live)
            def _():
                mask = plist[at + 1]
                place = plist[at + 2]

                @pl.when(mask == 0)
                def _():
                    source[...] = boxes[place].astype(jnp.float32)

                for m in range(1, columns):

                    @pl.when(mask == m)
                    def _():
                        source[...] = recvs[m - 1][place].astype(jnp.float32)

                other = shifted(source[...], (plist[at + 4], plist[at + 5], plist[at + 6]))
                partner[rows, :] = other
                density[rows, :] = boxes[plist[at]].astype(jnp.float32) * other

            @pl.when(jnp.logical_not(live))
            def _():
                density[rows, :] = jnp.zeros((edge, plane), jnp.float32)

        spectrum = along_right(along_left(density[...]))
        scaled = (spectrum.reshape(BATCH, edge, plane) * gain[...]).reshape(BATCH * edge, plane)
        potential = along_left(along_right(scaled))
        work = density[...] * potential
        total[...] += jnp.sum(work.reshape(BATCH * edge // 8, 8, plane), 0)
        for s in range(BATCH):
            pair = index * BATCH + s
            at = jnp.minimum(pair, count - 1) * FIELDS
            live = (pair < count) & (plist[at + 3] == chunk)

            @pl.when(live)
            def _():
                rows = slice(s * edge, (s + 1) * edge)
                place = plist[at]
                out[place] = out[place] - damping * (potential[rows] * partner[rows, :])

        return carry

    lax.fori_loop(0, lax.div(count + BATCH - 1, BATCH), batch_step, 0)
    energy[...] = jnp.full(energy.shape, jnp.sum(total[...]))


def local(orbitals, gradient, offsets, pairs, counts):
    own, edge, plane = orbitals.shape
    columns = lax.axis_size("col")
    rows = lax.axis_size("row")
    owners, slots = pairs.shape[0], pairs.shape[1]
    group = columns * own
    masks = range(1, columns)
    basis = sine_basis(edge)
    basis_hi, basis_lo = split(jnp.asarray(np.kron(basis, basis), jnp.float32))
    left_hi, left_lo = split(jnp.asarray(np.kron(np.eye(BATCH), basis), jnp.float32))
    gain = jnp.asarray(solve_gain(edge), jnp.float32)
    box_shape = jax.ShapeDtypeStruct((own, edge, plane), jnp.bfloat16)
    send_shapes = [jax.ShapeDtypeStruct((capacity(m, columns), edge, plane), jnp.bfloat16) for m in masks]

    def ints(size):
        return jax.ShapeDtypeStruct((size,), jnp.int32)

    plist, meta, send_tab, boxes, *sends = pl.pallas_call(
        functools.partial(plan_kernel, (columns, own, slots)),
        out_shape=[ints(owners * slots * FIELDS), ints(8), ints(columns * own), box_shape, *send_shapes],
        in_specs=[SMEM, SMEM, SMEM, VMEM],
        out_specs=[SMEM, SMEM, SMEM, VMEM] + [VMEM] * len(send_shapes),
        scratch_shapes=[pltpu.SMEM((columns * group,), jnp.int32), pltpu.SMEM((columns * columns,), jnp.int32)],
        name="plan",
    )(pairs, counts, offsets, orbitals)

    def pack(step, phi):
        boxes, *sends = pl.pallas_call(
            functools.partial(pack_kernel, (columns, own)),
            out_shape=[box_shape, *send_shapes],
            in_specs=[SMEM, SMEM, VMEM],
            out_specs=[VMEM] * (1 + len(send_shapes)),
            name="pack",
        )(step, send_tab, phi)
        return boxes, sends

    def exchange(sends):
        got = {}
        for m in reversed(masks):
            got[m] = lax.ppermute(sends[m - 1], "col", [(c, c ^ m) for c in range(columns)])
        return [got[m] for m in masks]

    def compute(step, with_gradient, boxes, base, recvs):
        out, energy = pl.pallas_call(
            functools.partial(pair_kernel, (columns, own), with_gradient),
            out_shape=[jax.ShapeDtypeStruct((own, edge, plane), jnp.float32), jax.ShapeDtypeStruct((8, 128), jnp.float32)],
            in_specs=[SMEM] * 3 + [VMEM] * (8 + len(recvs)),
            out_specs=[VMEM, VMEM],
            scratch_shapes=[
                pltpu.VMEM((BATCH * edge, plane), jnp.float32),
                pltpu.VMEM((BATCH * edge, plane), jnp.float32),
                pltpu.VMEM((edge, plane), jnp.float32),
                pltpu.VMEM((8, plane), jnp.float32),
            ],
            name="pairs",
        )(step, plist, meta, boxes, base, gradient, basis_hi, basis_lo, left_hi, left_lo, gain, *recvs)
        return out, energy

    zero = jnp.zeros((1,), jnp.int32)
    current = orbitals
    totals = []
    for round_idx in range(ROUNDS):
        if round_idx > 0:
            boxes, sends = pack(zero, current)
        before = current
        current, energy = compute(zero, True, boxes, current, exchange(sends))

        def further(index, state, before=before):
            current, energy = state
            step = jnp.full((1,), index, jnp.int32)
            boxes, sends = pack(step, before)
            current, more = compute(step, False, boxes, current, exchange(sends))
            return current, energy + more

        current, energy = lax.fori_loop(1, meta[1], further, (current, energy))
        totals.append(energy[0, 0])
    devices = rows * columns
    mine = jnp.concatenate([jnp.stack(totals), jnp.zeros((128 - ROUNDS,), jnp.float32)])
    every = lax.all_to_all(jnp.broadcast_to(mine, (devices, 128)), ("row", "col"), 0, 0, tiled=True)
    energies = jnp.sum(every, 0)[:ROUNDS] / (edge * edge * edge * devices)
    return current, energies


def solution(mesh):
    return jax.shard_map(
        local,
        mesh=mesh,
        in_specs=(
            P(("row", "col"), None, None),
            P(("row", "col"), None, None),
            P(),
            P("row", None, None),
            P("row"),
        ),
        out_specs=(P(("row", "col"), None, None), P()),
        check_vma=False,
    )
```

```python
import functools

import jax
import jax.numpy as jnp
import numpy as np
from jax import lax
from jax.experimental import pallas as pl
from jax.experimental.pallas import tpu as pltpu
from jax.sharding import PartitionSpec as P

SWEEPS = 12
ROUNDS = 2
BATCH = 4
FIELDS = 8

screen_mu = 0.1
damping = 0.5

SMEM = pl.BlockSpec(memory_space=pltpu.SMEM)
VMEM = pl.BlockSpec(memory_space=pltpu.VMEM)
ANY = pl.BlockSpec(memory_space=pl.ANY)


def split(values):
    high = values.astype(jnp.bfloat16)
    return high, (values - high.astype(jnp.float32)).astype(jnp.bfloat16)


def sine_basis(edge):
    index = np.arange(1, edge + 1)
    return np.sqrt(2.0 / (edge + 1)) * np.sin(np.pi * np.outer(index, index) / (edge + 1))


def solve_gain(edge):
    cosines = 2.0 * np.cos(np.pi * np.arange(1, edge + 1) / (edge + 1))
    eigen = 6.0 + screen_mu - (cosines[:, None, None] + cosines[None, :, None] + cosines[None, None, :])
    center, half = 6.0 + screen_mu, 6.0
    ratio = center / half
    prev = 1.0 / ratio
    gain, rest = np.zeros_like(eigen), np.ones_like(eigen)
    step = rest / center
    for _ in range(SWEEPS):
        gain = gain + step
        rest = rest - eigen * step
        coef = 1.0 / (2.0 * ratio - prev)
        step = coef * prev * step + (2.0 * coef / half) * rest
        prev = coef
    return gain.reshape(edge, edge * edge)


def dot(a, b):
    return jnp.dot(a, b, preferred_element_type=jnp.float32)


def capacity(mask, columns):
    return 2 if mask < columns // 2 else 1


def bits(word, size):
    return [(word >> b) & 1 for b in range(size)]


def owner_of(orbital, own):
    return orbital >> (own.bit_length() - 1) if own & (own - 1) == 0 else lax.div(orbital, own)


def each_pair(pairs, counts, slots, base, step):
    def owner_step(p, carry):
        def slot_step(k, carry):
            step(p, k, pairs[k, 0, p] - base, pairs[k, 1, p] - base)
            return carry

        return lax.fori_loop(0, jnp.minimum(counts[p], slots), slot_step, carry)

    lax.fori_loop(0, counts.shape[0], owner_step, 0)


def pack(columns, own, me, need, boxes, sends):
    for mask in range(1, columns):
        limit = capacity(mask, columns)
        rank = 0
        for b, bit in enumerate(bits(need[(me ^ mask) * columns + me], own)):
            place = rank if limit > 1 else 0

            @pl.when((bit != 0) & (rank < limit))
            def _():
                sends[mask - 1][place] = boxes[b]

            rank = rank + bit


def need_kernel(dims, pairs, counts, phi, need, boxes, *sends):
    columns, own, slots = dims
    me = lax.axis_index("col")
    base = lax.axis_index("row") * (columns * own)

    def clear(at, carry):
        for lane in range(columns):
            need[at * columns + lane] = 0
        return carry

    lax.fori_loop(0, columns, clear, 0)

    def step(p, k, first, second):
        source = owner_of(second, own)
        key = owner_of(first, own) * columns + source
        need[key] = need[key] | (1 << (second - source * own))

    each_pair(pairs, counts, slots, base, step)
    for b in range(own):
        boxes[b] = phi[b].astype(jnp.bfloat16)
    pack(columns, own, me, need, boxes, sends)


def plan_kernel(dims, need, pairs, counts, offsets, plist, meta, extra_mask, extra_box, unset, start):
    columns, own, slots = dims
    del unset
    me = lax.axis_index("col")
    base = lax.axis_index("row") * (columns * own)
    meta[0] = 0
    meta[1] = 0
    for mask in range(1, columns):
        limit = capacity(mask, columns)
        start[mask] = meta[1]
        mine = bits(need[(me ^ mask) * columns + me], own)

        def most(c, carry):
            return jnp.maximum(carry, sum(bits(need[c * columns + (c ^ mask)], own)))

        longest = lax.fori_loop(0, columns, most, 0)
        for over in range(own - limit):

            @pl.when(longest > limit + over)
            def _():
                at = meta[1]
                meta[1] = at + 1
                rank, box = 0, 0
                for b, bit in enumerate(mine):
                    box = jnp.where((bit != 0) & (rank == limit + over), b, box)
                    rank = rank + bit
                extra_mask[at] = mask - 1
                extra_box[at] = box

    def step(p, k, first, second):
        @pl.when(owner_of(first, own) == me)
        def _():
            source = owner_of(second, own)
            mask = me ^ source
            place = second - source * own
            rank = sum(bits(need[me * columns + source] & ((1 << place) - 1), own))
            limit = jnp.where(mask < columns // 2, 2, 1)
            fits = rank < limit
            at = meta[0] * FIELDS
            meta[0] = meta[0] + 1
            plist[at] = first - me * own
            plist[at + 1] = jnp.where((mask == 0) | fits, mask, columns)
            plist[at + 2] = jnp.where(mask == 0, place, jnp.where(fits, rank, start[mask] + rank - limit))
            for axis in range(3):
                plist[at + 3 + axis] = offsets[axis, first + base] - offsets[axis, second + base]
            opens, closes = jnp.int32(1), jnp.int32(1)
            for other in range(slots):
                same = (other < counts[p]) & (pairs[other, 0, p] - base == first)
                opens = jnp.where(same & (other < k), 0, opens)
                closes = jnp.where(same & (other > k), 0, closes)
            plist[at + 6] = opens
            plist[at + 7] = closes

    each_pair(pairs, counts, slots, base, step)


def shifted(box, move):
    edge, plane = box.shape
    along_x, along_y, along_z = move
    flat = along_y * edge + along_z
    out = pltpu.roll(box, lax.rem(edge - along_x, edge), 0)
    out = pltpu.roll(out, lax.rem(plane - flat, plane), 1)
    row = lax.broadcasted_iota(jnp.int32, (edge, plane), 0) + along_x
    lane = lax.broadcasted_iota(jnp.int32, (edge, plane), 1)
    depth = (lane & (edge - 1)) + along_z
    lane = lane + (along_y * edge)
    keep = (row >= 0) & (row < edge) & (lane >= 0) & (lane < plane) & (depth >= 0) & (depth < edge)
    return jnp.where(keep, out, 0.0)


def pair_kernel(dims, plist, meta, need, before, boxes, base, gradient, left_hi, left_lo, gain, basis_hi, basis_lo, extra, *rest):
    columns, own, last = dims
    recvs, rest = rest[: columns - 1], rest[columns - 1 :]
    if last:
        out, energy = rest[:2]
    else:
        out, energy, next_boxes = rest[:3]
        sends = rest[3:-9]
    right_hi, right_lo, sems, partner, density, source, running, total, box_sem = rest[-9:]
    edge, plane = gain.shape
    copies = [
        pltpu.make_async_copy(basis_hi, right_hi, sems.at[0]),
        pltpu.make_async_copy(basis_lo, right_lo, sems.at[1]),
    ]
    for copy in copies:
        copy.start()
    for b in range(own):
        out[b] = base[b] - damping * gradient[b]
    total[...] = jnp.zeros_like(total)
    count = meta[0]

    def along_left(values):
        high, low = split(values)
        return dot(left_hi[...], high) + (dot(left_hi[...], low) + dot(left_lo[...], high))

    def along_right(values):
        high, low = split(values)
        both = dot(jnp.concatenate([high, low], 0), right_hi[...])
        rows = values.shape[0]
        return both[:rows] + (both[rows:] + dot(high, right_lo[...]))

    def batch_step(index, carry):
        for s in range(BATCH):
            pair = index * BATCH + s
            rows = pl.ds(s * edge, edge)

            @pl.when(pair < count)
            def _():
                at = pair * FIELDS
                code = plist[at + 1]
                place = plist[at + 2]

                @pl.when(code == 0)
                def _():
                    source[...] = boxes[place]

                for m in range(1, columns):

                    @pl.when(code == m)
                    def _():
                        source[...] = recvs[m - 1][place if capacity(m, columns) > 1 else 0]

                @pl.when(code == columns)
                def _():
                    copy = pltpu.make_async_copy(extra.at[place], source, box_sem)
                    copy.start()
                    copy.wait()

                other = shifted(source[...].astype(jnp.float32), (plist[at + 3], plist[at + 4], plist[at + 5]))
                partner[rows, :] = other
                density[rows, :] = boxes[plist[at]].astype(jnp.float32) * other

            @pl.when(pair >= count)
            def _():
                density[rows, :] = jnp.zeros((edge, plane), jnp.float32)

        @pl.when(index == 0)
        def _():
            for copy in copies:
                copy.wait()

        spectrum = along_right(along_left(density[...]))
        scaled = (spectrum.reshape(BATCH, edge, plane) * gain[...]).reshape(BATCH * edge, plane)
        potential = along_left(along_right(scaled))
        work = density[...] * potential
        total[...] += jnp.sum(work.reshape(BATCH * edge // 8, 8, plane), 0)
        for s in range(BATCH):
            pair = index * BATCH + s

            @pl.when(pair < count)
            def _():
                at = pair * FIELDS
                place = plist[at]
                rows = slice(s * edge, (s + 1) * edge)
                running[rows, :] = potential[rows] * partner[rows, :]

                @pl.when(plist[at + 6] == 0)
                def _():
                    running[rows, :] = running[rows, :] + partial(place)[...]

                @pl.when(plist[at + 7] == 0)
                def _():
                    partial(place)[...] = running[rows, :]

                @pl.when(plist[at + 7] != 0)
                def _():
                    rounded = running[rows, :].astype(jnp.bfloat16).astype(jnp.float32)
                    out[place] = out[place] - damping * rounded

        return carry

    def partial(place):
        return running.at[pl.ds(pl.multiple_of((BATCH + place) * edge, edge), edge)]

    lax.fori_loop(0, lax.div(count + BATCH - 1, BATCH), batch_step, 0)

    @pl.when(count == 0)
    def _():
        for copy in copies:
            copy.wait()

    mine = jnp.sum(total[...])
    if last:
        lane = lax.broadcasted_iota(jnp.int32, (1, 128), 1)
        row = jnp.where(lane == 0, before[:1], jnp.where(lane == 1, mine, 0.0))
        for device in range(energy.shape[0]):
            energy[device] = row
    else:
        energy[...] = jnp.full(energy.shape, mine)
        for b in range(own):
            next_boxes[b] = out[b].astype(jnp.bfloat16)
        pack(columns, own, lax.axis_index("col"), need, next_boxes, sends)


def local(orbitals, gradient, offsets, pairs, counts):
    own, edge, plane = orbitals.shape
    columns = lax.axis_size("col")
    devices = lax.axis_size("row") * columns
    owners, slots = pairs.shape[0], pairs.shape[1]
    masks = range(1, columns)
    basis = sine_basis(edge)
    basis_hi, basis_lo = split(jnp.asarray(np.kron(basis, basis), jnp.float32))
    left_hi, left_lo = split(jnp.asarray(np.kron(np.eye(BATCH), basis), jnp.float32))
    gain = jnp.asarray(solve_gain(edge), jnp.float32)
    box_shape = jax.ShapeDtypeStruct((own, edge, plane), jnp.bfloat16)
    send_shapes = [jax.ShapeDtypeStruct((capacity(m, columns), edge, plane), jnp.bfloat16) for m in masks]
    most_extra = sum(max(own - capacity(m, columns), 0) for m in masks)
    pairs = pairs.transpose(1, 2, 0)
    offsets = offsets.T

    def ints(size):
        return jax.ShapeDtypeStruct((size,), jnp.int32)

    need, boxes, *sends = pl.pallas_call(
        functools.partial(need_kernel, (columns, own, slots)),
        out_shape=[ints(columns * columns), box_shape, *send_shapes],
        in_specs=[SMEM, SMEM, VMEM],
        out_specs=[SMEM, VMEM] + [VMEM] * len(send_shapes),
        name="need",
    )(pairs, counts, orbitals)
    plist, meta, extra_mask, extra_box, extra = pl.pallas_call(
        functools.partial(plan_kernel, (columns, own, slots)),
        out_shape=[
            ints(owners * slots * FIELDS),
            ints(8),
            ints(most_extra),
            ints(most_extra),
            jax.ShapeDtypeStruct((most_extra, edge, plane), jnp.bfloat16),
        ],
        in_specs=[SMEM] * 4,
        out_specs=[SMEM] * 4 + [ANY],
        scratch_shapes=[pltpu.SMEM((columns,), jnp.int32)],
        name="plan",
    )(need, pairs, counts, offsets)

    def hop(mask, values):
        return lax.ppermute(values, "col", [(c, c ^ mask) for c in range(columns)])

    def exchange(boxes, sends, extra):
        got = {m: hop(m, sends[m - 1]) for m in reversed(masks)}

        def one_more(at, extra):
            box = lax.dynamic_index_in_dim(boxes, extra_box[at], 0, True)
            box = lax.switch(extra_mask[at], [functools.partial(hop, m) for m in masks], box)
            return lax.dynamic_update_slice_in_dim(extra, box, at, 0)

        extra = lax.fori_loop(0, meta[1], one_more, extra)
        return [got[m] for m in masks], extra

    current = orbitals
    energy = jnp.zeros((8, 128), jnp.float32)
    for round_idx in range(ROUNDS):
        last = round_idx == ROUNDS - 1
        recvs, extra = exchange(boxes, sends, extra)
        energy_shape = (devices, 1, 128) if last else (8, 128)
        out_shape = [jax.ShapeDtypeStruct((own, edge, plane), jnp.float32), jax.ShapeDtypeStruct(energy_shape, jnp.float32)]
        if not last:
            out_shape += [box_shape, *send_shapes]
        current, energy, *rest = pl.pallas_call(
            functools.partial(pair_kernel, (columns, own, last)),
            out_shape=out_shape,
            in_specs=[SMEM] * 3 + [VMEM] * 7 + [ANY] * 3 + [VMEM] * len(recvs),
            out_specs=[VMEM] * len(out_shape),
            scratch_shapes=[
                pltpu.VMEM((plane, plane), jnp.bfloat16),
                pltpu.VMEM((plane, plane), jnp.bfloat16),
                pltpu.SemaphoreType.DMA((2,)),
                pltpu.VMEM((BATCH * edge, plane), jnp.float32),
                pltpu.VMEM((BATCH * edge, plane), jnp.float32),
                pltpu.VMEM((edge, plane), jnp.bfloat16),
                pltpu.VMEM(((BATCH + own) * edge, plane), jnp.float32),
                pltpu.VMEM((8, plane), jnp.float32),
                pltpu.SemaphoreType.DMA,
            ],
            name="pairs",
        )(plist, meta, need, energy, boxes, current, gradient, left_hi, left_lo, gain, basis_hi, basis_lo, extra, *recvs)
        if not last:
            boxes, *sends = rest
    every = lax.all_to_all(energy, ("row", "col"), 0, 0, tiled=True)
    energies = jnp.sum(every, (0, 1))[:ROUNDS] / (edge * edge * edge * devices)
    return current, energies


def solution(mesh):
    return jax.shard_map(
        local,
        mesh=mesh,
        in_specs=(
            P(("row", "col"), None, None),
            P(("row", "col"), None, None),
            P(),
            P("row", None, None),
            P("row"),
        ),
        out_specs=(P(("row", "col"), None, None), P()),
        check_vma=False,
    )
```

```python
import functools

import jax
import jax.numpy as jnp
import numpy as np
from jax import lax
from jax.experimental import pallas as pl
from jax.experimental.pallas import tpu as pltpu
from jax.sharding import PartitionSpec as P

SWEEPS = 12
ROUNDS = 2
BATCH = 4
FIELDS = 8

screen_mu = 0.1
damping = 0.5

SMEM = pl.BlockSpec(memory_space=pltpu.SMEM)
VMEM = pl.BlockSpec(memory_space=pltpu.VMEM)
ANY = pl.BlockSpec(memory_space=pl.ANY)
GRANT = pltpu.CompilerParams(vmem_limit_bytes=24 * 2**20)


def split(values):
    high = values.astype(jnp.bfloat16)
    return high, (values - high.astype(jnp.float32)).astype(jnp.bfloat16)


def sine_basis(edge):
    index = np.arange(1, edge + 1)
    return np.sqrt(2.0 / (edge + 1)) * np.sin(np.pi * np.outer(index, index) / (edge + 1))


def solve_gain(edge):
    cosines = 2.0 * np.cos(np.pi * np.arange(1, edge + 1) / (edge + 1))
    eigen = 6.0 + screen_mu - (cosines[:, None, None] + cosines[None, :, None] + cosines[None, None, :])
    center, half = 6.0 + screen_mu, 6.0
    ratio = center / half
    prev = 1.0 / ratio
    gain, rest = np.zeros_like(eigen), np.ones_like(eigen)
    step = rest / center
    for _ in range(SWEEPS):
        gain = gain + step
        rest = rest - eigen * step
        coef = 1.0 / (2.0 * ratio - prev)
        step = coef * prev * step + (2.0 * coef / half) * rest
        prev = coef
    return gain.reshape(edge, edge * edge)


def dot(a, b):
    return jnp.dot(a, b, preferred_element_type=jnp.float32)


def capacity(mask, columns):
    return 2 if mask < columns // 2 else 1


def bits(word, size):
    return [(word >> b) & 1 for b in range(size)]


def owner_of(orbital, own):
    return orbital >> (own.bit_length() - 1) if own & (own - 1) == 0 else lax.div(orbital, own)


def each_pair(pairs, counts, slots, base, step):
    def owner_step(p, carry):
        def slot_step(k, carry):
            step(p, k, pairs[k, 0, p] - base, pairs[k, 1, p] - base)
            return carry

        return lax.fori_loop(0, jnp.minimum(counts[p], slots), slot_step, carry)

    lax.fori_loop(0, counts.shape[0], owner_step, 0)


def pack(columns, own, me, need, boxes, sends):
    for mask in range(1, columns):
        limit = capacity(mask, columns)
        rank = 0
        for b, bit in enumerate(bits(need[(me ^ mask) * columns + me], own)):
            place = rank if limit > 1 else 0

            @pl.when((bit != 0) & (rank < limit))
            def _():
                sends[mask - 1][place] = boxes[b]

            rank = rank + bit


def need_kernel(dims, pairs, counts, phi, need, boxes, *sends):
    columns, own, slots = dims
    me = lax.axis_index("col")
    base = lax.axis_index("row") * (columns * own)

    def clear(at, carry):
        for lane in range(columns):
            need[at * columns + lane] = 0
        return carry

    lax.fori_loop(0, columns, clear, 0)

    def step(p, k, first, second):
        source = owner_of(second, own)
        key = owner_of(first, own) * columns + source
        need[key] = need[key] | (1 << (second - source * own))

    each_pair(pairs, counts, slots, base, step)
    for b in range(own):
        boxes[b] = phi[b].astype(jnp.bfloat16)
    pack(columns, own, me, need, boxes, sends)


def plan_kernel(dims, need, pairs, counts, offsets, plist, meta, extra_count, extra_mask, extra_box, unset, start):
    columns, own, slots = dims
    del unset
    me = lax.axis_index("col")
    base = lax.axis_index("row") * (columns * own)
    meta[0] = 0
    extra_count[0] = 0
    for mask in range(1, columns):
        limit = capacity(mask, columns)
        start[mask] = extra_count[0]
        mine = bits(need[(me ^ mask) * columns + me], own)

        def most(c, carry):
            return jnp.maximum(carry, sum(bits(need[c * columns + (c ^ mask)], own)))

        longest = lax.fori_loop(0, columns, most, 0)
        for over in range(own - limit):

            @pl.when(longest > limit + over)
            def _():
                at = extra_count[0]
                extra_count[0] = at + 1
                rank, box = 0, 0
                for b, bit in enumerate(mine):
                    box = jnp.where((bit != 0) & (rank == limit + over), b, box)
                    rank = rank + bit
                extra_mask[at] = mask - 1
                extra_box[at] = box

    def step(p, k, first, second):
        @pl.when(owner_of(first, own) == me)
        def _():
            source = owner_of(second, own)
            mask = me ^ source
            place = second - source * own
            rank = sum(bits(need[me * columns + source] & ((1 << place) - 1), own))
            limit = jnp.where(mask < columns // 2, 2, 1)
            fits = rank < limit
            at = meta[0] * FIELDS
            meta[0] = meta[0] + 1
            plist[at] = first - me * own
            plist[at + 1] = jnp.where((mask == 0) | fits, mask, columns)
            plist[at + 2] = jnp.where(mask == 0, place, jnp.where(fits, rank, start[mask] + rank - limit))
            for axis in range(3):
                plist[at + 3 + axis] = offsets[axis, first + base] - offsets[axis, second + base]
            opens, closes = jnp.int32(1), jnp.int32(1)
            for other in range(slots):
                same = (other < counts[p]) & (pairs[other, 0, p] - base == first)
                opens = jnp.where(same & (other < k), 0, opens)
                closes = jnp.where(same & (other > k), 0, closes)
            plist[at + 6] = opens
            plist[at + 7] = closes

    each_pair(pairs, counts, slots, base, step)


def shifted(box, move):
    edge, plane = box.shape
    along_x, along_y, along_z = move
    flat = along_y * edge + along_z
    out = pltpu.roll(box, lax.rem(edge - along_x, edge), 0)
    out = pltpu.roll(out, lax.rem(plane - flat, plane), 1)
    row = lax.broadcasted_iota(jnp.int32, (edge, plane), 0) + along_x
    lane = lax.broadcasted_iota(jnp.int32, (edge, plane), 1)
    depth = (lane & (edge - 1)) + along_z
    lane = lane + (along_y * edge)
    keep = (row >= 0) & (row < edge) & (lane >= 0) & (lane < plane) & (depth >= 0) & (depth < edge)
    return jnp.where(keep, out, 0.0)


def pair_kernel(dims, plist, meta, boxes, left_hi, left_lo, gain, right_hi, right_lo, base, gradient, extra, *rest):
    columns, own, last = dims
    recvs, (side, out, energy), rest = rest[: columns - 1], rest[columns - 1 : columns + 2], rest[columns + 2 :]
    partner, density, source, running, total, field, held, slope, sems = rest[-9:]
    edge, plane = gain.shape
    copies = [pltpu.make_async_copy(base, held, sems.at[0]), pltpu.make_async_copy(gradient, slope, sems.at[1])]
    for copy in copies:
        copy.start()
    field[...] = jnp.zeros_like(field)
    total[...] = jnp.zeros_like(total)
    count = meta[0]

    def along_left(values):
        high, low = split(values)
        return dot(left_hi[...], high) + (dot(left_hi[...], low) + dot(left_lo[...], high))

    def along_right(values):
        high, low = split(values)
        both = dot(jnp.concatenate([high, low], 0), right_hi[...])
        rows = values.shape[0]
        return both[:rows] + (both[rows:] + dot(high, right_lo[...]))

    def batch_step(index, carry):
        for s in range(BATCH):
            pair = index * BATCH + s
            rows = pl.ds(s * edge, edge)

            @pl.when(pair < count)
            def _():
                at = pair * FIELDS
                code = plist[at + 1]
                place = plist[at + 2]

                @pl.when(code == 0)
                def _():
                    source[...] = boxes[place]

                for m in range(1, columns):

                    @pl.when(code == m)
                    def _():
                        source[...] = recvs[m - 1][place if capacity(m, columns) > 1 else 0]

                @pl.when(code == columns)
                def _():
                    copy = pltpu.make_async_copy(extra.at[place], source, sems.at[2])
                    copy.start()
                    copy.wait()

                other = shifted(source[...].astype(jnp.float32), (plist[at + 3], plist[at + 4], plist[at + 5]))
                partner[rows, :] = other
                density[rows, :] = boxes[plist[at]].astype(jnp.float32) * other

            @pl.when(pair >= count)
            def _():
                density[rows, :] = jnp.zeros((edge, plane), jnp.float32)

        spectrum = along_right(along_left(density[...]))
        scaled = (spectrum.reshape(BATCH, edge, plane) * gain[...]).reshape(BATCH * edge, plane)
        potential = along_left(along_right(scaled))
        work = density[...] * potential
        total[...] += jnp.sum(work.reshape(BATCH * edge // 8, 8, plane), 0)
        for s in range(BATCH):
            pair = index * BATCH + s

            @pl.when(pair < count)
            def _():
                at = pair * FIELDS
                place = plist[at]
                rows = slice(s * edge, (s + 1) * edge)
                running[rows, :] = potential[rows] * partner[rows, :]

                @pl.when(plist[at + 6] == 0)
                def _():
                    running[rows, :] = running[rows, :] + partial(place)[...]

                @pl.when(plist[at + 7] == 0)
                def _():
                    partial(place)[...] = running[rows, :]

                @pl.when(plist[at + 7] != 0)
                def _():
                    rounded = running[rows, :].astype(jnp.bfloat16).astype(jnp.float32)
                    field[place] = field[place] + rounded

        return carry

    def partial(place):
        return running.at[pl.ds(pl.multiple_of((BATCH + place) * edge, edge), edge)]

    lax.fori_loop(0, lax.div(count + BATCH - 1, BATCH), batch_step, 0)

    for copy in copies:
        copy.wait()
    for b in range(own):
        out[b] = held[b] - damping * (slope[b] + field[b])
    mine = jnp.sum(total[...])
    if last:
        lane = lax.broadcasted_iota(jnp.int32, (1, 128), 1)
        row = jnp.where(lane == 0, side[:1], jnp.where(lane == 1, mine, 0.0))
        for device in range(energy.shape[0]):
            energy[device] = row
    else:
        next_boxes, sends = rest[0], rest[1:-9]
        energy[...] = jnp.full(energy.shape, mine)
        for b in range(own):
            next_boxes[b] = out[b].astype(jnp.bfloat16)
        pack(columns, own, lax.axis_index("col"), side, next_boxes, sends)


def local(orbitals, gradient, offsets, pairs, counts):
    own, edge, plane = orbitals.shape
    columns = lax.axis_size("col")
    devices = lax.axis_size("row") * columns
    owners, slots = pairs.shape[0], pairs.shape[1]
    masks = range(1, columns)
    basis = sine_basis(edge)
    basis_hi, basis_lo = split(jnp.asarray(np.kron(basis, basis), jnp.float32))
    left_hi, left_lo = split(jnp.asarray(np.kron(np.eye(BATCH), basis), jnp.float32))
    gain = jnp.asarray(solve_gain(edge), jnp.float32)
    box_shape = jax.ShapeDtypeStruct((own, edge, plane), jnp.bfloat16)
    send_shapes = [jax.ShapeDtypeStruct((capacity(m, columns), edge, plane), jnp.bfloat16) for m in masks]
    most_extra = sum(max(own - capacity(m, columns), 0) for m in masks)
    pairs = pairs.transpose(1, 2, 0)
    offsets = offsets.T

    def ints(size):
        return jax.ShapeDtypeStruct((size,), jnp.int32)

    need, boxes, *sends = pl.pallas_call(
        functools.partial(need_kernel, (columns, own, slots)),
        out_shape=[ints(columns * columns), box_shape, *send_shapes],
        in_specs=[SMEM, SMEM, VMEM],
        out_specs=[SMEM, VMEM] + [VMEM] * len(send_shapes),
        compiler_params=GRANT,
        name="need",
    )(pairs, counts, orbitals)
    plist, meta, extra_count, extra_mask, extra_box, extra = pl.pallas_call(
        functools.partial(plan_kernel, (columns, own, slots)),
        out_shape=[
            ints(owners * slots * FIELDS),
            ints(1),
            ints(1),
            ints(most_extra),
            ints(most_extra),
            jax.ShapeDtypeStruct((most_extra, edge, plane), jnp.bfloat16),
        ],
        in_specs=[SMEM] * 4,
        out_specs=[SMEM] * 5 + [ANY],
        scratch_shapes=[pltpu.SMEM((columns,), jnp.int32)],
        compiler_params=GRANT,
        name="plan",
    )(need, pairs, counts, offsets)

    def hop(mask, values):
        return lax.ppermute(values, "col", [(c, c ^ mask) for c in range(columns)])

    def exchange(boxes, sends, extra):
        got = {m: hop(m, sends[m - 1]) for m in reversed(masks)}

        def one_more(at, extra):
            box = lax.dynamic_index_in_dim(boxes, extra_box[at], 0, True)
            box = lax.switch(extra_mask[at], [functools.partial(hop, m) for m in masks], box)
            return lax.dynamic_update_slice_in_dim(extra, box, at, 0)

        extra = lax.fori_loop(0, extra_count[0], one_more, extra)
        return [got[m] for m in masks], extra

    current = orbitals
    side = need
    for round_idx in range(ROUNDS):
        last = round_idx == ROUNDS - 1
        recvs, extra = exchange(boxes, sends, extra)
        energy_shape = (devices, 1, 128) if last else (8, 128)
        out_shape = [jax.ShapeDtypeStruct((own, edge, plane), jnp.float32), jax.ShapeDtypeStruct(energy_shape, jnp.float32)]
        if not last:
            out_shape += [box_shape, *send_shapes]
        current, side, *rest = pl.pallas_call(
            functools.partial(pair_kernel, (columns, own, last)),
            out_shape=out_shape,
            in_specs=[SMEM] * 2 + [VMEM] * 6 + [ANY] * 3 + [VMEM] * len(recvs) + [VMEM if last else SMEM],
            out_specs=[VMEM] * len(out_shape),
            scratch_shapes=[
                pltpu.VMEM((BATCH * edge, plane), jnp.float32),
                pltpu.VMEM((BATCH * edge, plane), jnp.float32),
                pltpu.VMEM((edge, plane), jnp.bfloat16),
                pltpu.VMEM(((BATCH + own) * edge, plane), jnp.float32),
                pltpu.VMEM((8, plane), jnp.float32),
                pltpu.VMEM((own, edge, plane), jnp.float32),
                pltpu.VMEM((own, edge, plane), jnp.float32),
                pltpu.VMEM((own, edge, plane), jnp.float32),
                pltpu.SemaphoreType.DMA((3,)),
            ],
            compiler_params=GRANT,
            name="pairs",
        )(plist, meta, boxes, left_hi, left_lo, gain, basis_hi, basis_lo, current, gradient, extra, *recvs, side)
        if not last:
            boxes, *sends = rest
    every = lax.all_to_all(side, ("row", "col"), 0, 0, tiled=True)
    energies = jnp.sum(every, (0, 1))[:ROUNDS] / (edge * edge * edge * devices)
    return current, energies


def solution(mesh):
    return jax.shard_map(
        local,
        mesh=mesh,
        in_specs=(
            P(("row", "col"), None, None),
            P(("row", "col"), None, None),
            P(),
            P("row", None, None),
            P("row"),
        ),
        out_specs=(P(("row", "col"), None, None), P()),
        check_vma=False,
    )
```

```python
import functools

import jax
import jax.numpy as jnp
import numpy as np
from jax import lax
from jax.experimental import pallas as pl
from jax.experimental.pallas import tpu as pltpu
from jax.sharding import PartitionSpec as P

SWEEPS = 12
ROUNDS = 2
BATCH = 4
FIELDS = 8

screen_mu = 0.1
damping = 0.5

SMEM = pl.BlockSpec(memory_space=pltpu.SMEM)
VMEM = pl.BlockSpec(memory_space=pltpu.VMEM)
ANY = pl.BlockSpec(memory_space=pl.ANY)


def split(values):
    high = values.astype(jnp.bfloat16)
    return high, (values - high.astype(jnp.float32)).astype(jnp.bfloat16)


def sine_basis(edge):
    index = np.arange(1, edge + 1)
    return np.sqrt(2.0 / (edge + 1)) * np.sin(np.pi * np.outer(index, index) / (edge + 1))


def solve_gain(edge):
    cosines = 2.0 * np.cos(np.pi * np.arange(1, edge + 1) / (edge + 1))
    eigen = 6.0 + screen_mu - (cosines[:, None, None] + cosines[None, :, None] + cosines[None, None, :])
    center, half = 6.0 + screen_mu, 6.0
    ratio = center / half
    prev = 1.0 / ratio
    gain, rest = np.zeros_like(eigen), np.ones_like(eigen)
    step = rest / center
    for _ in range(SWEEPS):
        gain = gain + step
        rest = rest - eigen * step
        coef = 1.0 / (2.0 * ratio - prev)
        step = coef * prev * step + (2.0 * coef / half) * rest
        prev = coef
    return gain.reshape(edge, edge * edge)


def dot(a, b):
    return jnp.dot(a, b, preferred_element_type=jnp.float32)


def capacity(mask, columns):
    return 2 if mask < columns // 2 else 1


def bits(word, size):
    return [(word >> b) & 1 for b in range(size)]


def owner_of(orbital, own):
    return orbital >> (own.bit_length() - 1) if own & (own - 1) == 0 else lax.div(orbital, own)


def each_pair(pairs, counts, slots, base, step):
    def owner_step(p, carry):
        def slot_step(k, carry):
            step(p, k, pairs[k, 0, p] - base, pairs[k, 1, p] - base)
            return carry

        return lax.fori_loop(0, jnp.minimum(counts[p], slots), slot_step, carry)

    lax.fori_loop(0, counts.shape[0], owner_step, 0)


def ship(columns, own, me, need, values, boxes, sends, sems):
    whole = pltpu.make_async_copy(values, boxes, sems.at[0])
    whole.start()

    def each_send(act):
        for mask in range(1, columns):
            limit = capacity(mask, columns)
            rank = 0
            for b, bit in enumerate(bits(need[(me ^ mask) * columns + me], own)):
                place = rank if limit > 1 else 0

                @pl.when((bit != 0) & (rank < limit))
                def _():
                    sem = sems.at[1 + (mask - 1) * own + b]
                    act(pltpu.make_async_copy(values.at[b], sends[mask - 1].at[place], sem))

                rank = rank + bit

    each_send(lambda copy: copy.start())

    def wait():
        whole.wait()
        each_send(lambda copy: copy.wait())

    return wait


def need_kernel(dims, pairs, counts, phi, need, boxes, *rest):
    columns, own, slots = dims
    sends, (held, values, sems, phi_sem) = rest[: columns - 1], rest[columns - 1 :]
    me = lax.axis_index("col")
    base = lax.axis_index("row") * (columns * own)
    coming = pltpu.make_async_copy(phi, held, phi_sem)
    coming.start()

    def clear(at, carry):
        for lane in range(columns):
            need[at * columns + lane] = 0
        return carry

    lax.fori_loop(0, columns, clear, 0)

    def step(p, k, first, second):
        source = owner_of(second, own)
        key = owner_of(first, own) * columns + source
        need[key] = need[key] | (1 << (second - source * own))

    each_pair(pairs, counts, slots, base, step)
    coming.wait()
    for b in range(own):
        values[b] = held[b].astype(jnp.bfloat16)
    ship(columns, own, me, need, values, boxes, sends, sems)()


def plan_kernel(dims, need, pairs, counts, offsets, plist, meta, extra_count, extra_mask, extra_box, unset, start):
    columns, own, slots = dims
    del unset
    me = lax.axis_index("col")
    base = lax.axis_index("row") * (columns * own)
    meta[0] = 0
    extra_count[0] = 0
    for mask in range(1, columns):
        limit = capacity(mask, columns)
        start[mask] = extra_count[0]
        mine = bits(need[(me ^ mask) * columns + me], own)

        def most(c, carry):
            return jnp.maximum(carry, sum(bits(need[c * columns + (c ^ mask)], own)))

        longest = lax.fori_loop(0, columns, most, 0)
        for over in range(own - limit):

            @pl.when(longest > limit + over)
            def _():
                at = extra_count[0]
                extra_count[0] = at + 1
                rank, box = 0, 0
                for b, bit in enumerate(mine):
                    box = jnp.where((bit != 0) & (rank == limit + over), b, box)
                    rank = rank + bit
                extra_mask[at] = mask - 1
                extra_box[at] = box

    def step(p, k, first, second):
        @pl.when(owner_of(first, own) == me)
        def _():
            source = owner_of(second, own)
            mask = me ^ source
            place = second - source * own
            rank = sum(bits(need[me * columns + source] & ((1 << place) - 1), own))
            limit = jnp.where(mask < columns // 2, 2, 1)
            fits = rank < limit
            at = meta[0] * FIELDS
            meta[0] = meta[0] + 1
            plist[at] = first - me * own
            plist[at + 1] = jnp.where((mask == 0) | fits, mask, columns)
            plist[at + 2] = jnp.where(mask == 0, place, jnp.where(fits, rank, start[mask] + rank - limit))
            for axis in range(3):
                plist[at + 3 + axis] = offsets[axis, first + base] - offsets[axis, second + base]
            opens, closes = jnp.int32(1), jnp.int32(1)
            for other in range(slots):
                same = (other < counts[p]) & (pairs[other, 0, p] - base == first)
                opens = jnp.where(same & (other < k), 0, opens)
                closes = jnp.where(same & (other > k), 0, closes)
            plist[at + 6] = opens
            plist[at + 7] = closes

    each_pair(pairs, counts, slots, base, step)


def shifted(box, move):
    edge, plane = box.shape
    along_x, along_y, along_z = move
    flat = along_y * edge + along_z
    out = pltpu.roll(box, lax.rem(edge - along_x, edge), 0)
    out = pltpu.roll(out, lax.rem(plane - flat, plane), 1)
    row = lax.broadcasted_iota(jnp.int32, (edge, plane), 0) + along_x
    lane = lax.broadcasted_iota(jnp.int32, (edge, plane), 1)
    depth = (lane & (edge - 1)) + along_z
    lane = lane + (along_y * edge)
    keep = (row >= 0) & (row < edge) & (lane >= 0) & (lane < plane) & (depth >= 0) & (depth < edge)
    return jnp.where(keep, out, 0.0)


def pair_kernel(dims, plist, meta, side, boxes, left_hi, left_lo, gain, right_hi, right_lo, base, gradient, extra, *rest):
    columns, own, last = dims
    recvs, out, energy, rest = rest[: columns - 1], rest[columns - 1], rest[columns], rest[columns + 1 :]
    partner, density, running, total, field, own_boxes, sources, source_sems, sems, *loaded = rest[-16:]
    given = [boxes, left_hi, left_lo, gain, right_hi, right_lo, base, gradient]
    own_boxes, left_hi, left_lo, gain, right_hi, right_lo, held, slope = [own_boxes] + loaded
    edge, plane = gain.shape
    count = meta[0]
    copies = [
        pltpu.make_async_copy(there, here, sems.at[at])
        for at, (there, here) in enumerate(zip(given, [own_boxes] + loaded))
    ]
    copies[0].start()

    def fetch(pair, carry):
        code = plist[pair * FIELDS + 1]
        place = plist[pair * FIELDS + 2]
        for m in range(1, columns):

            @pl.when(code == m)
            def _():
                there = recvs[m - 1].at[place if capacity(m, columns) > 1 else 0]
                pltpu.make_async_copy(there, sources.at[pair], source_sems.at[pair]).start()

        @pl.when(code == columns)
        def _():
            pltpu.make_async_copy(extra.at[place], sources.at[pair], source_sems.at[pair]).start()

        return carry

    lax.fori_loop(0, count, fetch, 0)
    for copy in copies[1:]:
        copy.start()
    field[...] = jnp.zeros_like(field)
    total[...] = jnp.zeros_like(total)
    copies[0].wait()

    def along_left(values):
        high, low = split(values)
        return dot(left_hi[...], high) + (dot(left_hi[...], low) + dot(left_lo[...], high))

    def along_right(values):
        high, low = split(values)
        both = dot(jnp.concatenate([high, low], 0), right_hi[...])
        rows = values.shape[0]
        return both[:rows] + (both[rows:] + dot(high, right_lo[...]))

    def batch_step(index, carry):
        for s in range(BATCH):
            pair = index * BATCH + s
            rows = pl.ds(s * edge, edge)

            @pl.when(pair < count)
            def _():
                at = pair * FIELDS
                place = plist[at + 2]

                @pl.when(plist[at + 1] == 0)
                def _():
                    sources[pair] = own_boxes[place]

                @pl.when(plist[at + 1] != 0)
                def _():
                    pltpu.make_async_copy(extra.at[0], sources.at[pair], source_sems.at[pair]).wait()

                other = shifted(sources[pair].astype(jnp.float32), (plist[at + 3], plist[at + 4], plist[at + 5]))
                partner[rows, :] = other
                density[rows, :] = own_boxes[plist[at]].astype(jnp.float32) * other

            @pl.when(pair >= count)
            def _():
                density[rows, :] = jnp.zeros((edge, plane), jnp.float32)

        @pl.when(index == 0)
        def _():
            for copy in copies[1:6]:
                copy.wait()

        spectrum = along_right(along_left(density[...]))
        scaled = (spectrum.reshape(BATCH, edge, plane) * gain[...]).reshape(BATCH * edge, plane)
        potential = along_left(along_right(scaled))
        work = density[...] * potential
        total[...] += jnp.sum(work.reshape(BATCH * edge // 8, 8, plane), 0)
        for s in range(BATCH):
            pair = index * BATCH + s

            @pl.when(pair < count)
            def _():
                at = pair * FIELDS
                place = plist[at]
                rows = slice(s * edge, (s + 1) * edge)
                running[rows, :] = potential[rows] * partner[rows, :]

                @pl.when(plist[at + 6] == 0)
                def _():
                    running[rows, :] = running[rows, :] + partial(place)[...]

                @pl.when(plist[at + 7] == 0)
                def _():
                    partial(place)[...] = running[rows, :]

                @pl.when(plist[at + 7] != 0)
                def _():
                    rounded = running[rows, :].astype(jnp.bfloat16).astype(jnp.float32)
                    field[place] = field[place] + rounded

        return carry

    def partial(place):
        return running.at[pl.ds(pl.multiple_of((BATCH + place) * edge, edge), edge)]

    lax.fori_loop(0, lax.div(count + BATCH - 1, BATCH), batch_step, 0)

    @pl.when(count == 0)
    def _():
        for copy in copies[1:6]:
            copy.wait()

    for copy in copies[6:]:
        copy.wait()
    for b in range(own):
        field[b] = held[b] - damping * (slope[b] + field[b])
    result = pltpu.make_async_copy(field, out, sems.at[8])
    result.start()
    if not last:
        next_boxes, sends, send_sems = rest[0], rest[1:columns], rest[columns]
        for b in range(own):
            own_boxes[b] = field[b].astype(jnp.bfloat16)
        wait = ship(columns, own, lax.axis_index("col"), side, own_boxes, next_boxes, sends, send_sems)
    mine = jnp.sum(total[...])
    if last:
        lane = lax.broadcasted_iota(jnp.int32, (1, 128), 1)
        row = jnp.where(lane == 0, side[:1], jnp.where(lane == 1, mine, 0.0))
        for device in range(energy.shape[0]):
            energy[device] = row
    else:
        energy[...] = jnp.full(energy.shape, mine)
        wait()
    result.wait()


def local(orbitals, gradient, offsets, pairs, counts):
    own, edge, plane = orbitals.shape
    columns = lax.axis_size("col")
    devices = lax.axis_size("row") * columns
    owners, slots = pairs.shape[0], pairs.shape[1]
    masks = range(1, columns)
    basis = sine_basis(edge)
    basis_hi, basis_lo = split(jnp.asarray(np.kron(basis, basis), jnp.float32))
    left_hi, left_lo = split(jnp.asarray(np.kron(np.eye(BATCH), basis), jnp.float32))
    gain = jnp.asarray(solve_gain(edge), jnp.float32)
    box_shape = jax.ShapeDtypeStruct((own, edge, plane), jnp.bfloat16)
    send_shapes = [jax.ShapeDtypeStruct((capacity(m, columns), edge, plane), jnp.bfloat16) for m in masks]
    most_extra = sum(max(own - capacity(m, columns), 0) for m in masks)
    pairs = pairs.transpose(1, 2, 0)
    offsets = offsets.T

    send_sems = pltpu.SemaphoreType.DMA((1 + len(masks) * own,))

    def ints(size):
        return jax.ShapeDtypeStruct((size,), jnp.int32)

    need, boxes, *sends = pl.pallas_call(
        functools.partial(need_kernel, (columns, own, slots)),
        out_shape=[ints(columns * columns), box_shape, *send_shapes],
        in_specs=[SMEM, SMEM, ANY],
        out_specs=[SMEM, ANY] + [ANY] * len(send_shapes),
        scratch_shapes=[
            pltpu.VMEM((own, edge, plane), jnp.float32),
            pltpu.VMEM((own, edge, plane), jnp.bfloat16),
            send_sems,
            pltpu.SemaphoreType.DMA,
        ],
        name="need",
    )(pairs, counts, orbitals)
    plist, meta, extra_count, extra_mask, extra_box, extra = pl.pallas_call(
        functools.partial(plan_kernel, (columns, own, slots)),
        out_shape=[
            ints(owners * slots * FIELDS),
            ints(1),
            ints(1),
            ints(most_extra),
            ints(most_extra),
            jax.ShapeDtypeStruct((most_extra, edge, plane), jnp.bfloat16),
        ],
        in_specs=[SMEM] * 4,
        out_specs=[SMEM] * 5 + [ANY],
        scratch_shapes=[pltpu.SMEM((columns,), jnp.int32)],
        name="plan",
    )(need, pairs, counts, offsets)

    def hop(mask, values):
        return lax.ppermute(values, "col", [(c, c ^ mask) for c in range(columns)])

    def exchange(boxes, sends, extra):
        got = {m: hop(m, sends[m - 1]) for m in reversed(masks)}

        def one_more(at, extra):
            box = lax.dynamic_index_in_dim(boxes, extra_box[at], 0, True)
            box = lax.switch(extra_mask[at], [functools.partial(hop, m) for m in masks], box)
            return lax.dynamic_update_slice_in_dim(extra, box, at, 0)

        extra = lax.fori_loop(0, extra_count[0], one_more, extra)
        return [got[m] for m in masks], extra

    current = orbitals
    side = need
    for round_idx in range(ROUNDS):
        last = round_idx == ROUNDS - 1
        recvs, extra = exchange(boxes, sends, extra)
        energy_shape = (devices, 1, 128) if last else (8, 128)
        out_shape = [jax.ShapeDtypeStruct((own, edge, plane), jnp.float32), jax.ShapeDtypeStruct(energy_shape, jnp.float32)]
        if not last:
            out_shape += [box_shape, *send_shapes]
        current, side, *rest = pl.pallas_call(
            functools.partial(pair_kernel, (columns, own, last)),
            out_shape=out_shape,
            in_specs=[SMEM, SMEM, VMEM if last else SMEM] + [ANY] * (9 + len(recvs)),
            out_specs=[ANY, VMEM] + [ANY] * (len(out_shape) - 2),
            scratch_shapes=([] if last else [send_sems])
            + [
                pltpu.VMEM((BATCH * edge, plane), jnp.float32),
                pltpu.VMEM((BATCH * edge, plane), jnp.float32),
                pltpu.VMEM(((BATCH + own) * edge, plane), jnp.float32),
                pltpu.VMEM((8, plane), jnp.float32),
                pltpu.VMEM((own, edge, plane), jnp.float32),
                pltpu.VMEM((own, edge, plane), jnp.bfloat16),
                pltpu.VMEM((owners * slots, edge, plane), jnp.bfloat16),
                pltpu.SemaphoreType.DMA((owners * slots,)),
                pltpu.SemaphoreType.DMA((9,)),
                pltpu.VMEM(left_hi.shape, jnp.bfloat16),
                pltpu.VMEM(left_lo.shape, jnp.bfloat16),
                pltpu.VMEM((edge, plane), jnp.float32),
                pltpu.VMEM((plane, plane), jnp.bfloat16),
                pltpu.VMEM((plane, plane), jnp.bfloat16),
                pltpu.VMEM((own, edge, plane), jnp.float32),
                pltpu.VMEM((own, edge, plane), jnp.float32),
            ],
            name="pairs",
        )(plist, meta, side, boxes, left_hi, left_lo, gain, basis_hi, basis_lo, current, gradient, extra, *recvs)
        if not last:
            boxes, *sends = rest
    every = lax.all_to_all(side, ("row", "col"), 0, 0, tiled=True)
    energies = jnp.sum(every, (0, 1))[:ROUNDS] / (edge * edge * edge * devices)
    return current, energies


def solution(mesh):
    return jax.shard_map(
        local,
        mesh=mesh,
        in_specs=(
            P(("row", "col"), None, None),
            P(("row", "col"), None, None),
            P(),
            P("row", None, None),
            P("row"),
        ),
        out_specs=(P(("row", "col"), None, None), P()),
        check_vma=False,
    )
```

```python
import functools

import jax
import jax.numpy as jnp
import numpy as np
from jax import lax
from jax.experimental import pallas as pl
from jax.experimental.pallas import tpu as pltpu
from jax.sharding import PartitionSpec as P

SWEEPS = 12
ROUNDS = 2
BATCH = 4
FIELDS = 8

screen_mu = 0.1
damping = 0.5

SMEM = pl.BlockSpec(memory_space=pltpu.SMEM)
VMEM = pl.BlockSpec(memory_space=pltpu.VMEM)
ANY = pl.BlockSpec(memory_space=pl.ANY)


def split(values):
    high = values.astype(jnp.bfloat16)
    return high, (values - high.astype(jnp.float32)).astype(jnp.bfloat16)


def sine_basis(edge):
    index = np.arange(1, edge + 1)
    return np.sqrt(2.0 / (edge + 1)) * np.sin(np.pi * np.outer(index, index) / (edge + 1))


def solve_gain(edge):
    cosines = 2.0 * np.cos(np.pi * np.arange(1, edge + 1) / (edge + 1))
    eigen = 6.0 + screen_mu - (cosines[:, None, None] + cosines[None, :, None] + cosines[None, None, :])
    center, half = 6.0 + screen_mu, 6.0
    ratio = center / half
    prev = 1.0 / ratio
    gain, rest = np.zeros_like(eigen), np.ones_like(eigen)
    step = rest / center
    for _ in range(SWEEPS):
        gain = gain + step
        rest = rest - eigen * step
        coef = 1.0 / (2.0 * ratio - prev)
        step = coef * prev * step + (2.0 * coef / half) * rest
        prev = coef
    return gain.reshape(edge, edge * edge)


def dot(a, b):
    return jnp.dot(a, b, preferred_element_type=jnp.float32)


def capacity(mask, columns):
    return 2 if mask < columns // 2 else 1


def bits(word, size):
    return [(word >> b) & 1 for b in range(size)]


def owner_of(orbital, own):
    return orbital >> (own.bit_length() - 1) if own & (own - 1) == 0 else lax.div(orbital, own)


def each_pair(pairs, counts, slots, base, step):
    def owner_step(p, carry):
        def slot_step(k, carry):
            step(p, k, pairs[k, 0, p] - base, pairs[k, 1, p] - base)
            return carry

        return lax.fori_loop(0, jnp.minimum(counts[p], slots), slot_step, carry)

    lax.fori_loop(0, counts.shape[0], owner_step, 0)


def ship(columns, own, me, need, values, boxes, sends, sems):
    whole = pltpu.make_async_copy(values, boxes, sems.at[0])
    whole.start()

    def each_send(act):
        for mask in range(1, columns):
            limit = capacity(mask, columns)
            rank = 0
            for b, bit in enumerate(bits(need[(me ^ mask) * columns + me], own)):
                place = rank if limit > 1 else 0

                @pl.when((bit != 0) & (rank < limit))
                def _():
                    sem = sems.at[1 + (mask - 1) * own + b]
                    act(pltpu.make_async_copy(values.at[b], sends[mask - 1].at[place], sem))

                rank = rank + bit

    each_send(lambda copy: copy.start())

    def wait():
        whole.wait()
        each_send(lambda copy: copy.wait())

    return wait


def pack(columns, own, me, need, boxes, sends):
    for mask in range(1, columns):
        limit = capacity(mask, columns)
        rank = 0
        for b, bit in enumerate(bits(need[(me ^ mask) * columns + me], own)):
            place = rank if limit > 1 else 0

            @pl.when((bit != 0) & (rank < limit))
            def _():
                sends[mask - 1][place] = boxes[b]

            rank = rank + bit


def need_kernel(dims, pairs, counts, phi, need, boxes, *sends):
    columns, own, slots = dims
    me = lax.axis_index("col")
    base = lax.axis_index("row") * (columns * own)

    def clear(at, carry):
        for lane in range(columns):
            need[at * columns + lane] = 0
        return carry

    lax.fori_loop(0, columns, clear, 0)

    def step(p, k, first, second):
        source = owner_of(second, own)
        key = owner_of(first, own) * columns + source
        need[key] = need[key] | (1 << (second - source * own))

    each_pair(pairs, counts, slots, base, step)
    for b in range(own):
        boxes[b] = phi[b].astype(jnp.bfloat16)
    pack(columns, own, me, need, boxes, sends)


def plan_kernel(dims, need, pairs, counts, offsets, plist, meta, extra_count, extra_mask, extra_box, unset, start):
    columns, own, slots = dims
    del unset
    me = lax.axis_index("col")
    base = lax.axis_index("row") * (columns * own)
    meta[0] = 0
    extra_count[0] = 0
    for mask in range(1, columns):
        limit = capacity(mask, columns)
        start[mask] = extra_count[0]
        mine = bits(need[(me ^ mask) * columns + me], own)

        def most(c, carry):
            return jnp.maximum(carry, sum(bits(need[c * columns + (c ^ mask)], own)))

        longest = lax.fori_loop(0, columns, most, 0)
        for over in range(own - limit):

            @pl.when(longest > limit + over)
            def _():
                at = extra_count[0]
                extra_count[0] = at + 1
                rank, box = 0, 0
                for b, bit in enumerate(mine):
                    box = jnp.where((bit != 0) & (rank == limit + over), b, box)
                    rank = rank + bit
                extra_mask[at] = mask - 1
                extra_box[at] = box

    def step(p, k, first, second):
        @pl.when(owner_of(first, own) == me)
        def _():
            source = owner_of(second, own)
            mask = me ^ source
            place = second - source * own
            rank = sum(bits(need[me * columns + source] & ((1 << place) - 1), own))
            limit = jnp.where(mask < columns // 2, 2, 1)
            fits = rank < limit
            at = meta[0] * FIELDS
            meta[0] = meta[0] + 1
            plist[at] = first - me * own
            plist[at + 1] = jnp.where((mask == 0) | fits, mask, columns)
            plist[at + 2] = jnp.where(mask == 0, place, jnp.where(fits, rank, start[mask] + rank - limit))
            for axis in range(3):
                plist[at + 3 + axis] = offsets[axis, first + base] - offsets[axis, second + base]
            opens, closes = jnp.int32(1), jnp.int32(1)
            for other in range(slots):
                same = (other < counts[p]) & (pairs[other, 0, p] - base == first)
                opens = jnp.where(same & (other < k), 0, opens)
                closes = jnp.where(same & (other > k), 0, closes)
            plist[at + 6] = opens
            plist[at + 7] = closes

    each_pair(pairs, counts, slots, base, step)


def shifted(box, move):
    edge, plane = box.shape
    along_x, along_y, along_z = move
    flat = along_y * edge + along_z
    out = pltpu.roll(box, lax.rem(edge - along_x, edge), 0)
    out = pltpu.roll(out, lax.rem(plane - flat, plane), 1)
    row = lax.broadcasted_iota(jnp.int32, (edge, plane), 0) + along_x
    lane = lax.broadcasted_iota(jnp.int32, (edge, plane), 1)
    depth = (lane & (edge - 1)) + along_z
    lane = lane + (along_y * edge)
    keep = (row >= 0) & (row < edge) & (lane >= 0) & (lane < plane) & (depth >= 0) & (depth < edge)
    return jnp.where(keep, out, 0.0)


def pair_kernel(dims, plist, meta, side, boxes, tables, left_hi, left_lo, gain, base, gradient, extra, *rest):
    columns, own, last = dims
    recvs, out, energy, rest = rest[: columns - 1], rest[columns - 1], rest[columns], rest[columns + 1 :]
    partner, density, running, total, field, own_boxes, sources, source_sems, sems, right_hi, right_lo, *loaded = rest[-17:]
    given = [boxes, tables, left_hi, left_lo, gain, base, gradient]
    tables, left_hi, left_lo, gain, held, slope = loaded
    edge, plane = gain.shape
    count = meta[0]
    copies = [
        pltpu.make_async_copy(there, here, sems.at[at])
        for at, (there, here) in enumerate(zip(given, [own_boxes] + loaded))
    ]
    for copy in copies[:2]:
        copy.start()

    def fetch(pair, carry):
        code = plist[pair * FIELDS + 1]
        place = plist[pair * FIELDS + 2]
        for m in range(1, columns):

            @pl.when(code == m)
            def _():
                there = recvs[m - 1].at[place if capacity(m, columns) > 1 else 0]
                pltpu.make_async_copy(there, sources.at[pair], source_sems.at[pair]).start()

        @pl.when(code == columns)
        def _():
            pltpu.make_async_copy(extra.at[place], sources.at[pair], source_sems.at[pair]).start()

        return carry

    lax.fori_loop(0, count, fetch, 0)
    for copy in copies[2:]:
        copy.start()
    field[...] = jnp.zeros_like(field)
    total[...] = jnp.zeros_like(total)
    for copy in copies[:2]:
        copy.wait()

    def basis_rows(y, carry):
        rows = pl.ds(pl.multiple_of(y * edge, edge), edge)
        values = tables[0, pl.ds(y, 1), :] * tables[1]
        high, low = split(values)
        right_hi[rows, :] = high
        right_lo[rows, :] = low
        return carry

    lax.fori_loop(0, edge, basis_rows, 0)

    def along_left(values):
        high, low = split(values)
        return dot(left_hi[...], high) + (dot(left_hi[...], low) + dot(left_lo[...], high))

    def along_right(values):
        high, low = split(values)
        both = dot(jnp.concatenate([high, low], 0), right_hi[...])
        rows = values.shape[0]
        return both[:rows] + (both[rows:] + dot(high, right_lo[...]))

    def batch_step(index, carry):
        for s in range(BATCH):
            pair = index * BATCH + s
            rows = pl.ds(s * edge, edge)

            @pl.when(pair < count)
            def _():
                at = pair * FIELDS
                place = plist[at + 2]

                @pl.when(plist[at + 1] == 0)
                def _():
                    sources[pair] = own_boxes[place]

                @pl.when(plist[at + 1] != 0)
                def _():
                    pltpu.make_async_copy(extra.at[0], sources.at[pair], source_sems.at[pair]).wait()

                other = shifted(sources[pair].astype(jnp.float32), (plist[at + 3], plist[at + 4], plist[at + 5]))
                partner[rows, :] = other
                density[rows, :] = own_boxes[plist[at]].astype(jnp.float32) * other

            @pl.when(pair >= count)
            def _():
                density[rows, :] = jnp.zeros((edge, plane), jnp.float32)

        @pl.when(index == 0)
        def _():
            for copy in copies[2:5]:
                copy.wait()

        spectrum = along_right(along_left(density[...]))
        scaled = (spectrum.reshape(BATCH, edge, plane) * gain[...]).reshape(BATCH * edge, plane)
        potential = along_left(along_right(scaled))
        work = density[...] * potential
        total[...] += jnp.sum(work.reshape(BATCH * edge // 8, 8, plane), 0)
        for s in range(BATCH):
            pair = index * BATCH + s

            @pl.when(pair < count)
            def _():
                at = pair * FIELDS
                place = plist[at]
                rows = slice(s * edge, (s + 1) * edge)
                running[rows, :] = potential[rows] * partner[rows, :]

                @pl.when(plist[at + 6] == 0)
                def _():
                    running[rows, :] = running[rows, :] + partial(place)[...]

                @pl.when(plist[at + 7] == 0)
                def _():
                    partial(place)[...] = running[rows, :]

                @pl.when(plist[at + 7] != 0)
                def _():
                    rounded = running[rows, :].astype(jnp.bfloat16).astype(jnp.float32)
                    field[place] = field[place] + rounded

        return carry

    def partial(place):
        return running.at[pl.ds(pl.multiple_of((BATCH + place) * edge, edge), edge)]

    lax.fori_loop(0, lax.div(count + BATCH - 1, BATCH), batch_step, 0)

    @pl.when(count == 0)
    def _():
        for copy in copies[2:5]:
            copy.wait()

    for copy in copies[5:]:
        copy.wait()
    for b in range(own):
        field[b] = held[b] - damping * (slope[b] + field[b])
    result = pltpu.make_async_copy(field, out, sems.at[7])
    result.start()
    if not last:
        next_boxes, sends, send_sems = rest[0], rest[1:columns], rest[columns]
        for b in range(own):
            own_boxes[b] = field[b].astype(jnp.bfloat16)
        wait = ship(columns, own, lax.axis_index("col"), side, own_boxes, next_boxes, sends, send_sems)
    mine = jnp.sum(total[...])
    if last:
        lane = lax.broadcasted_iota(jnp.int32, (1, 128), 1)
        row = jnp.where(lane == 0, side[:1], jnp.where(lane == 1, mine, 0.0))
        for device in range(energy.shape[0]):
            energy[device] = row
    else:
        energy[...] = jnp.full(energy.shape, mine)
        wait()
    result.wait()


def local(orbitals, gradient, offsets, pairs, counts):
    own, edge, plane = orbitals.shape
    columns = lax.axis_size("col")
    devices = lax.axis_size("row") * columns
    owners, slots = pairs.shape[0], pairs.shape[1]
    masks = range(1, columns)
    basis = sine_basis(edge)
    tables = jnp.asarray(np.stack([np.repeat(basis, edge, 1), np.tile(basis, (1, edge))]), jnp.float32)
    left_hi, left_lo = split(jnp.asarray(np.kron(np.eye(BATCH), basis), jnp.float32))
    gain = jnp.asarray(solve_gain(edge), jnp.float32)
    box_shape = jax.ShapeDtypeStruct((own, edge, plane), jnp.bfloat16)
    send_shapes = [jax.ShapeDtypeStruct((capacity(m, columns), edge, plane), jnp.bfloat16) for m in masks]
    most_extra = sum(max(own - capacity(m, columns), 0) for m in masks)
    pairs = pairs.transpose(1, 2, 0)
    offsets = offsets.T

    send_sems = pltpu.SemaphoreType.DMA((1 + len(masks) * own,))

    def ints(size):
        return jax.ShapeDtypeStruct((size,), jnp.int32)

    need, boxes, *sends = pl.pallas_call(
        functools.partial(need_kernel, (columns, own, slots)),
        out_shape=[ints(columns * columns), box_shape, *send_shapes],
        in_specs=[SMEM, SMEM, VMEM],
        out_specs=[SMEM, VMEM] + [VMEM] * len(send_shapes),
        name="need",
    )(pairs, counts, orbitals)
    plist, meta, extra_count, extra_mask, extra_box, extra = pl.pallas_call(
        functools.partial(plan_kernel, (columns, own, slots)),
        out_shape=[
            ints(owners * slots * FIELDS),
            ints(1),
            ints(1),
            ints(most_extra),
            ints(most_extra),
            jax.ShapeDtypeStruct((most_extra, edge, plane), jnp.bfloat16),
        ],
        in_specs=[SMEM] * 4,
        out_specs=[SMEM] * 5 + [ANY],
        scratch_shapes=[pltpu.SMEM((columns,), jnp.int32)],
        name="plan",
    )(need, pairs, counts, offsets)

    def hop(mask, values):
        return lax.ppermute(values, "col", [(c, c ^ mask) for c in range(columns)])

    def exchange(boxes, sends, extra):
        got = {m: hop(m, sends[m - 1]) for m in reversed(masks)}

        def one_more(at, extra):
            box = lax.dynamic_index_in_dim(boxes, extra_box[at], 0, True)
            box = lax.switch(extra_mask[at], [functools.partial(hop, m) for m in masks], box)
            return lax.dynamic_update_slice_in_dim(extra, box, at, 0)

        extra = lax.fori_loop(0, extra_count[0], one_more, extra)
        return [got[m] for m in masks], extra

    current = orbitals
    side = need
    for round_idx in range(ROUNDS):
        last = round_idx == ROUNDS - 1
        recvs, extra = exchange(boxes, sends, extra)
        energy_shape = (devices, 1, 128) if last else (8, 128)
        out_shape = [jax.ShapeDtypeStruct((own, edge, plane), jnp.float32), jax.ShapeDtypeStruct(energy_shape, jnp.float32)]
        if not last:
            out_shape += [box_shape, *send_shapes]
        current, side, *rest = pl.pallas_call(
            functools.partial(pair_kernel, (columns, own, last)),
            out_shape=out_shape,
            in_specs=[SMEM, SMEM, VMEM if last else SMEM] + [ANY] * (8 + len(recvs)),
            out_specs=[ANY, VMEM] + [ANY] * (len(out_shape) - 2),
            scratch_shapes=([] if last else [send_sems])
            + [
                pltpu.VMEM((BATCH * edge, plane), jnp.float32),
                pltpu.VMEM((BATCH * edge, plane), jnp.float32),
                pltpu.VMEM(((BATCH + own) * edge, plane), jnp.float32),
                pltpu.VMEM((8, plane), jnp.float32),
                pltpu.VMEM((own, edge, plane), jnp.float32),
                pltpu.VMEM((own, edge, plane), jnp.bfloat16),
                pltpu.VMEM((owners * slots, edge, plane), jnp.bfloat16),
                pltpu.SemaphoreType.DMA((owners * slots,)),
                pltpu.SemaphoreType.DMA((8,)),
                pltpu.VMEM((plane, plane), jnp.bfloat16),
                pltpu.VMEM((plane, plane), jnp.bfloat16),
                pltpu.VMEM(tables.shape, jnp.float32),
                pltpu.VMEM(left_hi.shape, jnp.bfloat16),
                pltpu.VMEM(left_lo.shape, jnp.bfloat16),
                pltpu.VMEM((edge, plane), jnp.float32),
                pltpu.VMEM((own, edge, plane), jnp.float32),
                pltpu.VMEM((own, edge, plane), jnp.float32),
            ],
            name="pairs",
        )(plist, meta, side, boxes, tables, left_hi, left_lo, gain, current, gradient, extra, *recvs)
        if not last:
            boxes, *sends = rest
    every = lax.all_to_all(side, ("row", "col"), 0, 0, tiled=True)
    energies = jnp.sum(every, (0, 1))[:ROUNDS] / (edge * edge * edge * devices)
    return current, energies


def solution(mesh):
    return jax.shard_map(
        local,
        mesh=mesh,
        in_specs=(
            P(("row", "col"), None, None),
            P(("row", "col"), None, None),
            P(),
            P("row", None, None),
            P("row"),
        ),
        out_specs=(P(("row", "col"), None, None), P()),
        check_vma=False,
    )
```

```python
import functools

import jax
import jax.numpy as jnp
import numpy as np
from jax import lax
from jax.experimental import pallas as pl
from jax.experimental.pallas import tpu as pltpu
from jax.sharding import PartitionSpec as P

SWEEPS = 12
ROUNDS = 2
BATCH = 4
FIELDS = 8

screen_mu = 0.1
damping = 0.5

SMEM = pl.BlockSpec(memory_space=pltpu.SMEM)
VMEM = pl.BlockSpec(memory_space=pltpu.VMEM)
ANY = pl.BlockSpec(memory_space=pl.ANY)


def split(values):
    high = values.astype(jnp.bfloat16)
    return high, (values - high.astype(jnp.float32)).astype(jnp.bfloat16)


def sine_basis(edge):
    index = np.arange(1, edge + 1)
    return np.sqrt(2.0 / (edge + 1)) * np.sin(np.pi * np.outer(index, index) / (edge + 1))


def solve_gain(edge):
    cosines = 2.0 * np.cos(np.pi * np.arange(1, edge + 1) / (edge + 1))
    eigen = 6.0 + screen_mu - (cosines[:, None, None] + cosines[None, :, None] + cosines[None, None, :])
    center, half = 6.0 + screen_mu, 6.0
    ratio = center / half
    prev = 1.0 / ratio
    gain, rest = np.zeros_like(eigen), np.ones_like(eigen)
    step = rest / center
    for _ in range(SWEEPS):
        gain = gain + step
        rest = rest - eigen * step
        coef = 1.0 / (2.0 * ratio - prev)
        step = coef * prev * step + (2.0 * coef / half) * rest
        prev = coef
    return gain.reshape(edge, edge * edge)


def dot(a, b):
    return jnp.dot(a, b, preferred_element_type=jnp.float32)


def capacity(mask, columns):
    return 2 if mask < columns // 2 else 1


def bits(word, size):
    return [(word >> b) & 1 for b in range(size)]


def owner_of(orbital, own):
    return orbital >> (own.bit_length() - 1) if own & (own - 1) == 0 else lax.div(orbital, own)


def each_pair(pairs, counts, slots, base, step):
    def owner_step(p, carry):
        def slot_step(k, carry):
            step(p, k, pairs[k, 0, p] - base, pairs[k, 1, p] - base)
            return carry

        return lax.fori_loop(0, jnp.minimum(counts[p], slots), slot_step, carry)

    lax.fori_loop(0, counts.shape[0], owner_step, 0)


def ship(columns, own, me, need, values, boxes, sends, sems):
    whole = pltpu.make_async_copy(values, boxes, sems.at[0])
    whole.start()

    def each_send(act):
        for mask in range(1, columns):
            limit = capacity(mask, columns)
            rank = 0
            for b, bit in enumerate(bits(need[(me ^ mask) * columns + me], own)):
                place = rank if limit > 1 else 0

                @pl.when((bit != 0) & (rank < limit))
                def _():
                    sem = sems.at[1 + (mask - 1) * own + b]
                    act(pltpu.make_async_copy(values.at[b], sends[mask - 1].at[place], sem))

                rank = rank + bit

    each_send(lambda copy: copy.start())

    def wait():
        whole.wait()
        each_send(lambda copy: copy.wait())

    return wait


def pack(columns, own, me, need, boxes, sends):
    for mask in range(1, columns):
        limit = capacity(mask, columns)
        rank = 0
        for b, bit in enumerate(bits(need[(me ^ mask) * columns + me], own)):
            place = rank if limit > 1 else 0

            @pl.when((bit != 0) & (rank < limit))
            def _():
                sends[mask - 1][place] = boxes[b]

            rank = rank + bit


def need_kernel(dims, pairs, counts, phi, need, boxes, *sends):
    columns, own, slots = dims
    me = lax.axis_index("col")
    base = lax.axis_index("row") * (columns * own)

    def clear(at, carry):
        for lane in range(columns):
            need[at * columns + lane] = 0
        return carry

    lax.fori_loop(0, columns, clear, 0)

    def step(p, k, first, second):
        source = owner_of(second, own)
        key = owner_of(first, own) * columns + source
        need[key] = need[key] | (1 << (second - source * own))

    each_pair(pairs, counts, slots, base, step)
    for b in range(own):
        boxes[b] = phi[b].astype(jnp.bfloat16)
    pack(columns, own, me, need, boxes, sends)


def plan_kernel(dims, need, pairs, counts, offsets, boxes, plist, meta, extra_count, first, extra_mask, extra_box, unset, send, start, sem):
    columns, own, slots = dims
    del unset
    me = lax.axis_index("col")
    base = lax.axis_index("row") * (columns * own)
    meta[0] = 0
    extra_count[0] = 0
    extra_mask[0] = 0
    extra_box[0] = 0
    for mask in range(1, columns):
        limit = capacity(mask, columns)
        start[mask] = extra_count[0]
        mine = bits(need[(me ^ mask) * columns + me], own)

        def most(c, carry):
            return jnp.maximum(carry, sum(bits(need[c * columns + (c ^ mask)], own)))

        longest = lax.fori_loop(0, columns, most, 0)
        for over in range(own - limit):

            @pl.when(longest > limit + over)
            def _():
                at = extra_count[0]
                extra_count[0] = at + 1
                rank, box = 0, 0
                for b, bit in enumerate(mine):
                    box = jnp.where((bit != 0) & (rank == limit + over), b, box)
                    rank = rank + bit
                extra_mask[at] = mask - 1
                extra_box[at] = box

    first[0] = jnp.where(extra_count[0] > 0, extra_mask[0] + 1, 0)

    def sent(act):
        @pl.when(extra_count[0] > 0)
        def _():
            act(pltpu.make_async_copy(boxes.at[pl.ds(extra_box[0], 1)], send, sem))

    sent(lambda copy: copy.start())

    def step(p, k, first, second):
        @pl.when(owner_of(first, own) == me)
        def _():
            source = owner_of(second, own)
            mask = me ^ source
            place = second - source * own
            rank = sum(bits(need[me * columns + source] & ((1 << place) - 1), own))
            limit = jnp.where(mask < columns // 2, 2, 1)
            fits = rank < limit
            at = meta[0] * FIELDS
            meta[0] = meta[0] + 1
            plist[at] = first - me * own
            plist[at + 1] = jnp.where((mask == 0) | fits, mask, columns)
            plist[at + 2] = jnp.where(mask == 0, place, jnp.where(fits, rank, start[mask] + rank - limit))
            for axis in range(3):
                plist[at + 3 + axis] = offsets[axis, first + base] - offsets[axis, second + base]
            opens, closes = jnp.int32(1), jnp.int32(1)
            for other in range(slots):
                same = (other < counts[p]) & (pairs[other, 0, p] - base == first)
                opens = jnp.where(same & (other < k), 0, opens)
                closes = jnp.where(same & (other > k), 0, closes)
            plist[at + 6] = opens
            plist[at + 7] = closes

    each_pair(pairs, counts, slots, base, step)
    sent(lambda copy: copy.wait())


def shifted(box, move):
    edge, plane = box.shape
    along_x, along_y, along_z = move
    flat = along_y * edge + along_z
    out = pltpu.roll(box, lax.rem(edge - along_x, edge), 0)
    out = pltpu.roll(out, lax.rem(plane - flat, plane), 1)
    row = lax.broadcasted_iota(jnp.int32, (edge, plane), 0) + along_x
    lane = lax.broadcasted_iota(jnp.int32, (edge, plane), 1)
    depth = (lane & (edge - 1)) + along_z
    lane = lane + (along_y * edge)
    keep = (row >= 0) & (row < edge) & (lane >= 0) & (lane < plane) & (depth >= 0) & (depth < edge)
    return jnp.where(keep, out, 0.0)


def pair_kernel(dims, plist, meta, first, extra_box, side, boxes, tables, left_hi, left_lo, gain, base, gradient, extra, *rest):
    columns, own, last = dims
    recvs, early, out, energy, rest = rest[: columns - 1], rest[columns - 1], rest[columns], rest[columns + 1], rest[columns + 2 :]
    partner, density, running, total, field, own_boxes, sources, source_sems, sems, right_hi, right_lo, *loaded = rest[-17:]
    given = [boxes, tables, left_hi, left_lo, gain, base, gradient]
    tables, left_hi, left_lo, gain, held, slope = loaded
    edge, plane = gain.shape
    count = meta[0]
    copies = [
        pltpu.make_async_copy(there, here, sems.at[at])
        for at, (there, here) in enumerate(zip(given, [own_boxes] + loaded))
    ]
    for copy in copies[:2]:
        copy.start()

    def fetch(pair, carry):
        code = plist[pair * FIELDS + 1]
        place = plist[pair * FIELDS + 2]
        for m in range(1, columns):

            @pl.when(code == m)
            def _():
                there = recvs[m - 1].at[place if capacity(m, columns) > 1 else 0]
                pltpu.make_async_copy(there, sources.at[pair], source_sems.at[pair]).start()

        @pl.when((code == columns) & (place == 0))
        def _():
            pltpu.make_async_copy(early.at[0], sources.at[pair], source_sems.at[pair]).start()

        @pl.when((code == columns) & (place > 0))
        def _():
            pltpu.make_async_copy(extra.at[place], sources.at[pair], source_sems.at[pair]).start()

        return carry

    lax.fori_loop(0, count, fetch, 0)
    for copy in copies[2:]:
        copy.start()
    field[...] = jnp.zeros_like(field)
    total[...] = jnp.zeros_like(total)
    for copy in copies[:2]:
        copy.wait()

    def basis_rows(y, carry):
        rows = pl.ds(pl.multiple_of(y * edge, edge), edge)
        values = tables[0, pl.ds(y, 1), :] * tables[1]
        high, low = split(values)
        right_hi[rows, :] = high
        right_lo[rows, :] = low
        rows = pl.ds(pl.multiple_of((edge - 1 - y) * edge, edge), edge)
        right_hi[rows, :] = high * sign
        right_lo[rows, :] = low * sign
        return carry

    lane = lax.broadcasted_iota(jnp.int32, (edge, plane), 1)
    sign = (1 - 2 * (lax.div(lane, edge) & 1)).astype(jnp.float32).astype(jnp.bfloat16)
    lax.fori_loop(0, edge // 2, basis_rows, 0)

    def along_left(values):
        high, low = split(values)
        return dot(left_hi[...], high) + (dot(left_hi[...], low) + dot(left_lo[...], high))

    def along_right(values):
        high, low = split(values)
        both = dot(jnp.concatenate([high, low], 0), right_hi[...])
        rows = values.shape[0]
        return both[:rows] + (both[rows:] + dot(high, right_lo[...]))

    def batch_step(index, carry):
        for s in range(BATCH):
            pair = index * BATCH + s
            rows = pl.ds(s * edge, edge)

            @pl.when(pair < count)
            def _():
                at = pair * FIELDS
                place = plist[at + 2]

                @pl.when(plist[at + 1] == 0)
                def _():
                    sources[pair] = own_boxes[place]

                @pl.when(plist[at + 1] != 0)
                def _():
                    pltpu.make_async_copy(extra.at[0], sources.at[pair], source_sems.at[pair]).wait()

                other = shifted(sources[pair].astype(jnp.float32), (plist[at + 3], plist[at + 4], plist[at + 5]))
                partner[rows, :] = other
                density[rows, :] = own_boxes[plist[at]].astype(jnp.float32) * other

            @pl.when(pair >= count)
            def _():
                density[rows, :] = jnp.zeros((edge, plane), jnp.float32)

        @pl.when(index == 0)
        def _():
            for copy in copies[2:5]:
                copy.wait()

        spectrum = along_right(along_left(density[...]))
        scaled = (spectrum.reshape(BATCH, edge, plane) * gain[...]).reshape(BATCH * edge, plane)
        potential = along_left(along_right(scaled))
        work = density[...] * potential
        total[...] += jnp.sum(work.reshape(BATCH * edge // 8, 8, plane), 0)
        for s in range(BATCH):
            pair = index * BATCH + s

            @pl.when(pair < count)
            def _():
                at = pair * FIELDS
                place = plist[at]
                rows = slice(s * edge, (s + 1) * edge)
                running[rows, :] = potential[rows] * partner[rows, :]

                @pl.when(plist[at + 6] == 0)
                def _():
                    running[rows, :] = running[rows, :] + partial(place)[...]

                @pl.when(plist[at + 7] == 0)
                def _():
                    partial(place)[...] = running[rows, :]

                @pl.when(plist[at + 7] != 0)
                def _():
                    rounded = running[rows, :].astype(jnp.bfloat16).astype(jnp.float32)
                    field[place] = field[place] + rounded

        return carry

    def partial(place):
        return running.at[pl.ds(pl.multiple_of((BATCH + place) * edge, edge), edge)]

    lax.fori_loop(0, lax.div(count + BATCH - 1, BATCH), batch_step, 0)

    @pl.when(count == 0)
    def _():
        for copy in copies[2:5]:
            copy.wait()

    for copy in copies[5:]:
        copy.wait()
    for b in range(own):
        field[b] = held[b] - damping * (slope[b] + field[b])
    result = pltpu.make_async_copy(field, out, sems.at[7])
    result.start()
    if not last:
        next_boxes, send, sends, send_sems = rest[0], rest[1], rest[2 : columns + 1], rest[columns + 1]
        for b in range(own):
            own_boxes[b] = field[b].astype(jnp.bfloat16)
        early_copy = pltpu.make_async_copy(own_boxes.at[pl.ds(extra_box[0], 1)], send, sems.at[0])

        @pl.when(first[0] > 0)
        def _():
            early_copy.start()

        wait = ship(columns, own, lax.axis_index("col"), side, own_boxes, next_boxes, sends, send_sems)
    mine = jnp.sum(total[...])
    if last:
        lane = lax.broadcasted_iota(jnp.int32, (1, 128), 1)
        row = jnp.where(lane == 0, side[:1], jnp.where(lane == 1, mine, 0.0))
        for device in range(energy.shape[0]):
            energy[device] = row
    else:
        energy[...] = jnp.full(energy.shape, mine)
        wait()

        @pl.when(first[0] > 0)
        def _():
            early_copy.wait()

    result.wait()


def local(orbitals, gradient, offsets, pairs, counts):
    own, edge, plane = orbitals.shape
    columns = lax.axis_size("col")
    devices = lax.axis_size("row") * columns
    owners, slots = pairs.shape[0], pairs.shape[1]
    masks = range(1, columns)
    basis = sine_basis(edge)
    tables = jnp.asarray(np.stack([np.repeat(basis, edge, 1), np.tile(basis, (1, edge))]), jnp.float32)
    left_hi, left_lo = split(jnp.asarray(np.kron(np.eye(BATCH), basis), jnp.float32))
    gain = jnp.asarray(solve_gain(edge), jnp.float32)
    box_shape = jax.ShapeDtypeStruct((own, edge, plane), jnp.bfloat16)
    send_shapes = [jax.ShapeDtypeStruct((capacity(m, columns), edge, plane), jnp.bfloat16) for m in masks]
    most_extra = sum(max(own - capacity(m, columns), 0) for m in masks)
    pairs = pairs.transpose(1, 2, 0)
    offsets = offsets.T

    one_box = jax.ShapeDtypeStruct((1, edge, plane), jnp.bfloat16)
    send_sems = pltpu.SemaphoreType.DMA((1 + len(masks) * own,))

    def ints(size):
        return jax.ShapeDtypeStruct((size,), jnp.int32)

    need, boxes, *sends = pl.pallas_call(
        functools.partial(need_kernel, (columns, own, slots)),
        out_shape=[ints(columns * columns), box_shape, *send_shapes],
        in_specs=[SMEM, SMEM, VMEM],
        out_specs=[SMEM, VMEM] + [VMEM] * len(send_shapes),
        name="need",
    )(pairs, counts, orbitals)
    plist, meta, extra_count, first, extra_mask, extra_box, extra, send = pl.pallas_call(
        functools.partial(plan_kernel, (columns, own, slots)),
        out_shape=[
            ints(owners * slots * FIELDS),
            ints(1),
            ints(1),
            ints(1),
            ints(most_extra),
            ints(most_extra),
            jax.ShapeDtypeStruct((most_extra, edge, plane), jnp.bfloat16),
            one_box,
        ],
        in_specs=[SMEM] * 4 + [ANY],
        out_specs=[SMEM] * 6 + [ANY, ANY],
        scratch_shapes=[pltpu.SMEM((columns,), jnp.int32), pltpu.SemaphoreType.DMA],
        name="plan",
    )(need, pairs, counts, offsets, boxes)

    def hop(mask, values):
        return lax.ppermute(values, "col", [(c, c ^ mask) for c in range(columns)])

    def exchange(boxes, sends, send, extra):
        got = {m: hop(m, sends[m - 1]) for m in reversed(masks)}
        early = lax.switch(first[0], [lambda box: box] + [functools.partial(hop, m) for m in masks], send)

        def one_more(at, extra):
            box = lax.dynamic_index_in_dim(boxes, extra_box[at], 0, True)
            box = lax.switch(extra_mask[at], [functools.partial(hop, m) for m in masks], box)
            return lax.dynamic_update_slice_in_dim(extra, box, at, 0)

        extra = lax.fori_loop(1, extra_count[0], one_more, extra)
        return [got[m] for m in masks] + [early], extra

    current = orbitals
    side = need
    for round_idx in range(ROUNDS):
        last = round_idx == ROUNDS - 1
        recvs, extra = exchange(boxes, sends, send, extra)
        energy_shape = (devices, 1, 128) if last else (8, 128)
        out_shape = [jax.ShapeDtypeStruct((own, edge, plane), jnp.float32), jax.ShapeDtypeStruct(energy_shape, jnp.float32)]
        if not last:
            out_shape += [box_shape, one_box, *send_shapes]
        current, side, *rest = pl.pallas_call(
            functools.partial(pair_kernel, (columns, own, last)),
            out_shape=out_shape,
            in_specs=[SMEM, SMEM, SMEM, SMEM, VMEM if last else SMEM] + [ANY] * (8 + len(recvs)),
            out_specs=[ANY, VMEM] + [ANY] * (len(out_shape) - 2),
            scratch_shapes=([] if last else [send_sems])
            + [
                pltpu.VMEM((BATCH * edge, plane), jnp.float32),
                pltpu.VMEM((BATCH * edge, plane), jnp.float32),
                pltpu.VMEM(((BATCH + own) * edge, plane), jnp.float32),
                pltpu.VMEM((8, plane), jnp.float32),
                pltpu.VMEM((own, edge, plane), jnp.float32),
                pltpu.VMEM((own, edge, plane), jnp.bfloat16),
                pltpu.VMEM((owners * slots, edge, plane), jnp.bfloat16),
                pltpu.SemaphoreType.DMA((owners * slots,)),
                pltpu.SemaphoreType.DMA((8,)),
                pltpu.VMEM((plane, plane), jnp.bfloat16),
                pltpu.VMEM((plane, plane), jnp.bfloat16),
                pltpu.VMEM(tables.shape, jnp.float32),
                pltpu.VMEM(left_hi.shape, jnp.bfloat16),
                pltpu.VMEM(left_lo.shape, jnp.bfloat16),
                pltpu.VMEM((edge, plane), jnp.float32),
                pltpu.VMEM((own, edge, plane), jnp.float32),
                pltpu.VMEM((own, edge, plane), jnp.float32),
            ],
            name="pairs",
        )(plist, meta, first, extra_box, side, boxes, tables, left_hi, left_lo, gain, current, gradient, extra, *recvs)
        if not last:
            boxes, send, *sends = rest
    every = lax.all_to_all(side, ("row", "col"), 0, 0, tiled=True)
    energies = jnp.sum(every, (0, 1))[:ROUNDS] / (edge * edge * edge * devices)
    return current, energies


def solution(mesh):
    return jax.shard_map(
        local,
        mesh=mesh,
        in_specs=(
            P(("row", "col"), None, None),
            P(("row", "col"), None, None),
            P(),
            P("row", None, None),
            P("row"),
        ),
        out_specs=(P(("row", "col"), None, None), P()),
        check_vma=False,
    )
```

```python
import functools

import jax
import jax.numpy as jnp
import numpy as np
from jax import lax
from jax.experimental import pallas as pl
from jax.experimental.pallas import tpu as pltpu
from jax.sharding import PartitionSpec as P

SWEEPS = 12
ROUNDS = 2
BATCH = 4
FIELDS = 8

screen_mu = 0.1
damping = 0.5

SMEM = pl.BlockSpec(memory_space=pltpu.SMEM)
VMEM = pl.BlockSpec(memory_space=pltpu.VMEM)
ANY = pl.BlockSpec(memory_space=pl.ANY)


def split(values):
    high = values.astype(jnp.bfloat16)
    return high, (values - high.astype(jnp.float32)).astype(jnp.bfloat16)


def sine_basis(edge):
    index = np.arange(1, edge + 1)
    return np.sqrt(2.0 / (edge + 1)) * np.sin(np.pi * np.outer(index, index) / (edge + 1))


def solve_gain(edge):
    cosines = 2.0 * np.cos(np.pi * np.arange(1, edge + 1) / (edge + 1))
    eigen = 6.0 + screen_mu - (cosines[:, None, None] + cosines[None, :, None] + cosines[None, None, :])
    center, half = 6.0 + screen_mu, 6.0
    ratio = center / half
    prev = 1.0 / ratio
    gain, rest = np.zeros_like(eigen), np.ones_like(eigen)
    step = rest / center
    for _ in range(SWEEPS):
        gain = gain + step
        rest = rest - eigen * step
        coef = 1.0 / (2.0 * ratio - prev)
        step = coef * prev * step + (2.0 * coef / half) * rest
        prev = coef
    return gain.reshape(edge, edge * edge)


def dot(a, b):
    return jnp.dot(a, b, preferred_element_type=jnp.float32)


def capacity(mask, columns):
    return 2 if mask < columns // 2 else 1


def bits(word, size):
    return [(word >> b) & 1 for b in range(size)]


def owner_of(orbital, own):
    return orbital >> (own.bit_length() - 1) if own & (own - 1) == 0 else lax.div(orbital, own)


def each_pair(pairs, counts, slots, base, step):
    def owner_step(p, carry):
        def slot_step(k, carry):
            step(p, k, pairs[k, 0, p] - base, pairs[k, 1, p] - base)
            return carry

        return lax.fori_loop(0, jnp.minimum(counts[p], slots), slot_step, carry)

    lax.fori_loop(0, counts.shape[0], owner_step, 0)


def pack(columns, own, me, need, boxes, sends):
    for mask in range(1, columns):
        limit = capacity(mask, columns)
        rank = 0
        for b, bit in enumerate(bits(need[(me ^ mask) * columns + me], own)):
            place = rank if limit > 1 else 0

            @pl.when((bit != 0) & (rank < limit))
            def _():
                sends[mask - 1][place] = boxes[b]

            rank = rank + bit


def need_kernel(dims, pairs, counts, phi, need, boxes, *sends):
    columns, own, slots = dims
    me = lax.axis_index("col")
    base = lax.axis_index("row") * (columns * own)

    def clear(at, carry):
        for lane in range(columns):
            need[at * columns + lane] = 0
        return carry

    lax.fori_loop(0, columns, clear, 0)

    def step(p, k, first, second):
        source = owner_of(second, own)
        key = owner_of(first, own) * columns + source
        need[key] = need[key] | (1 << (second - source * own))

    each_pair(pairs, counts, slots, base, step)
    for b in range(own):
        boxes[b] = phi[b].astype(jnp.bfloat16)
    pack(columns, own, me, need, boxes, sends)


def plan_kernel(dims, need, pairs, counts, offsets, boxes, plist, meta, extra_count, first, extra_mask, extra_box, unset, send, start, sem):
    columns, own, slots = dims
    del unset
    me = lax.axis_index("col")
    base = lax.axis_index("row") * (columns * own)
    meta[0] = 0
    extra_count[0] = 0
    extra_mask[0] = 0
    extra_box[0] = 0
    for mask in range(1, columns):
        limit = capacity(mask, columns)
        start[mask] = extra_count[0]
        mine = bits(need[(me ^ mask) * columns + me], own)

        def most(c, carry):
            return jnp.maximum(carry, sum(bits(need[c * columns + (c ^ mask)], own)))

        longest = lax.fori_loop(0, columns, most, 0)
        for over in range(own - limit):

            @pl.when(longest > limit + over)
            def _():
                at = extra_count[0]
                extra_count[0] = at + 1
                rank, box = 0, 0
                for b, bit in enumerate(mine):
                    box = jnp.where((bit != 0) & (rank == limit + over), b, box)
                    rank = rank + bit
                extra_mask[at] = mask - 1
                extra_box[at] = box

    first[0] = jnp.where(extra_count[0] > 0, extra_mask[0] + 1, 0)

    def sent(act):
        @pl.when(extra_count[0] > 0)
        def _():
            act(pltpu.make_async_copy(boxes.at[pl.ds(extra_box[0], 1)], send, sem))

    sent(lambda copy: copy.start())

    def step(p, k, first, second):
        @pl.when(owner_of(first, own) == me)
        def _():
            source = owner_of(second, own)
            mask = me ^ source
            place = second - source * own
            rank = sum(bits(need[me * columns + source] & ((1 << place) - 1), own))
            limit = jnp.where(mask < columns // 2, 2, 1)
            fits = rank < limit
            at = meta[0] * FIELDS
            meta[0] = meta[0] + 1
            plist[at] = first - me * own
            plist[at + 1] = jnp.where((mask == 0) | fits, mask, columns)
            plist[at + 2] = jnp.where(mask == 0, place, jnp.where(fits, rank, start[mask] + rank - limit))
            for axis in range(3):
                plist[at + 3 + axis] = offsets[axis, first + base] - offsets[axis, second + base]
            opens, closes = jnp.int32(1), jnp.int32(1)
            for other in range(slots):
                same = (other < counts[p]) & (pairs[other, 0, p] - base == first)
                opens = jnp.where(same & (other < k), 0, opens)
                closes = jnp.where(same & (other > k), 0, closes)
            plist[at + 6] = opens
            plist[at + 7] = closes

    each_pair(pairs, counts, slots, base, step)
    sent(lambda copy: copy.wait())


def shifted(box, move):
    edge, plane = box.shape
    along_x, along_y, along_z = move
    flat = along_y * edge + along_z
    out = pltpu.roll(box, lax.rem(edge - along_x, edge), 0)
    out = pltpu.roll(out, lax.rem(plane - flat, plane), 1)
    row = lax.broadcasted_iota(jnp.int32, (edge, plane), 0) + along_x
    lane = lax.broadcasted_iota(jnp.int32, (edge, plane), 1)
    depth = (lane & (edge - 1)) + along_z
    lane = lane + (along_y * edge)
    keep = (row >= 0) & (row < edge) & (lane >= 0) & (lane < plane) & (depth >= 0) & (depth < edge)
    return jnp.where(keep, out, 0.0)


def pair_kernel(dims, plist, meta, first, extra_box, side, boxes, left_hi, left_lo, gain, basis_hi, basis_lo, base, gradient, extra, *rest):
    columns, own, last = dims
    recvs, (early, out, energy), rest = rest[: columns - 1], rest[columns - 1 : columns + 2], rest[columns + 2 :]
    partner, density, source, running, total, field, held, slope, right_hi, right_lo, sems = rest[-11:]
    edge, plane = gain.shape
    moves = ((basis_hi, right_hi), (basis_lo, right_lo), (base, held), (gradient, slope))
    copies = [pltpu.make_async_copy(there, here, sems.at[at]) for at, (there, here) in enumerate(moves)]
    for copy in copies:
        copy.start()
    field[...] = jnp.zeros_like(field)
    total[...] = jnp.zeros_like(total)
    count = meta[0]

    def along_left(values):
        high, low = split(values)
        return dot(left_hi[...], high) + (dot(left_hi[...], low) + dot(left_lo[...], high))

    def along_right(values):
        high, low = split(values)
        both = dot(jnp.concatenate([high, low], 0), right_hi[...])
        rows = values.shape[0]
        return both[:rows] + (both[rows:] + dot(high, right_lo[...]))

    def batch_step(index, carry):
        for s in range(BATCH):
            pair = index * BATCH + s
            rows = pl.ds(s * edge, edge)

            @pl.when(pair < count)
            def _():
                at = pair * FIELDS
                code = plist[at + 1]
                place = plist[at + 2]

                @pl.when(code == 0)
                def _():
                    source[...] = boxes[place]

                for m in range(1, columns):

                    @pl.when(code == m)
                    def _():
                        source[...] = recvs[m - 1][place if capacity(m, columns) > 1 else 0]

                @pl.when((code == columns) & (place == 0))
                def _():
                    source[...] = early[0]

                @pl.when((code == columns) & (place > 0))
                def _():
                    copy = pltpu.make_async_copy(extra.at[place], source, sems.at[4])
                    copy.start()
                    copy.wait()

                other = shifted(source[...].astype(jnp.float32), (plist[at + 3], plist[at + 4], plist[at + 5]))
                partner[rows, :] = other
                density[rows, :] = boxes[plist[at]].astype(jnp.float32) * other

            @pl.when(pair >= count)
            def _():
                density[rows, :] = jnp.zeros((edge, plane), jnp.float32)

        partly = along_left(density[...])

        @pl.when(index == 0)
        def _():
            for copy in copies[:2]:
                copy.wait()

        spectrum = along_right(partly)
        scaled = (spectrum.reshape(BATCH, edge, plane) * gain[...]).reshape(BATCH * edge, plane)
        potential = along_left(along_right(scaled))
        work = density[...] * potential
        total[...] += jnp.sum(work.reshape(BATCH * edge // 8, 8, plane), 0)
        for s in range(BATCH):
            pair = index * BATCH + s

            @pl.when(pair < count)
            def _():
                at = pair * FIELDS
                place = plist[at]
                rows = slice(s * edge, (s + 1) * edge)
                running[rows, :] = potential[rows] * partner[rows, :]

                @pl.when(plist[at + 6] == 0)
                def _():
                    running[rows, :] = running[rows, :] + partial(place)[...]

                @pl.when(plist[at + 7] == 0)
                def _():
                    partial(place)[...] = running[rows, :]

                @pl.when(plist[at + 7] != 0)
                def _():
                    rounded = running[rows, :].astype(jnp.bfloat16).astype(jnp.float32)
                    field[place] = field[place] + rounded

        return carry

    def partial(place):
        return running.at[pl.ds(pl.multiple_of((BATCH + place) * edge, edge), edge)]

    lax.fori_loop(0, lax.div(count + BATCH - 1, BATCH), batch_step, 0)

    @pl.when(count == 0)
    def _():
        for copy in copies[:2]:
            copy.wait()

    for copy in copies[2:]:
        copy.wait()
    for b in range(own):
        out[b] = held[b] - damping * (slope[b] + field[b])
    mine = jnp.sum(total[...])
    if last:
        lane = lax.broadcasted_iota(jnp.int32, (1, 128), 1)
        row = jnp.where(lane == 0, side[:1], jnp.where(lane == 1, mine, 0.0))
        for device in range(energy.shape[0]):
            energy[device] = row
    else:
        next_boxes, send, sends = rest[0], rest[1], rest[2:-11]
        energy[...] = jnp.full(energy.shape, mine)
        for b in range(own):
            next_boxes[b] = out[b].astype(jnp.bfloat16)
        pack(columns, own, lax.axis_index("col"), side, next_boxes, sends)

        @pl.when(first[0] > 0)
        def _():
            send[0] = next_boxes[extra_box[0]]


def local(orbitals, gradient, offsets, pairs, counts):
    own, edge, plane = orbitals.shape
    columns = lax.axis_size("col")
    devices = lax.axis_size("row") * columns
    owners, slots = pairs.shape[0], pairs.shape[1]
    masks = range(1, columns)
    basis = sine_basis(edge)
    basis_hi, basis_lo = split(jnp.asarray(np.kron(basis, basis), jnp.float32))
    left_hi, left_lo = split(jnp.asarray(np.kron(np.eye(BATCH), basis), jnp.float32))
    gain = jnp.asarray(solve_gain(edge), jnp.float32)
    box_shape = jax.ShapeDtypeStruct((own, edge, plane), jnp.bfloat16)
    send_shapes = [jax.ShapeDtypeStruct((capacity(m, columns), edge, plane), jnp.bfloat16) for m in masks]
    most_extra = sum(max(own - capacity(m, columns), 0) for m in masks)
    pairs = pairs.transpose(1, 2, 0)
    offsets = offsets.T

    one_box = jax.ShapeDtypeStruct((1, edge, plane), jnp.bfloat16)

    def ints(size):
        return jax.ShapeDtypeStruct((size,), jnp.int32)

    need, boxes, *sends = pl.pallas_call(
        functools.partial(need_kernel, (columns, own, slots)),
        out_shape=[ints(columns * columns), box_shape, *send_shapes],
        in_specs=[SMEM, SMEM, VMEM],
        out_specs=[SMEM, VMEM] + [VMEM] * len(send_shapes),
        name="need",
    )(pairs, counts, orbitals)
    plist, meta, extra_count, first, extra_mask, extra_box, extra, send = pl.pallas_call(
        functools.partial(plan_kernel, (columns, own, slots)),
        out_shape=[
            ints(owners * slots * FIELDS),
            ints(1),
            ints(1),
            ints(1),
            ints(most_extra),
            ints(most_extra),
            jax.ShapeDtypeStruct((most_extra, edge, plane), jnp.bfloat16),
            one_box,
        ],
        in_specs=[SMEM] * 4 + [ANY],
        out_specs=[SMEM] * 6 + [ANY, ANY],
        scratch_shapes=[pltpu.SMEM((columns,), jnp.int32), pltpu.SemaphoreType.DMA],
        name="plan",
    )(need, pairs, counts, offsets, boxes)

    def hop(mask, values):
        return lax.ppermute(values, "col", [(c, c ^ mask) for c in range(columns)])

    def exchange(boxes, sends, send, extra):
        got = {m: hop(m, sends[m - 1]) for m in reversed(masks)}
        early = lax.switch(first[0], [lambda box: box] + [functools.partial(hop, m) for m in masks], send)

        def one_more(at, extra):
            box = lax.dynamic_index_in_dim(boxes, extra_box[at], 0, True)
            box = lax.switch(extra_mask[at], [functools.partial(hop, m) for m in masks], box)
            return lax.dynamic_update_slice_in_dim(extra, box, at, 0)

        extra = lax.fori_loop(1, extra_count[0], one_more, extra)
        return [got[m] for m in masks] + [early], extra

    current = orbitals
    side = need
    for round_idx in range(ROUNDS):
        last = round_idx == ROUNDS - 1
        recvs, extra = exchange(boxes, sends, send, extra)
        energy_shape = (devices, 1, 128) if last else (8, 128)
        out_shape = [jax.ShapeDtypeStruct((own, edge, plane), jnp.float32), jax.ShapeDtypeStruct(energy_shape, jnp.float32)]
        if not last:
            out_shape += [box_shape, one_box, *send_shapes]
        current, side, *rest = pl.pallas_call(
            functools.partial(pair_kernel, (columns, own, last)),
            out_shape=out_shape,
            in_specs=[SMEM] * 4 + [VMEM if last else SMEM] + [VMEM] * 4 + [ANY] * 5 + [VMEM] * len(recvs),
            out_specs=[VMEM] * len(out_shape),
            scratch_shapes=[
                pltpu.VMEM((BATCH * edge, plane), jnp.float32),
                pltpu.VMEM((BATCH * edge, plane), jnp.float32),
                pltpu.VMEM((edge, plane), jnp.bfloat16),
                pltpu.VMEM(((BATCH + own) * edge, plane), jnp.float32),
                pltpu.VMEM((8, plane), jnp.float32),
                pltpu.VMEM((own, edge, plane), jnp.float32),
                pltpu.VMEM((own, edge, plane), jnp.float32),
                pltpu.VMEM((own, edge, plane), jnp.float32),
                pltpu.VMEM((plane, plane), jnp.bfloat16),
                pltpu.VMEM((plane, plane), jnp.bfloat16),
                pltpu.SemaphoreType.DMA((5,)),
            ],
            name="pairs",
        )(plist, meta, first, extra_box, side, boxes, left_hi, left_lo, gain, basis_hi, basis_lo, current, gradient, extra, *recvs)
        if not last:
            boxes, send, *sends = rest
    every = lax.all_to_all(side, ("row", "col"), 0, 0, tiled=True)
    energies = jnp.sum(every, (0, 1))[:ROUNDS] / (edge * edge * edge * devices)
    return current, energies


def solution(mesh):
    return jax.shard_map(
        local,
        mesh=mesh,
        in_specs=(
            P(("row", "col"), None, None),
            P(("row", "col"), None, None),
            P(),
            P("row", None, None),
            P("row"),
        ),
        out_specs=(P(("row", "col"), None, None), P()),
        check_vma=False,
    )
```

```python
import functools

import jax
import jax.numpy as jnp
import numpy as np
from jax import lax
from jax.experimental import pallas as pl
from jax.experimental.pallas import tpu as pltpu
from jax.sharding import PartitionSpec as P

SWEEPS = 12
ROUNDS = 2
BATCH = 4
FIELDS = 8

screen_mu = 0.1
damping = 0.5

SMEM = pl.BlockSpec(memory_space=pltpu.SMEM)
VMEM = pl.BlockSpec(memory_space=pltpu.VMEM)
ANY = pl.BlockSpec(memory_space=pl.ANY)


def split(values):
    high = values.astype(jnp.bfloat16)
    return high, (values - high.astype(jnp.float32)).astype(jnp.bfloat16)


def sine_basis(edge):
    index = np.arange(1, edge + 1)
    return np.sqrt(2.0 / (edge + 1)) * np.sin(np.pi * np.outer(index, index) / (edge + 1))


def solve_gain(edge):
    cosines = 2.0 * np.cos(np.pi * np.arange(1, edge + 1) / (edge + 1))
    eigen = 6.0 + screen_mu - (cosines[:, None, None] + cosines[None, :, None] + cosines[None, None, :])
    center, half = 6.0 + screen_mu, 6.0
    ratio = center / half
    prev = 1.0 / ratio
    gain, rest = np.zeros_like(eigen), np.ones_like(eigen)
    step = rest / center
    for _ in range(SWEEPS):
        gain = gain + step
        rest = rest - eigen * step
        coef = 1.0 / (2.0 * ratio - prev)
        step = coef * prev * step + (2.0 * coef / half) * rest
        prev = coef
    return gain.reshape(edge, edge * edge)


def dot(a, b):
    return jnp.dot(a, b, preferred_element_type=jnp.float32)


def capacity(mask, columns):
    return 2 if mask < columns // 2 else 1


def bits(word, size):
    return [(word >> b) & 1 for b in range(size)]


def owner_of(orbital, own):
    return orbital >> (own.bit_length() - 1) if own & (own - 1) == 0 else lax.div(orbital, own)


def each_pair(pairs, counts, slots, base, step):
    def owner_step(p, carry):
        def slot_step(k, carry):
            step(p, k, pairs[k, 0, p] - base, pairs[k, 1, p] - base)
            return carry

        return lax.fori_loop(0, jnp.minimum(counts[p], slots), slot_step, carry)

    lax.fori_loop(0, counts.shape[0], owner_step, 0)


def pack(columns, own, me, need, boxes, sends):
    for mask in range(1, columns):
        limit = capacity(mask, columns)
        rank = 0
        for b, bit in enumerate(bits(need[(me ^ mask) * columns + me], own)):
            place = rank if limit > 1 else 0

            @pl.when((bit != 0) & (rank < limit))
            def _():
                sends[mask - 1][place] = boxes[b]

            rank = rank + bit


def need_kernel(dims, pairs, counts, phi, need, boxes, *sends):
    columns, own, slots = dims
    me = lax.axis_index("col")
    base = lax.axis_index("row") * (columns * own)

    def clear(at, carry):
        for lane in range(columns):
            need[at * columns + lane] = 0
        return carry

    lax.fori_loop(0, columns, clear, 0)

    def step(p, k, first, second):
        source = owner_of(second, own)
        key = owner_of(first, own) * columns + source
        need[key] = need[key] | (1 << (second - source * own))

    each_pair(pairs, counts, slots, base, step)
    for b in range(own):
        boxes[b] = phi[b].astype(jnp.bfloat16)
    pack(columns, own, me, need, boxes, sends)


def plan_kernel(dims, need, pairs, counts, offsets, boxes, plist, meta, extra_count, first, extra_mask, extra_box, unset, send, start, sem):
    columns, own, slots = dims
    del unset
    me = lax.axis_index("col")
    base = lax.axis_index("row") * (columns * own)
    meta[0] = 0
    extra_count[0] = 0
    extra_mask[0] = 0
    extra_box[0] = 0
    for mask in range(1, columns):
        limit = capacity(mask, columns)
        start[mask] = extra_count[0]
        mine = bits(need[(me ^ mask) * columns + me], own)

        def most(c, carry):
            return jnp.maximum(carry, sum(bits(need[c * columns + (c ^ mask)], own)))

        longest = lax.fori_loop(0, columns, most, 0)
        for over in range(own - limit):

            @pl.when(longest > limit + over)
            def _():
                at = extra_count[0]
                extra_count[0] = at + 1
                rank, box = 0, 0
                for b, bit in enumerate(mine):
                    box = jnp.where((bit != 0) & (rank == limit + over), b, box)
                    rank = rank + bit
                extra_mask[at] = mask - 1
                extra_box[at] = box

    first[0] = jnp.where(extra_count[0] > 0, extra_mask[0] + 1, 0)

    def sent(act):
        @pl.when(extra_count[0] > 0)
        def _():
            act(pltpu.make_async_copy(boxes.at[pl.ds(extra_box[0], 1)], send, sem))

    sent(lambda copy: copy.start())

    def step(p, k, first, second):
        @pl.when(owner_of(first, own) == me)
        def _():
            source = owner_of(second, own)
            mask = me ^ source
            place = second - source * own
            rank = sum(bits(need[me * columns + source] & ((1 << place) - 1), own))
            limit = jnp.where(mask < columns // 2, 2, 1)
            fits = rank < limit
            at = meta[0] * FIELDS
            meta[0] = meta[0] + 1
            plist[at] = first - me * own
            plist[at + 1] = jnp.where((mask == 0) | fits, mask, columns)
            plist[at + 2] = jnp.where(mask == 0, place, jnp.where(fits, rank, start[mask] + rank - limit))
            for axis in range(3):
                plist[at + 3 + axis] = offsets[axis, first + base] - offsets[axis, second + base]
            opens, closes = jnp.int32(1), jnp.int32(1)
            for other in range(slots):
                same = (other < counts[p]) & (pairs[other, 0, p] - base == first)
                opens = jnp.where(same & (other < k), 0, opens)
                closes = jnp.where(same & (other > k), 0, closes)
            plist[at + 6] = opens
            plist[at + 7] = closes

    each_pair(pairs, counts, slots, base, step)
    sent(lambda copy: copy.wait())


def shifted(box, move):
    edge, plane = box.shape
    along_x, along_y, along_z = move
    flat = along_y * edge + along_z
    out = pltpu.roll(box, lax.rem(edge - along_x, edge), 0)
    out = pltpu.roll(out, lax.rem(plane - flat, plane), 1)
    row = lax.broadcasted_iota(jnp.int32, (edge, plane), 0) + along_x
    lane = lax.broadcasted_iota(jnp.int32, (edge, plane), 1)
    depth = (lane & (edge - 1)) + along_z
    lane = lane + (along_y * edge)
    keep = (row >= 0) & (row < edge) & (lane >= 0) & (lane < plane) & (depth >= 0) & (depth < edge)
    return jnp.where(keep, out, 0.0)


def pair_kernel(dims, plist, meta, first, extra_box, side, boxes, left_hi, left_lo, gain, basis_hi, basis_lo, base, gradient, extra, *rest):
    columns, own, last = dims
    recvs, (early, out, energy), rest = rest[: columns - 1], rest[columns - 1 : columns + 2], rest[columns + 2 :]
    partner, density, source, running, total, field, held, slope, right_hi, right_lo, sems = rest[-11:]
    edge, plane = gain.shape
    halves = [pl.ds(0, plane // 2), pl.ds(plane // 2, plane // 2)]
    moves = [(there.at[half], here.at[half]) for half in halves for there, here in ((basis_hi, right_hi), (basis_lo, right_lo))]
    moves += [(base, held), (gradient, slope)]
    copies = [pltpu.make_async_copy(there, here, sems.at[at]) for at, (there, here) in enumerate(moves)]
    for copy in copies[:4]:
        copy.start()
    field[...] = jnp.zeros_like(field)
    total[...] = jnp.zeros_like(total)
    count = meta[0]

    def turn():
        for copy in copies[:4]:
            copy.wait()
        for copy in copies[4:]:
            copy.start()

    def along_left(values):
        high, low = split(values)
        return dot(left_hi[...], high) + (dot(left_hi[...], low) + dot(left_lo[...], high))

    def along_right(values):
        high, low = split(values)
        both = dot(jnp.concatenate([high, low], 0), right_hi[...])
        rows = values.shape[0]
        return both[:rows] + (both[rows:] + dot(high, right_lo[...]))

    def batch_step(index, carry):
        for s in range(BATCH):
            pair = index * BATCH + s
            rows = pl.ds(s * edge, edge)

            @pl.when(pair < count)
            def _():
                at = pair * FIELDS
                code = plist[at + 1]
                place = plist[at + 2]

                @pl.when(code == 0)
                def _():
                    source[...] = boxes[place]

                for m in range(1, columns):

                    @pl.when(code == m)
                    def _():
                        source[...] = recvs[m - 1][place if capacity(m, columns) > 1 else 0]

                @pl.when((code == columns) & (place == 0))
                def _():
                    source[...] = early[0]

                @pl.when((code == columns) & (place > 0))
                def _():
                    copy = pltpu.make_async_copy(extra.at[place], source, sems.at[6])
                    copy.start()
                    copy.wait()

                other = shifted(source[...].astype(jnp.float32), (plist[at + 3], plist[at + 4], plist[at + 5]))
                partner[rows, :] = other
                density[rows, :] = boxes[plist[at]].astype(jnp.float32) * other

            @pl.when(pair >= count)
            def _():
                density[rows, :] = jnp.zeros((edge, plane), jnp.float32)

        partly = along_left(density[...])

        @pl.when(index == 0)
        def _():
            turn()

        spectrum = along_right(partly)
        scaled = (spectrum.reshape(BATCH, edge, plane) * gain[...]).reshape(BATCH * edge, plane)
        potential = along_left(along_right(scaled))
        work = density[...] * potential
        total[...] += jnp.sum(work.reshape(BATCH * edge // 8, 8, plane), 0)
        for s in range(BATCH):
            pair = index * BATCH + s

            @pl.when(pair < count)
            def _():
                at = pair * FIELDS
                place = plist[at]
                rows = slice(s * edge, (s + 1) * edge)
                running[rows, :] = potential[rows] * partner[rows, :]

                @pl.when(plist[at + 6] == 0)
                def _():
                    running[rows, :] = running[rows, :] + partial(place)[...]

                @pl.when(plist[at + 7] == 0)
                def _():
                    partial(place)[...] = running[rows, :]

                @pl.when(plist[at + 7] != 0)
                def _():
                    rounded = running[rows, :].astype(jnp.bfloat16).astype(jnp.float32)
                    field[place] = field[place] + rounded

        return carry

    def partial(place):
        return running.at[pl.ds(pl.multiple_of((BATCH + place) * edge, edge), edge)]

    lax.fori_loop(0, lax.div(count + BATCH - 1, BATCH), batch_step, 0)

    @pl.when(count == 0)
    def _():
        turn()

    for copy in copies[4:]:
        copy.wait()
    for b in range(own):
        out[b] = held[b] - damping * (slope[b] + field[b])
    mine = jnp.sum(total[...])
    if last:
        lane = lax.broadcasted_iota(jnp.int32, (1, 128), 1)
        row = jnp.where(lane == 0, side[:1], jnp.where(lane == 1, mine, 0.0))
        for device in range(energy.shape[0]):
            energy[device] = row
    else:
        next_boxes, send, sends = rest[0], rest[1], rest[2:-11]
        energy[...] = jnp.full(energy.shape, mine)
        for b in range(own):
            next_boxes[b] = out[b].astype(jnp.bfloat16)
        pack(columns, own, lax.axis_index("col"), side, next_boxes, sends)

        @pl.when(first[0] > 0)
        def _():
            send[0] = next_boxes[extra_box[0]]


def local(orbitals, gradient, offsets, pairs, counts):
    own, edge, plane = orbitals.shape
    columns = lax.axis_size("col")
    devices = lax.axis_size("row") * columns
    owners, slots = pairs.shape[0], pairs.shape[1]
    masks = range(1, columns)
    basis = sine_basis(edge)
    basis_hi, basis_lo = split(jnp.asarray(np.kron(basis, basis), jnp.float32))
    left_hi, left_lo = split(jnp.asarray(np.kron(np.eye(BATCH), basis), jnp.float32))
    gain = jnp.asarray(solve_gain(edge), jnp.float32)
    box_shape = jax.ShapeDtypeStruct((own, edge, plane), jnp.bfloat16)
    send_shapes = [jax.ShapeDtypeStruct((capacity(m, columns), edge, plane), jnp.bfloat16) for m in masks]
    most_extra = sum(max(own - capacity(m, columns), 0) for m in masks)
    pairs = pairs.transpose(1, 2, 0)
    offsets = offsets.T

    one_box = jax.ShapeDtypeStruct((1, edge, plane), jnp.bfloat16)

    def ints(size):
        return jax.ShapeDtypeStruct((size,), jnp.int32)

    need, boxes, *sends = pl.pallas_call(
        functools.partial(need_kernel, (columns, own, slots)),
        out_shape=[ints(columns * columns), box_shape, *send_shapes],
        in_specs=[SMEM, SMEM, VMEM],
        out_specs=[SMEM, VMEM] + [VMEM] * len(send_shapes),
        name="need",
    )(pairs, counts, orbitals)
    plist, meta, extra_count, first, extra_mask, extra_box, extra, send = pl.pallas_call(
        functools.partial(plan_kernel, (columns, own, slots)),
        out_shape=[
            ints(owners * slots * FIELDS),
            ints(1),
            ints(1),
            ints(1),
            ints(most_extra),
            ints(most_extra),
            jax.ShapeDtypeStruct((most_extra, edge, plane), jnp.bfloat16),
            one_box,
        ],
        in_specs=[SMEM] * 4 + [ANY],
        out_specs=[SMEM] * 6 + [ANY, ANY],
        scratch_shapes=[pltpu.SMEM((columns,), jnp.int32), pltpu.SemaphoreType.DMA],
        name="plan",
    )(need, pairs, counts, offsets, boxes)

    def hop(mask, values):
        return lax.ppermute(values, "col", [(c, c ^ mask) for c in range(columns)])

    def exchange(boxes, sends, send, extra):
        got = {m: hop(m, sends[m - 1]) for m in reversed(masks)}
        early = lax.switch(first[0], [lambda box: box] + [functools.partial(hop, m) for m in masks], send)

        def one_more(at, extra):
            box = lax.dynamic_index_in_dim(boxes, extra_box[at], 0, True)
            box = lax.switch(extra_mask[at], [functools.partial(hop, m) for m in masks], box)
            return lax.dynamic_update_slice_in_dim(extra, box, at, 0)

        extra = lax.fori_loop(1, extra_count[0], one_more, extra)
        return [got[m] for m in masks] + [early], extra

    current = orbitals
    side = need
    for round_idx in range(ROUNDS):
        last = round_idx == ROUNDS - 1
        recvs, extra = exchange(boxes, sends, send, extra)
        energy_shape = (devices, 1, 128) if last else (8, 128)
        out_shape = [jax.ShapeDtypeStruct((own, edge, plane), jnp.float32), jax.ShapeDtypeStruct(energy_shape, jnp.float32)]
        if not last:
            out_shape += [box_shape, one_box, *send_shapes]
        current, side, *rest = pl.pallas_call(
            functools.partial(pair_kernel, (columns, own, last)),
            out_shape=out_shape,
            in_specs=[SMEM] * 4 + [VMEM if last else SMEM] + [VMEM] * 4 + [ANY] * 5 + [VMEM] * len(recvs),
            out_specs=[VMEM] * len(out_shape),
            scratch_shapes=[
                pltpu.VMEM((BATCH * edge, plane), jnp.float32),
                pltpu.VMEM((BATCH * edge, plane), jnp.float32),
                pltpu.VMEM((edge, plane), jnp.bfloat16),
                pltpu.VMEM(((BATCH + own) * edge, plane), jnp.float32),
                pltpu.VMEM((8, plane), jnp.float32),
                pltpu.VMEM((own, edge, plane), jnp.float32),
                pltpu.VMEM((own, edge, plane), jnp.float32),
                pltpu.VMEM((own, edge, plane), jnp.float32),
                pltpu.VMEM((plane, plane), jnp.bfloat16),
                pltpu.VMEM((plane, plane), jnp.bfloat16),
                pltpu.SemaphoreType.DMA((7,)),
            ],
            name="pairs",
        )(plist, meta, first, extra_box, side, boxes, left_hi, left_lo, gain, basis_hi, basis_lo, current, gradient, extra, *recvs)
        if not last:
            boxes, send, *sends = rest
    every = lax.all_to_all(side, ("row", "col"), 0, 0, tiled=True)
    energies = jnp.sum(every, (0, 1))[:ROUNDS] / (edge * edge * edge * devices)
    return current, energies


def solution(mesh):
    return jax.shard_map(
        local,
        mesh=mesh,
        in_specs=(
            P(("row", "col"), None, None),
            P(("row", "col"), None, None),
            P(),
            P("row", None, None),
            P("row"),
        ),
        out_specs=(P(("row", "col"), None, None), P()),
        check_vma=False,
    )
```

```python
import functools

import jax
import jax.numpy as jnp
import numpy as np
from jax import lax
from jax.experimental import pallas as pl
from jax.experimental.pallas import tpu as pltpu
from jax.sharding import PartitionSpec as P

SWEEPS = 12
ROUNDS = 2
BATCH = 4
FIELDS = 8

screen_mu = 0.1
damping = 0.5

SMEM = pl.BlockSpec(memory_space=pltpu.SMEM)
VMEM = pl.BlockSpec(memory_space=pltpu.VMEM)
ANY = pl.BlockSpec(memory_space=pl.ANY)


def split(values):
    high = values.astype(jnp.bfloat16)
    return high, (values - high.astype(jnp.float32)).astype(jnp.bfloat16)


def sine_basis(edge):
    index = np.arange(1, edge + 1)
    return np.sqrt(2.0 / (edge + 1)) * np.sin(np.pi * np.outer(index, index) / (edge + 1))


def solve_gain(edge):
    cosines = 2.0 * np.cos(np.pi * np.arange(1, edge + 1) / (edge + 1))
    eigen = 6.0 + screen_mu - (cosines[:, None, None] + cosines[None, :, None] + cosines[None, None, :])
    center, half = 6.0 + screen_mu, 6.0
    ratio = center / half
    prev = 1.0 / ratio
    gain, rest = np.zeros_like(eigen), np.ones_like(eigen)
    step = rest / center
    for _ in range(SWEEPS):
        gain = gain + step
        rest = rest - eigen * step
        coef = 1.0 / (2.0 * ratio - prev)
        step = coef * prev * step + (2.0 * coef / half) * rest
        prev = coef
    return gain.reshape(edge, edge * edge)


def dot(a, b):
    return jnp.dot(a, b, preferred_element_type=jnp.float32)


def capacity(mask, columns):
    return 2 if mask < columns // 2 else 1


def bits(word, size):
    return [(word >> b) & 1 for b in range(size)]


def owner_of(orbital, own):
    return orbital >> (own.bit_length() - 1) if own & (own - 1) == 0 else lax.div(orbital, own)


def each_pair(pairs, counts, slots, base, step):
    def owner_step(p, carry):
        def slot_step(k, carry):
            step(p, k, pairs[k, 0, p] - base, pairs[k, 1, p] - base)
            return carry

        return lax.fori_loop(0, jnp.minimum(counts[p], slots), slot_step, carry)

    lax.fori_loop(0, counts.shape[0], owner_step, 0)


def pack(columns, own, me, need, boxes, sends):
    for mask in range(1, columns):
        limit = capacity(mask, columns)
        rank = 0
        for b, bit in enumerate(bits(need[(me ^ mask) * columns + me], own)):
            place = rank if limit > 1 else 0

            @pl.when((bit != 0) & (rank < limit))
            def _():
                sends[mask - 1][place] = boxes[b]

            rank = rank + bit


def need_kernel(dims, pairs, counts, phi, need, boxes, *sends):
    columns, own, slots = dims
    me = lax.axis_index("col")
    base = lax.axis_index("row") * (columns * own)

    def clear(at, carry):
        for lane in range(columns):
            need[at * columns + lane] = 0
        return carry

    lax.fori_loop(0, columns, clear, 0)

    def step(p, k, first, second):
        source = owner_of(second, own)
        key = owner_of(first, own) * columns + source
        need[key] = need[key] | (1 << (second - source * own))

    each_pair(pairs, counts, slots, base, step)
    for b in range(own):
        boxes[b] = phi[b].astype(jnp.bfloat16)
    pack(columns, own, me, need, boxes, sends)


def plan_kernel(dims, need, pairs, counts, offsets, boxes, plist, meta, extra_count, first, extra_mask, extra_box, unset, send, start, sem):
    columns, own, slots = dims
    del unset
    me = lax.axis_index("col")
    base = lax.axis_index("row") * (columns * own)
    meta[0] = 0
    extra_count[0] = 0
    extra_mask[0] = 0
    extra_box[0] = 0
    for mask in range(1, columns):
        limit = capacity(mask, columns)
        start[mask] = extra_count[0]
        mine = bits(need[(me ^ mask) * columns + me], own)

        def most(c, carry):
            return jnp.maximum(carry, sum(bits(need[c * columns + (c ^ mask)], own)))

        longest = lax.fori_loop(0, columns, most, 0)
        for over in range(own - limit):

            @pl.when(longest > limit + over)
            def _():
                at = extra_count[0]
                extra_count[0] = at + 1
                rank, box = 0, 0
                for b, bit in enumerate(mine):
                    box = jnp.where((bit != 0) & (rank == limit + over), b, box)
                    rank = rank + bit
                extra_mask[at] = mask - 1
                extra_box[at] = box

    first[0] = jnp.where(extra_count[0] > 0, extra_mask[0] + 1, 0)

    def sent(act):
        @pl.when(extra_count[0] > 0)
        def _():
            act(pltpu.make_async_copy(boxes.at[pl.ds(extra_box[0], 1)], send, sem))

    sent(lambda copy: copy.start())

    def step(p, k, first, second):
        @pl.when(owner_of(first, own) == me)
        def _():
            source = owner_of(second, own)
            mask = me ^ source
            place = second - source * own
            rank = sum(bits(need[me * columns + source] & ((1 << place) - 1), own))
            limit = jnp.where(mask < columns // 2, 2, 1)
            fits = rank < limit
            at = meta[0] * FIELDS
            meta[0] = meta[0] + 1
            plist[at] = first - me * own
            plist[at + 1] = jnp.where((mask == 0) | fits, mask, columns)
            plist[at + 2] = jnp.where(mask == 0, place, jnp.where(fits, rank, start[mask] + rank - limit))
            for axis in range(3):
                plist[at + 3 + axis] = offsets[axis, first + base] - offsets[axis, second + base]
            opens, closes = jnp.int32(1), jnp.int32(1)
            for other in range(slots):
                same = (other < counts[p]) & (pairs[other, 0, p] - base == first)
                opens = jnp.where(same & (other < k), 0, opens)
                closes = jnp.where(same & (other > k), 0, closes)
            plist[at + 6] = opens
            plist[at + 7] = closes

    each_pair(pairs, counts, slots, base, step)
    sent(lambda copy: copy.wait())


def shifted(box, move):
    edge, plane = box.shape
    along_x, along_y, along_z = move
    flat = along_y * edge + along_z
    out = pltpu.roll(box, lax.rem(edge - along_x, edge), 0)
    out = pltpu.roll(out, lax.rem(plane - flat, plane), 1)
    row = lax.broadcasted_iota(jnp.int32, (edge, plane), 0) + along_x
    lane = lax.broadcasted_iota(jnp.int32, (edge, plane), 1)
    depth = (lane & (edge - 1)) + along_z
    lane = lane + (along_y * edge)
    keep = (row >= 0) & (row < edge) & (lane >= 0) & (lane < plane) & (depth >= 0) & (depth < edge)
    return jnp.where(keep, out, 0.0)


def pair_kernel(dims, plist, meta, first, extra_box, side, boxes, base, gradient, left_hi, left_lo, gain, basis_hi, basis_lo, extra, *rest):
    columns, own, last = dims
    recvs, (early, out, energy), rest = rest[: columns - 1], rest[columns - 1 : columns + 2], rest[columns + 2 :]
    partner, density, source, running, total, right_hi, right_lo, sems = rest[-8:]
    edge, plane = gain.shape
    moves = ((basis_hi, right_hi), (basis_lo, right_lo))
    copies = [pltpu.make_async_copy(there, here, sems.at[at]) for at, (there, here) in enumerate(moves)]
    for copy in copies:
        copy.start()
    for b in range(own):
        out[b] = base[b] - damping * gradient[b]
    total[...] = jnp.zeros_like(total)
    count = meta[0]

    def along_left(values):
        high, low = split(values)
        return dot(left_hi[...], high) + (dot(left_hi[...], low) + dot(left_lo[...], high))

    def along_right(values):
        high, low = split(values)
        both = dot(jnp.concatenate([high, low], 0), right_hi[...])
        rows = values.shape[0]
        return both[:rows] + (both[rows:] + dot(high, right_lo[...]))

    def batch_step(index, carry):
        for s in range(BATCH):
            pair = index * BATCH + s
            rows = pl.ds(s * edge, edge)

            @pl.when(pair < count)
            def _():
                at = pair * FIELDS
                code = plist[at + 1]
                place = plist[at + 2]

                @pl.when(code == 0)
                def _():
                    source[...] = boxes[place]

                for m in range(1, columns):

                    @pl.when(code == m)
                    def _():
                        source[...] = recvs[m - 1][place if capacity(m, columns) > 1 else 0]

                @pl.when((code == columns) & (place == 0))
                def _():
                    source[...] = early[0]

                @pl.when((code == columns) & (place > 0))
                def _():
                    copy = pltpu.make_async_copy(extra.at[place], source, sems.at[2])
                    copy.start()
                    copy.wait()

                other = shifted(source[...].astype(jnp.float32), (plist[at + 3], plist[at + 4], plist[at + 5]))
                partner[rows, :] = other
                density[rows, :] = boxes[plist[at]].astype(jnp.float32) * other

            @pl.when(pair >= count)
            def _():
                density[rows, :] = jnp.zeros((edge, plane), jnp.float32)

        @pl.when(index == 0)
        def _():
            for copy in copies:
                copy.wait()

        spectrum = along_right(along_left(density[...]))
        scaled = (spectrum.reshape(BATCH, edge, plane) * gain[...]).reshape(BATCH * edge, plane)
        potential = along_left(along_right(scaled))
        work = density[...] * potential
        total[...] += jnp.sum(work.reshape(BATCH * edge // 8, 8, plane), 0)
        for s in range(BATCH):
            pair = index * BATCH + s

            @pl.when(pair < count)
            def _():
                at = pair * FIELDS
                place = plist[at]
                rows = slice(s * edge, (s + 1) * edge)
                running[rows, :] = potential[rows] * partner[rows, :]

                @pl.when(plist[at + 6] == 0)
                def _():
                    running[rows, :] = running[rows, :] + partial(place)[...]

                @pl.when(plist[at + 7] == 0)
                def _():
                    partial(place)[...] = running[rows, :]

                @pl.when(plist[at + 7] != 0)
                def _():
                    rounded = running[rows, :].astype(jnp.bfloat16).astype(jnp.float32)
                    out[place] = out[place] - damping * rounded

        return carry

    def partial(place):
        return running.at[pl.ds(pl.multiple_of((BATCH + place) * edge, edge), edge)]

    lax.fori_loop(0, lax.div(count + BATCH - 1, BATCH), batch_step, 0)

    @pl.when(count == 0)
    def _():
        for copy in copies:
            copy.wait()

    mine = jnp.sum(total[...])
    if last:
        lane = lax.broadcasted_iota(jnp.int32, (1, 128), 1)
        row = jnp.where(lane == 0, side[:1], jnp.where(lane == 1, mine, 0.0))
        for device in range(energy.shape[0]):
            energy[device] = row
    else:
        next_boxes, send, sends = rest[0], rest[1], rest[2:-8]
        energy[...] = jnp.full(energy.shape, mine)
        for b in range(own):
            next_boxes[b] = out[b].astype(jnp.bfloat16)
        pack(columns, own, lax.axis_index("col"), side, next_boxes, sends)

        @pl.when(first[0] > 0)
        def _():
            send[0] = next_boxes[extra_box[0]]


def local(orbitals, gradient, offsets, pairs, counts):
    own, edge, plane = orbitals.shape
    columns = lax.axis_size("col")
    devices = lax.axis_size("row") * columns
    owners, slots = pairs.shape[0], pairs.shape[1]
    masks = range(1, columns)
    basis = sine_basis(edge)
    basis_hi, basis_lo = split(jnp.asarray(np.kron(basis, basis), jnp.float32))
    left_hi, left_lo = split(jnp.asarray(np.kron(np.eye(BATCH), basis), jnp.float32))
    gain = jnp.asarray(solve_gain(edge), jnp.float32)
    box_shape = jax.ShapeDtypeStruct((own, edge, plane), jnp.bfloat16)
    send_shapes = [jax.ShapeDtypeStruct((capacity(m, columns), edge, plane), jnp.bfloat16) for m in masks]
    most_extra = sum(max(own - capacity(m, columns), 0) for m in masks)
    pairs = pairs.transpose(1, 2, 0)
    offsets = offsets.T

    one_box = jax.ShapeDtypeStruct((1, edge, plane), jnp.bfloat16)

    def ints(size):
        return jax.ShapeDtypeStruct((size,), jnp.int32)

    need, boxes, *sends = pl.pallas_call(
        functools.partial(need_kernel, (columns, own, slots)),
        out_shape=[ints(columns * columns), box_shape, *send_shapes],
        in_specs=[SMEM, SMEM, VMEM],
        out_specs=[SMEM, VMEM] + [VMEM] * len(send_shapes),
        name="need",
    )(pairs, counts, orbitals)
    plist, meta, extra_count, first, extra_mask, extra_box, extra, send = pl.pallas_call(
        functools.partial(plan_kernel, (columns, own, slots)),
        out_shape=[
            ints(owners * slots * FIELDS),
            ints(1),
            ints(1),
            ints(1),
            ints(most_extra),
            ints(most_extra),
            jax.ShapeDtypeStruct((most_extra, edge, plane), jnp.bfloat16),
            one_box,
        ],
        in_specs=[SMEM] * 4 + [ANY],
        out_specs=[SMEM] * 6 + [ANY, ANY],
        scratch_shapes=[pltpu.SMEM((columns,), jnp.int32), pltpu.SemaphoreType.DMA],
        name="plan",
    )(need, pairs, counts, offsets, boxes)

    def hop(mask, values):
        return lax.ppermute(values, "col", [(c, c ^ mask) for c in range(columns)])

    def exchange(boxes, sends, send, extra):
        got = {m: hop(m, sends[m - 1]) for m in reversed(masks)}
        early = lax.switch(first[0], [lambda box: box] + [functools.partial(hop, m) for m in masks], send)

        def one_more(at, extra):
            box = lax.dynamic_index_in_dim(boxes, extra_box[at], 0, True)
            box = lax.switch(extra_mask[at], [functools.partial(hop, m) for m in masks], box)
            return lax.dynamic_update_slice_in_dim(extra, box, at, 0)

        extra = lax.fori_loop(1, extra_count[0], one_more, extra)
        return [got[m] for m in masks] + [early], extra

    current = orbitals
    side = need
    for round_idx in range(ROUNDS):
        last = round_idx == ROUNDS - 1
        recvs, extra = exchange(boxes, sends, send, extra)
        energy_shape = (devices, 1, 128) if last else (8, 128)
        out_shape = [jax.ShapeDtypeStruct((own, edge, plane), jnp.float32), jax.ShapeDtypeStruct(energy_shape, jnp.float32)]
        if not last:
            out_shape += [box_shape, one_box, *send_shapes]
        current, side, *rest = pl.pallas_call(
            functools.partial(pair_kernel, (columns, own, last)),
            out_shape=out_shape,
            in_specs=[SMEM] * 4 + [VMEM if last else SMEM] + [VMEM] * 6 + [ANY] * 3 + [VMEM] * len(recvs),
            out_specs=[VMEM] * len(out_shape),
            scratch_shapes=[
                pltpu.VMEM((BATCH * edge, plane), jnp.float32),
                pltpu.VMEM((BATCH * edge, plane), jnp.float32),
                pltpu.VMEM((edge, plane), jnp.bfloat16),
                pltpu.VMEM(((BATCH + own) * edge, plane), jnp.float32),
                pltpu.VMEM((8, plane), jnp.float32),
                pltpu.VMEM((plane, plane), jnp.bfloat16),
                pltpu.VMEM((plane, plane), jnp.bfloat16),
                pltpu.SemaphoreType.DMA((3,)),
            ],
            name="pairs",
        )(plist, meta, first, extra_box, side, boxes, current, gradient, left_hi, left_lo, gain, basis_hi, basis_lo, extra, *recvs)
        if not last:
            boxes, send, *sends = rest
    every = lax.all_to_all(side, ("row", "col"), 0, 0, tiled=True)
    energies = jnp.sum(every, (0, 1))[:ROUNDS] / (edge * edge * edge * devices)
    return current, energies


def solution(mesh):
    return jax.shard_map(
        local,
        mesh=mesh,
        in_specs=(
            P(("row", "col"), None, None),
            P(("row", "col"), None, None),
            P(),
            P("row", None, None),
            P("row"),
        ),
        out_specs=(P(("row", "col"), None, None), P()),
        check_vma=False,
    )
```

```python
import functools

import jax
import jax.numpy as jnp
import numpy as np
from jax import lax
from jax.experimental import pallas as pl
from jax.experimental.pallas import tpu as pltpu
from jax.sharding import PartitionSpec as P

SWEEPS = 12
ROUNDS = 2
BATCH = 4
FIELDS = 8
WORDS = 4

screen_mu = 0.1
damping = 0.5

SMEM = pl.BlockSpec(memory_space=pltpu.SMEM)
VMEM = pl.BlockSpec(memory_space=pltpu.VMEM)
ANY = pl.BlockSpec(memory_space=pl.ANY)


def split(values):
    high = values.astype(jnp.bfloat16)
    return high, (values - high.astype(jnp.float32)).astype(jnp.bfloat16)


def sine_basis(edge):
    index = np.arange(1, edge + 1)
    return np.sqrt(2.0 / (edge + 1)) * np.sin(np.pi * np.outer(index, index) / (edge + 1))


def solve_gain(edge):
    cosines = 2.0 * np.cos(np.pi * np.arange(1, edge + 1) / (edge + 1))
    eigen = 6.0 + screen_mu - (cosines[:, None, None] + cosines[None, :, None] + cosines[None, None, :])
    center, half = 6.0 + screen_mu, 6.0
    ratio = center / half
    prev = 1.0 / ratio
    gain, rest = np.zeros_like(eigen), np.ones_like(eigen)
    step = rest / center
    for _ in range(SWEEPS):
        gain = gain + step
        rest = rest - eigen * step
        coef = 1.0 / (2.0 * ratio - prev)
        step = coef * prev * step + (2.0 * coef / half) * rest
        prev = coef
    return gain.reshape(edge, edge * edge)


def dot(a, b):
    return jnp.dot(a, b, preferred_element_type=jnp.float32)


def capacity(mask, columns):
    return 2 if mask < columns // 2 else 1


def bits(word, size):
    return [(word >> b) & 1 for b in range(size)]


def owner_of(orbital, own):
    return orbital >> (own.bit_length() - 1) if own & (own - 1) == 0 else lax.div(orbital, own)


def each_pair(pairs, counts, slots, base, step):
    def owner_step(p, carry):
        def slot_step(k, carry):
            step(p, k, pairs[k, 0, p] - base, pairs[k, 1, p] - base)
            return carry

        return lax.fori_loop(0, jnp.minimum(counts[p], slots), slot_step, carry)

    lax.fori_loop(0, counts.shape[0], owner_step, 0)


def pack(columns, own, words, boxes, sends):
    for mask in range(1, columns):
        limit = capacity(mask, columns)
        rank = 0
        for b, bit in enumerate(bits(words(mask), own)):
            place = rank if limit > 1 else 0

            @pl.when((bit != 0) & (rank < limit))
            def _():
                sends[mask - 1][place] = boxes[b]

            rank = rank + bit


def need_kernel(dims, pairs, counts, phi, need, boxes, *sends):
    columns, own, slots = dims
    me = lax.axis_index("col")
    base = lax.axis_index("row") * (columns * own)

    def clear(at, carry):
        for lane in range(columns):
            need[at * columns + lane] = 0
        return carry

    lax.fori_loop(0, columns, clear, 0)

    def step(p, k, first, second):
        source = owner_of(second, own)
        key = owner_of(first, own) * columns + source
        need[key] = need[key] | (1 << (second - source * own))

    each_pair(pairs, counts, slots, base, step)
    for b in range(own):
        boxes[b] = phi[b].astype(jnp.bfloat16)
    pack(columns, own, lambda mask: need[(me ^ mask) * columns + me], boxes, sends)


def plan_kernel(dims, need, pairs, counts, offsets, boxes, table, extra_count, first, extra_mask, extra_box, unset, send, start, sem):
    columns, own, slots = dims
    del unset
    me = lax.axis_index("col")
    base = lax.axis_index("row") * (columns * own)
    head = WORDS + columns
    table[0] = 0
    extra_count[0] = 0
    extra_mask[0] = 0
    extra_box[0] = 0
    for mask in range(1, columns):
        limit = capacity(mask, columns)
        start[mask] = extra_count[0]
        table[WORDS + mask] = need[(me ^ mask) * columns + me]
        mine = bits(need[(me ^ mask) * columns + me], own)

        def most(c, carry):
            return jnp.maximum(carry, sum(bits(need[c * columns + (c ^ mask)], own)))

        longest = lax.fori_loop(0, columns, most, 0)
        for over in range(own - limit):

            @pl.when(longest > limit + over)
            def _():
                at = extra_count[0]
                extra_count[0] = at + 1
                rank, box = 0, 0
                for b, bit in enumerate(mine):
                    box = jnp.where((bit != 0) & (rank == limit + over), b, box)
                    rank = rank + bit
                extra_mask[at] = mask - 1
                extra_box[at] = box

    first[0] = jnp.where(extra_count[0] > 0, extra_mask[0] + 1, 0)
    table[1] = first[0]
    table[2] = extra_box[0]

    def sent(act):
        @pl.when(extra_count[0] > 0)
        def _():
            act(pltpu.make_async_copy(boxes.at[pl.ds(extra_box[0], 1)], send, sem))

    sent(lambda copy: copy.start())

    def step(p, k, first, second):
        @pl.when(owner_of(first, own) == me)
        def _():
            source = owner_of(second, own)
            mask = me ^ source
            place = second - source * own
            rank = sum(bits(need[me * columns + source] & ((1 << place) - 1), own))
            limit = jnp.where(mask < columns // 2, 2, 1)
            fits = rank < limit
            at = head + table[0] * FIELDS
            table[0] = table[0] + 1
            table[at] = first - me * own
            table[at + 1] = jnp.where((mask == 0) | fits, mask, columns)
            table[at + 2] = jnp.where(mask == 0, place, jnp.where(fits, rank, start[mask] + rank - limit))
            for axis in range(3):
                table[at + 3 + axis] = offsets[axis, first + base] - offsets[axis, second + base]
            opens, closes = jnp.int32(1), jnp.int32(1)
            for other in range(slots):
                same = (other < counts[p]) & (pairs[other, 0, p] - base == first)
                opens = jnp.where(same & (other < k), 0, opens)
                closes = jnp.where(same & (other > k), 0, closes)
            table[at + 6] = opens
            table[at + 7] = closes

    each_pair(pairs, counts, slots, base, step)
    sent(lambda copy: copy.wait())


def shifted(box, move):
    edge, plane = box.shape
    along_x, along_y, along_z = move
    flat = along_y * edge + along_z
    out = pltpu.roll(box, lax.rem(edge - along_x, edge), 0)
    out = pltpu.roll(out, lax.rem(plane - flat, plane), 1)
    row = lax.broadcasted_iota(jnp.int32, (edge, plane), 0) + along_x
    lane = lax.broadcasted_iota(jnp.int32, (edge, plane), 1)
    depth = (lane & (edge - 1)) + along_z
    lane = lane + (along_y * edge)
    keep = (row >= 0) & (row < edge) & (lane >= 0) & (lane < plane) & (depth >= 0) & (depth < edge)
    return jnp.where(keep, out, 0.0)


def pair_kernel(dims, table, boxes, base, gradient, left_hi, left_lo, gain, basis_hi, basis_lo, extra, *rest):
    columns, own, last = dims
    head = WORDS + columns
    side, rest = (rest[0], rest[1:]) if last else (None, rest)
    recvs, (early, out, energy), rest = rest[: columns - 1], rest[columns - 1 : columns + 2], rest[columns + 2 :]
    partner, density, source, running, total, right_hi, right_lo, sems = rest[-8:]
    edge, plane = gain.shape
    moves = ((basis_hi, right_hi), (basis_lo, right_lo))
    copies = [pltpu.make_async_copy(there, here, sems.at[at]) for at, (there, here) in enumerate(moves)]
    for copy in copies:
        copy.start()
    for b in range(own):
        out[b] = base[b] - damping * gradient[b]
    total[...] = jnp.zeros_like(total)
    count = table[0]

    def along_left(values):
        high, low = split(values)
        return dot(left_hi[...], high) + (dot(left_hi[...], low) + dot(left_lo[...], high))

    def along_right(values):
        high, low = split(values)
        both = dot(jnp.concatenate([high, low], 0), right_hi[...])
        rows = values.shape[0]
        return both[:rows] + (both[rows:] + dot(high, right_lo[...]))

    def batch_step(index, carry):
        for s in range(BATCH):
            pair = index * BATCH + s
            rows = pl.ds(s * edge, edge)

            @pl.when(pair < count)
            def _():
                at = head + pair * FIELDS
                code = table[at + 1]
                place = table[at + 2]

                @pl.when(code == 0)
                def _():
                    source[...] = boxes[place]

                for m in range(1, columns):

                    @pl.when(code == m)
                    def _():
                        source[...] = recvs[m - 1][place if capacity(m, columns) > 1 else 0]

                @pl.when((code == columns) & (place == 0))
                def _():
                    source[...] = early[0]

                @pl.when((code == columns) & (place > 0))
                def _():
                    copy = pltpu.make_async_copy(extra.at[place], source, sems.at[2])
                    copy.start()
                    copy.wait()

                other = shifted(source[...].astype(jnp.float32), (table[at + 3], table[at + 4], table[at + 5]))
                partner[rows, :] = other
                density[rows, :] = boxes[table[at]].astype(jnp.float32) * other

            @pl.when(pair >= count)
            def _():
                density[rows, :] = jnp.zeros((edge, plane), jnp.float32)

        @pl.when(index == 0)
        def _():
            for copy in copies:
                copy.wait()

        spectrum = along_right(along_left(density[...]))
        scaled = (spectrum.reshape(BATCH, edge, plane) * gain[...]).reshape(BATCH * edge, plane)
        potential = along_left(along_right(scaled))
        work = density[...] * potential
        total[...] += jnp.sum(work.reshape(BATCH * edge // 8, 8, plane), 0)
        for s in range(BATCH):
            pair = index * BATCH + s

            @pl.when(pair < count)
            def _():
                at = head + pair * FIELDS
                place = table[at]
                rows = slice(s * edge, (s + 1) * edge)
                running[rows, :] = potential[rows] * partner[rows, :]

                @pl.when(table[at + 6] == 0)
                def _():
                    running[rows, :] = running[rows, :] + partial(place)[...]

                @pl.when(table[at + 7] == 0)
                def _():
                    partial(place)[...] = running[rows, :]

                @pl.when(table[at + 7] != 0)
                def _():
                    rounded = running[rows, :].astype(jnp.bfloat16).astype(jnp.float32)
                    out[place] = out[place] - damping * rounded

        return carry

    def partial(place):
        return running.at[pl.ds(pl.multiple_of((BATCH + place) * edge, edge), edge)]

    lax.fori_loop(0, lax.div(count + BATCH - 1, BATCH), batch_step, 0)

    @pl.when(count == 0)
    def _():
        for copy in copies:
            copy.wait()

    mine = jnp.sum(total[...])
    if last:
        lane = lax.broadcasted_iota(jnp.int32, (1, 128), 1)
        row = jnp.where(lane == 0, side[:1], jnp.where(lane == 1, mine, 0.0))
        for device in range(energy.shape[0]):
            energy[device] = row
    else:
        next_boxes, send, sends = rest[0], rest[1], rest[2:-8]
        energy[...] = jnp.full(energy.shape, mine)
        for b in range(own):
            next_boxes[b] = out[b].astype(jnp.bfloat16)
        pack(columns, own, lambda mask: table[WORDS + mask], next_boxes, sends)

        @pl.when(table[1] > 0)
        def _():
            send[0] = next_boxes[table[2]]


def local(orbitals, gradient, offsets, pairs, counts):
    own, edge, plane = orbitals.shape
    columns = lax.axis_size("col")
    devices = lax.axis_size("row") * columns
    owners, slots = pairs.shape[0], pairs.shape[1]
    masks = range(1, columns)
    basis = sine_basis(edge)
    basis_hi, basis_lo = split(jnp.asarray(np.kron(basis, basis), jnp.float32))
    left_hi, left_lo = split(jnp.asarray(np.kron(np.eye(BATCH), basis), jnp.float32))
    gain = jnp.asarray(solve_gain(edge), jnp.float32)
    box_shape = jax.ShapeDtypeStruct((own, edge, plane), jnp.bfloat16)
    send_shapes = [jax.ShapeDtypeStruct((capacity(m, columns), edge, plane), jnp.bfloat16) for m in masks]
    most_extra = sum(max(own - capacity(m, columns), 0) for m in masks)
    pairs = pairs.transpose(1, 2, 0)
    offsets = offsets.T

    one_box = jax.ShapeDtypeStruct((1, edge, plane), jnp.bfloat16)

    def ints(size):
        return jax.ShapeDtypeStruct((size,), jnp.int32)

    need, boxes, *sends = pl.pallas_call(
        functools.partial(need_kernel, (columns, own, slots)),
        out_shape=[ints(columns * columns), box_shape, *send_shapes],
        in_specs=[SMEM, SMEM, VMEM],
        out_specs=[SMEM, VMEM] + [VMEM] * len(send_shapes),
        name="need",
    )(pairs, counts, orbitals)
    table, extra_count, first, extra_mask, extra_box, extra, send = pl.pallas_call(
        functools.partial(plan_kernel, (columns, own, slots)),
        out_shape=[
            ints(WORDS + columns + owners * slots * FIELDS),
            ints(1),
            ints(1),
            ints(most_extra),
            ints(most_extra),
            jax.ShapeDtypeStruct((most_extra, edge, plane), jnp.bfloat16),
            one_box,
        ],
        in_specs=[SMEM] * 4 + [ANY],
        out_specs=[SMEM] * 5 + [ANY, ANY],
        scratch_shapes=[pltpu.SMEM((columns,), jnp.int32), pltpu.SemaphoreType.DMA],
        name="plan",
    )(need, pairs, counts, offsets, boxes)

    def hop(mask, values):
        return lax.ppermute(values, "col", [(c, c ^ mask) for c in range(columns)])

    def exchange(boxes, sends, send, extra):
        got = {m: hop(m, sends[m - 1]) for m in reversed(masks)}
        early = lax.switch(first[0], [lambda box: box] + [functools.partial(hop, m) for m in masks], send)

        def one_more(at, extra):
            box = lax.dynamic_index_in_dim(boxes, extra_box[at], 0, True)
            box = lax.switch(extra_mask[at], [functools.partial(hop, m) for m in masks], box)
            return lax.dynamic_update_slice_in_dim(extra, box, at, 0)

        extra = lax.fori_loop(1, extra_count[0], one_more, extra)
        return [got[m] for m in masks] + [early], extra

    current = orbitals
    side = None
    for round_idx in range(ROUNDS):
        last = round_idx == ROUNDS - 1
        recvs, extra = exchange(boxes, sends, send, extra)
        before = [side] if last else []
        energy_shape = (devices, 1, 128) if last else (8, 128)
        out_shape = [jax.ShapeDtypeStruct((own, edge, plane), jnp.float32), jax.ShapeDtypeStruct(energy_shape, jnp.float32)]
        if not last:
            out_shape += [box_shape, one_box, *send_shapes]
        current, side, *rest = pl.pallas_call(
            functools.partial(pair_kernel, (columns, own, last)),
            out_shape=out_shape,
            in_specs=[SMEM] + [VMEM] * 6 + [ANY] * 3 + [VMEM] * (len(recvs) + len(before)),
            out_specs=[VMEM] * len(out_shape),
            scratch_shapes=[
                pltpu.VMEM((BATCH * edge, plane), jnp.float32),
                pltpu.VMEM((BATCH * edge, plane), jnp.float32),
                pltpu.VMEM((edge, plane), jnp.bfloat16),
                pltpu.VMEM(((BATCH + own) * edge, plane), jnp.float32),
                pltpu.VMEM((8, plane), jnp.float32),
                pltpu.VMEM((plane, plane), jnp.bfloat16),
                pltpu.VMEM((plane, plane), jnp.bfloat16),
                pltpu.SemaphoreType.DMA((3,)),
            ],
            name="pairs",
        )(table, boxes, current, gradient, left_hi, left_lo, gain, basis_hi, basis_lo, extra, *before, *recvs)
        if not last:
            boxes, send, *sends = rest
    every = lax.all_to_all(side, ("row", "col"), 0, 0, tiled=True)
    energies = jnp.sum(every, (0, 1))[:ROUNDS] / (edge * edge * edge * devices)
    return current, energies


def solution(mesh):
    return jax.shard_map(
        local,
        mesh=mesh,
        in_specs=(
            P(("row", "col"), None, None),
            P(("row", "col"), None, None),
            P(),
            P("row", None, None),
            P("row"),
        ),
        out_specs=(P(("row", "col"), None, None), P()),
        check_vma=False,
    )
```

```python
import functools

import jax
import jax.numpy as jnp
import numpy as np
from jax import lax
from jax.experimental import pallas as pl
from jax.experimental.pallas import tpu as pltpu
from jax.sharding import PartitionSpec as P

SWEEPS = 12
ROUNDS = 2
BATCH = 4
FIELDS = 8
WORDS = 4

screen_mu = 0.1
damping = 0.5

SMEM = pl.BlockSpec(memory_space=pltpu.SMEM)
VMEM = pl.BlockSpec(memory_space=pltpu.VMEM)
ANY = pl.BlockSpec(memory_space=pl.ANY)


def split(values):
    high = values.astype(jnp.bfloat16)
    return high, (values - high.astype(jnp.float32)).astype(jnp.bfloat16)


def sine_basis(edge):
    index = np.arange(1, edge + 1)
    return np.sqrt(2.0 / (edge + 1)) * np.sin(np.pi * np.outer(index, index) / (edge + 1))


def solve_gain(edge):
    cosines = 2.0 * np.cos(np.pi * np.arange(1, edge + 1) / (edge + 1))
    eigen = 6.0 + screen_mu - (cosines[:, None, None] + cosines[None, :, None] + cosines[None, None, :])
    center, half = 6.0 + screen_mu, 6.0
    ratio = center / half
    prev = 1.0 / ratio
    gain, rest = np.zeros_like(eigen), np.ones_like(eigen)
    step = rest / center
    for _ in range(SWEEPS):
        gain = gain + step
        rest = rest - eigen * step
        coef = 1.0 / (2.0 * ratio - prev)
        step = coef * prev * step + (2.0 * coef / half) * rest
        prev = coef
    return gain.reshape(edge, edge * edge)


def dot(a, b):
    return jnp.dot(a, b, preferred_element_type=jnp.float32)


def capacity(mask, columns):
    return 2 if mask < columns // 2 else 1


def bits(word, size):
    return [(word >> b) & 1 for b in range(size)]


def owner_of(orbital, own):
    return orbital >> (own.bit_length() - 1) if own & (own - 1) == 0 else lax.div(orbital, own)


def each_pair(pairs, counts, slots, base, step):
    def owner_step(p, carry):
        def slot_step(k, carry):
            step(p, k, pairs[k, 0, p] - base, pairs[k, 1, p] - base)
            return carry

        return lax.fori_loop(0, jnp.minimum(counts[p], slots), slot_step, carry)

    lax.fori_loop(0, counts.shape[0], owner_step, 0)


def pack(columns, own, words, boxes, sends):
    for mask in range(1, columns):
        limit = capacity(mask, columns)
        rank = 0
        for b, bit in enumerate(bits(words(mask), own)):
            place = rank if limit > 1 else 0

            @pl.when((bit != 0) & (rank < limit))
            def _():
                sends[mask - 1][place] = boxes[b]

            rank = rank + bit


def need_kernel(dims, pairs, counts, phi, need, boxes, *sends):
    columns, own, slots = dims
    me = lax.axis_index("col")
    base = lax.axis_index("row") * (columns * own)

    def clear(at, carry):
        for lane in range(columns):
            need[at * columns + lane] = 0
        return carry

    lax.fori_loop(0, columns, clear, 0)

    def step(p, k, first, second):
        source = owner_of(second, own)
        key = owner_of(first, own) * columns + source
        need[key] = need[key] | (1 << (second - source * own))

    each_pair(pairs, counts, slots, base, step)
    for b in range(own):
        boxes[b] = phi[b].astype(jnp.bfloat16)
    pack(columns, own, lambda mask: need[(me ^ mask) * columns + me], boxes, sends)


def plan_kernel(dims, need, pairs, counts, offsets, boxes, table, extra_count, first, extra_mask, extra_box, unset, send, start, sem):
    columns, own, slots = dims
    del unset
    me = lax.axis_index("col")
    base = lax.axis_index("row") * (columns * own)
    head = WORDS + columns
    table[0] = 0
    extra_count[0] = 0
    extra_mask[0] = 0
    extra_box[0] = 0
    for mask in range(1, columns):
        limit = capacity(mask, columns)
        start[mask] = extra_count[0]
        table[WORDS + mask] = need[(me ^ mask) * columns + me]
        mine = bits(need[(me ^ mask) * columns + me], own)

        def most(c, carry):
            return jnp.maximum(carry, sum(bits(need[c * columns + (c ^ mask)], own)))

        longest = lax.fori_loop(0, columns, most, 0)
        for over in range(own - limit):

            @pl.when(longest > limit + over)
            def _():
                at = extra_count[0]
                extra_count[0] = at + 1
                rank, box = 0, 0
                for b, bit in enumerate(mine):
                    box = jnp.where((bit != 0) & (rank == limit + over), b, box)
                    rank = rank + bit
                extra_mask[at] = mask - 1
                extra_box[at] = box

    first[0] = jnp.where(extra_count[0] > 0, extra_mask[0] + 1, 0)
    table[1] = first[0]
    table[2] = extra_box[0]

    def sent(act):
        @pl.when(extra_count[0] > 0)
        def _():
            act(pltpu.make_async_copy(boxes.at[pl.ds(extra_box[0], 1)], send, sem))

    sent(lambda copy: copy.start())

    def step(p, k, first, second):
        @pl.when(owner_of(first, own) == me)
        def _():
            source = owner_of(second, own)
            mask = me ^ source
            place = second - source * own
            rank = sum(bits(need[me * columns + source] & ((1 << place) - 1), own))
            limit = jnp.where(mask < columns // 2, 2, 1)
            fits = rank < limit
            at = head + table[0] * FIELDS
            table[0] = table[0] + 1
            table[at] = first - me * own
            table[at + 1] = jnp.where((mask == 0) | fits, mask, columns)
            table[at + 2] = jnp.where(mask == 0, place, jnp.where(fits, rank, start[mask] + rank - limit))
            for axis in range(3):
                table[at + 3 + axis] = offsets[axis, first + base] - offsets[axis, second + base]
            opens, closes = jnp.int32(1), jnp.int32(1)
            for other in range(slots):
                same = (other < counts[p]) & (pairs[other, 0, p] - base == first)
                opens = jnp.where(same & (other < k), 0, opens)
                closes = jnp.where(same & (other > k), 0, closes)
            table[at + 6] = opens
            table[at + 7] = closes

    each_pair(pairs, counts, slots, base, step)
    sent(lambda copy: copy.wait())


def shifted(box, move):
    edge, plane = box.shape
    along_x, along_y, along_z = move
    flat = along_y * edge + along_z
    out = pltpu.roll(box, lax.rem(edge - along_x, edge), 0)
    out = pltpu.roll(out, lax.rem(plane - flat, plane), 1)
    row = lax.broadcasted_iota(jnp.int32, (edge, plane), 0) + along_x
    lane = lax.broadcasted_iota(jnp.int32, (edge, plane), 1)
    depth = (lane & (edge - 1)) + along_z
    lane = lane + (along_y * edge)
    keep = (row >= 0) & (row < edge) & (lane >= 0) & (lane < plane) & (depth >= 0) & (depth < edge)
    return jnp.where(keep, out, 0.0)


def pair_kernel(dims, table, boxes, base, gradient, *rest):
    columns, own, last = dims
    head = WORDS + columns
    constants, extra, rest = rest[:5], rest[5], rest[6:]
    side, rest = (rest[0], rest[1:]) if last else (None, rest)
    recvs, (early, out, energy), rest = rest[: columns - 1], rest[columns - 1 : columns + 2], rest[columns + 2 :]
    partner, density, source, running, total, right_hi, right_lo, left_hi, left_lo, gain, sems = rest[-11:]
    edge, plane = gain.shape
    here = [left_hi, left_lo, gain, right_hi, right_lo]
    copies = [pltpu.make_async_copy(constants[at], here[at], sems.at[at]) for at in range(5)]
    for copy in copies:
        copy.start()
    for b in range(own):
        out[b] = base[b] - damping * gradient[b]
    total[...] = jnp.zeros_like(total)
    count = table[0]

    def along_left(values):
        high, low = split(values)
        return dot(left_hi[...], high) + (dot(left_hi[...], low) + dot(left_lo[...], high))

    def along_right(values):
        high, low = split(values)
        both = dot(jnp.concatenate([high, low], 0), right_hi[...])
        rows = values.shape[0]
        return both[:rows] + (both[rows:] + dot(high, right_lo[...]))

    def batch_step(index, carry):
        for s in range(BATCH):
            pair = index * BATCH + s
            rows = pl.ds(s * edge, edge)

            @pl.when(pair < count)
            def _():
                at = head + pair * FIELDS
                code = table[at + 1]
                place = table[at + 2]

                @pl.when(code == 0)
                def _():
                    source[...] = boxes[place]

                for m in range(1, columns):

                    @pl.when(code == m)
                    def _():
                        source[...] = recvs[m - 1][place if capacity(m, columns) > 1 else 0]

                @pl.when((code == columns) & (place == 0))
                def _():
                    source[...] = early[0]

                @pl.when((code == columns) & (place > 0))
                def _():
                    copy = pltpu.make_async_copy(extra.at[place], source, sems.at[5])
                    copy.start()
                    copy.wait()

                other = shifted(source[...].astype(jnp.float32), (table[at + 3], table[at + 4], table[at + 5]))
                partner[rows, :] = other
                density[rows, :] = boxes[table[at]].astype(jnp.float32) * other

            @pl.when(pair >= count)
            def _():
                density[rows, :] = jnp.zeros((edge, plane), jnp.float32)

        @pl.when(index == 0)
        def _():
            for copy in copies:
                copy.wait()

        spectrum = along_right(along_left(density[...]))
        scaled = (spectrum.reshape(BATCH, edge, plane) * gain[...]).reshape(BATCH * edge, plane)
        potential = along_left(along_right(scaled))
        work = density[...] * potential
        total[...] += jnp.sum(work.reshape(BATCH * edge // 8, 8, plane), 0)
        for s in range(BATCH):
            pair = index * BATCH + s

            @pl.when(pair < count)
            def _():
                at = head + pair * FIELDS
                place = table[at]
                rows = slice(s * edge, (s + 1) * edge)
                running[rows, :] = potential[rows] * partner[rows, :]

                @pl.when(table[at + 6] == 0)
                def _():
                    running[rows, :] = running[rows, :] + partial(place)[...]

                @pl.when(table[at + 7] == 0)
                def _():
                    partial(place)[...] = running[rows, :]

                @pl.when(table[at + 7] != 0)
                def _():
                    rounded = running[rows, :].astype(jnp.bfloat16).astype(jnp.float32)
                    out[place] = out[place] - damping * rounded

        return carry

    def partial(place):
        return running.at[pl.ds(pl.multiple_of((BATCH + place) * edge, edge), edge)]

    lax.fori_loop(0, lax.div(count + BATCH - 1, BATCH), batch_step, 0)

    @pl.when(count == 0)
    def _():
        for copy in copies:
            copy.wait()

    mine = jnp.sum(total[...])
    if last:
        lane = lax.broadcasted_iota(jnp.int32, (1, 128), 1)
        row = jnp.where(lane == 0, side[:1], jnp.where(lane == 1, mine, 0.0))
        for device in range(energy.shape[0]):
            energy[device] = row
    else:
        next_boxes, send, sends = rest[0], rest[1], rest[2:-11]
        energy[...] = jnp.full(energy.shape, mine)
        for b in range(own):
            next_boxes[b] = out[b].astype(jnp.bfloat16)
        pack(columns, own, lambda mask: table[WORDS + mask], next_boxes, sends)

        @pl.when(table[1] > 0)
        def _():
            send[0] = next_boxes[table[2]]


def local(orbitals, gradient, offsets, pairs, counts):
    own, edge, plane = orbitals.shape
    columns = lax.axis_size("col")
    devices = lax.axis_size("row") * columns
    owners, slots = pairs.shape[0], pairs.shape[1]
    masks = range(1, columns)
    basis = sine_basis(edge)
    basis_hi, basis_lo = split(jnp.asarray(np.kron(basis, basis), jnp.float32))
    left_hi, left_lo = split(jnp.asarray(np.kron(np.eye(BATCH), basis), jnp.float32))
    gain = jnp.asarray(solve_gain(edge), jnp.float32)
    box_shape = jax.ShapeDtypeStruct((own, edge, plane), jnp.bfloat16)
    send_shapes = [jax.ShapeDtypeStruct((capacity(m, columns), edge, plane), jnp.bfloat16) for m in masks]
    most_extra = sum(max(own - capacity(m, columns), 0) for m in masks)
    pairs = pairs.transpose(1, 2, 0)
    offsets = offsets.T

    one_box = jax.ShapeDtypeStruct((1, edge, plane), jnp.bfloat16)

    def ints(size):
        return jax.ShapeDtypeStruct((size,), jnp.int32)

    need, boxes, *sends = pl.pallas_call(
        functools.partial(need_kernel, (columns, own, slots)),
        out_shape=[ints(columns * columns), box_shape, *send_shapes],
        in_specs=[SMEM, SMEM, VMEM],
        out_specs=[SMEM, VMEM] + [VMEM] * len(send_shapes),
        name="need",
    )(pairs, counts, orbitals)
    table, extra_count, first, extra_mask, extra_box, extra, send = pl.pallas_call(
        functools.partial(plan_kernel, (columns, own, slots)),
        out_shape=[
            ints(WORDS + columns + owners * slots * FIELDS),
            ints(1),
            ints(1),
            ints(most_extra),
            ints(most_extra),
            jax.ShapeDtypeStruct((most_extra, edge, plane), jnp.bfloat16),
            one_box,
        ],
        in_specs=[SMEM] * 4 + [ANY],
        out_specs=[SMEM] * 5 + [ANY, ANY],
        scratch_shapes=[pltpu.SMEM((columns,), jnp.int32), pltpu.SemaphoreType.DMA],
        name="plan",
    )(need, pairs, counts, offsets, boxes)

    def hop(mask, values):
        return lax.ppermute(values, "col", [(c, c ^ mask) for c in range(columns)])

    def exchange(boxes, sends, send, extra):
        got = {m: hop(m, sends[m - 1]) for m in reversed(masks)}
        early = lax.switch(first[0], [lambda box: box] + [functools.partial(hop, m) for m in masks], send)

        def one_more(at, extra):
            box = lax.dynamic_index_in_dim(boxes, extra_box[at], 0, True)
            box = lax.switch(extra_mask[at], [functools.partial(hop, m) for m in masks], box)
            return lax.dynamic_update_slice_in_dim(extra, box, at, 0)

        extra = lax.fori_loop(1, extra_count[0], one_more, extra)
        return [got[m] for m in masks] + [early], extra

    current = orbitals
    side = None
    for round_idx in range(ROUNDS):
        last = round_idx == ROUNDS - 1
        recvs, extra = exchange(boxes, sends, send, extra)
        before = [side] if last else []
        energy_shape = (devices, 1, 128) if last else (8, 128)
        out_shape = [jax.ShapeDtypeStruct((own, edge, plane), jnp.float32), jax.ShapeDtypeStruct(energy_shape, jnp.float32)]
        if not last:
            out_shape += [box_shape, one_box, *send_shapes]
        current, side, *rest = pl.pallas_call(
            functools.partial(pair_kernel, (columns, own, last)),
            out_shape=out_shape,
            in_specs=[SMEM] + [VMEM] * 3 + [ANY] * 6 + [VMEM] * (len(recvs) + len(before)),
            out_specs=[VMEM] * len(out_shape),
            scratch_shapes=[
                pltpu.VMEM((BATCH * edge, plane), jnp.float32),
                pltpu.VMEM((BATCH * edge, plane), jnp.float32),
                pltpu.VMEM((edge, plane), jnp.bfloat16),
                pltpu.VMEM(((BATCH + own) * edge, plane), jnp.float32),
                pltpu.VMEM((8, plane), jnp.float32),
                pltpu.VMEM((plane, plane), jnp.bfloat16),
                pltpu.VMEM((plane, plane), jnp.bfloat16),
                pltpu.VMEM(left_hi.shape, jnp.bfloat16),
                pltpu.VMEM(left_lo.shape, jnp.bfloat16),
                pltpu.VMEM(gain.shape, jnp.float32),
                pltpu.SemaphoreType.DMA((6,)),
            ],
            name="pairs",
        )(table, boxes, current, gradient, left_hi, left_lo, gain, basis_hi, basis_lo, extra, *before, *recvs)
        if not last:
            boxes, send, *sends = rest
    every = lax.all_to_all(side, ("row", "col"), 0, 0, tiled=True)
    energies = jnp.sum(every, (0, 1))[:ROUNDS] / (edge * edge * edge * devices)
    return current, energies


def solution(mesh):
    return jax.shard_map(
        local,
        mesh=mesh,
        in_specs=(
            P(("row", "col"), None, None),
            P(("row", "col"), None, None),
            P(),
            P("row", None, None),
            P("row"),
        ),
        out_specs=(P(("row", "col"), None, None), P()),
        check_vma=False,
    )
```

```python
import functools

import jax
import jax.numpy as jnp
import numpy as np
from jax import lax
from jax.experimental import pallas as pl
from jax.experimental.pallas import tpu as pltpu
from jax.sharding import PartitionSpec as P

SWEEPS = 12
ROUNDS = 2
BATCH = 4
FIELDS = 8
WORDS = 4

screen_mu = 0.1
damping = 0.5

SMEM = pl.BlockSpec(memory_space=pltpu.SMEM)
VMEM = pl.BlockSpec(memory_space=pltpu.VMEM)
ANY = pl.BlockSpec(memory_space=pl.ANY)


def split(values):
    high = values.astype(jnp.bfloat16)
    return high, (values - high.astype(jnp.float32)).astype(jnp.bfloat16)


def sine_basis(edge):
    index = np.arange(1, edge + 1)
    return np.sqrt(2.0 / (edge + 1)) * np.sin(np.pi * np.outer(index, index) / (edge + 1))


def solve_gain(edge):
    cosines = 2.0 * np.cos(np.pi * np.arange(1, edge + 1) / (edge + 1))
    eigen = 6.0 + screen_mu - (cosines[:, None, None] + cosines[None, :, None] + cosines[None, None, :])
    center, half = 6.0 + screen_mu, 6.0
    ratio = center / half
    prev = 1.0 / ratio
    gain, rest = np.zeros_like(eigen), np.ones_like(eigen)
    step = rest / center
    for _ in range(SWEEPS):
        gain = gain + step
        rest = rest - eigen * step
        coef = 1.0 / (2.0 * ratio - prev)
        step = coef * prev * step + (2.0 * coef / half) * rest
        prev = coef
    return gain.reshape(edge, edge * edge)


def dot(a, b):
    return jnp.dot(a, b, preferred_element_type=jnp.float32)


def capacity(mask, columns):
    return 2 if mask < columns // 2 else 1


def bits(word, size):
    return [(word >> b) & 1 for b in range(size)]


def owner_of(orbital, own):
    return orbital >> (own.bit_length() - 1) if own & (own - 1) == 0 else lax.div(orbital, own)


def each_pair(pairs, counts, slots, base, step):
    def owner_step(p, carry):
        def slot_step(k, carry):
            step(p, k, pairs[k, 0, p] - base, pairs[k, 1, p] - base)
            return carry

        return lax.fori_loop(0, jnp.minimum(counts[p], slots), slot_step, carry)

    lax.fori_loop(0, counts.shape[0], owner_step, 0)


def pack(columns, own, words, boxes, sends):
    for mask in range(1, columns):
        limit = capacity(mask, columns)
        rank = 0
        for b, bit in enumerate(bits(words(mask), own)):
            place = rank if limit > 1 else 0

            @pl.when((bit != 0) & (rank < limit))
            def _():
                sends[mask - 1][place] = boxes[b]

            rank = rank + bit


def need_kernel(dims, pairs, counts, phi, need, boxes, *sends):
    columns, own, slots = dims
    me = lax.axis_index("col")
    base = lax.axis_index("row") * (columns * own)

    def clear(at, carry):
        for lane in range(columns):
            need[at * columns + lane] = 0
        return carry

    lax.fori_loop(0, columns, clear, 0)

    def step(p, k, first, second):
        source = owner_of(second, own)
        key = owner_of(first, own) * columns + source
        need[key] = need[key] | (1 << (second - source * own))

    each_pair(pairs, counts, slots, base, step)
    for b in range(own):
        boxes[b] = phi[b].astype(jnp.bfloat16)
    pack(columns, own, lambda mask: need[(me ^ mask) * columns + me], boxes, sends)


def plan_kernel(dims, need, pairs, counts, offsets, boxes, table, extra_count, first, extra_mask, extra_box, unset, send, start, sem):
    columns, own, slots = dims
    del unset
    me = lax.axis_index("col")
    base = lax.axis_index("row") * (columns * own)
    head = WORDS + columns
    table[0] = 0
    extra_count[0] = 0
    extra_mask[0] = 0
    extra_box[0] = 0
    for mask in range(1, columns):
        limit = capacity(mask, columns)
        start[mask] = extra_count[0]
        table[WORDS + mask] = need[(me ^ mask) * columns + me]
        mine = bits(need[(me ^ mask) * columns + me], own)

        def most(c, carry):
            return jnp.maximum(carry, sum(bits(need[c * columns + (c ^ mask)], own)))

        longest = lax.fori_loop(0, columns, most, 0)
        for over in range(own - limit):

            @pl.when(longest > limit + over)
            def _():
                at = extra_count[0]
                extra_count[0] = at + 1
                rank, box = 0, 0
                for b, bit in enumerate(mine):
                    box = jnp.where((bit != 0) & (rank == limit + over), b, box)
                    rank = rank + bit
                extra_mask[at] = mask - 1
                extra_box[at] = box

    first[0] = jnp.where(extra_count[0] > 0, extra_mask[0] + 1, 0)
    table[1] = first[0]
    table[2] = extra_box[0]

    def sent(act):
        @pl.when(extra_count[0] > 0)
        def _():
            act(pltpu.make_async_copy(boxes.at[pl.ds(extra_box[0], 1)], send, sem))

    sent(lambda copy: copy.start())

    def step(p, k, first, second):
        @pl.when(owner_of(first, own) == me)
        def _():
            source = owner_of(second, own)
            mask = me ^ source
            place = second - source * own
            rank = sum(bits(need[me * columns + source] & ((1 << place) - 1), own))
            limit = jnp.where(mask < columns // 2, 2, 1)
            fits = rank < limit
            at = head + table[0] * FIELDS
            table[0] = table[0] + 1
            table[at] = first - me * own
            table[at + 1] = jnp.where((mask == 0) | fits, mask, columns)
            table[at + 2] = jnp.where(mask == 0, place, jnp.where(fits, rank, start[mask] + rank - limit))
            for axis in range(3):
                table[at + 3 + axis] = offsets[axis, first + base] - offsets[axis, second + base]
            opens, closes = jnp.int32(1), jnp.int32(1)
            for other in range(slots):
                same = (other < counts[p]) & (pairs[other, 0, p] - base == first)
                opens = jnp.where(same & (other < k), 0, opens)
                closes = jnp.where(same & (other > k), 0, closes)
            table[at + 6] = opens
            table[at + 7] = closes

    each_pair(pairs, counts, slots, base, step)
    sent(lambda copy: copy.wait())


def shifted(box, move):
    edge, plane = box.shape
    along_x, along_y, along_z = move
    flat = along_y * edge + along_z
    out = pltpu.roll(box, lax.rem(edge - along_x, edge), 0)
    out = pltpu.roll(out, lax.rem(plane - flat, plane), 1)
    row = lax.broadcasted_iota(jnp.int32, (edge, plane), 0) + along_x
    lane = lax.broadcasted_iota(jnp.int32, (edge, plane), 1)
    depth = (lane & (edge - 1)) + along_z
    lane = lane + (along_y * edge)
    keep = (row >= 0) & (row < edge) & (lane >= 0) & (lane < plane) & (depth >= 0) & (depth < edge)
    return jnp.where(keep, out, 0.0)


def pair_kernel(dims, table, boxes, base, gradient, *rest):
    columns, own, last = dims
    head = WORDS + columns
    constants, extra, rest = rest[:5], rest[5], rest[6:]
    side, rest = (rest[0], rest[1:]) if last else (None, rest)
    recvs, (early, out, energy), rest = rest[: columns - 1], rest[columns - 1 : columns + 2], rest[columns + 2 :]
    partner, density, source, running, total, right_hi, right_lo, left_hi, left_lo, gain, sems = rest[-11:]
    edge, plane = gain.shape
    here = [left_hi, left_lo, gain, right_hi, right_lo]
    copies = [pltpu.make_async_copy(constants[at], here[at], sems.at[at]) for at in range(5)]
    for copy in copies:
        copy.start()
    for b in range(own):
        out[b] = base[b] - damping * gradient[b]
    total[...] = jnp.zeros_like(total)
    count = table[0]

    def along_left(values):
        high, low = split(values)
        rows = values.shape[0]
        main, fine = left_hi[:rows, :rows], left_lo[:rows, :rows]
        return dot(main, high) + (dot(main, low) + dot(fine, high))

    def along_right(values):
        high, low = split(values)
        both = dot(jnp.concatenate([high, low], 0), right_hi[...])
        rows = values.shape[0]
        return both[:rows] + (both[rows:] + dot(high, right_lo[...]))

    def batch_step(index, carry, size=BATCH):
        for s in range(size):
            pair = index * BATCH + s
            rows = pl.ds(s * edge, edge)

            @pl.when(pair < count)
            def _():
                at = head + pair * FIELDS
                code = table[at + 1]
                place = table[at + 2]

                @pl.when(code == 0)
                def _():
                    source[...] = boxes[place]

                for m in range(1, columns):

                    @pl.when(code == m)
                    def _():
                        source[...] = recvs[m - 1][place if capacity(m, columns) > 1 else 0]

                @pl.when((code == columns) & (place == 0))
                def _():
                    source[...] = early[0]

                @pl.when((code == columns) & (place > 0))
                def _():
                    copy = pltpu.make_async_copy(extra.at[place], source, sems.at[5])
                    copy.start()
                    copy.wait()

                other = shifted(source[...].astype(jnp.float32), (table[at + 3], table[at + 4], table[at + 5]))
                partner[rows, :] = other
                density[rows, :] = boxes[table[at]].astype(jnp.float32) * other

            @pl.when(pair >= count)
            def _():
                density[rows, :] = jnp.zeros((edge, plane), jnp.float32)

        @pl.when(index == 0)
        def _():
            for copy in copies:
                copy.wait()

        spectrum = along_right(along_left(density[: size * edge, :]))
        scaled = (spectrum.reshape(size, edge, plane) * gain[...]).reshape(size * edge, plane)
        potential = along_left(along_right(scaled))
        work = density[: size * edge, :] * potential
        total[...] += jnp.sum(work.reshape(size * edge // 8, 8, plane), 0)
        for s in range(size):
            pair = index * BATCH + s

            @pl.when(pair < count)
            def _():
                at = head + pair * FIELDS
                place = table[at]
                rows = slice(s * edge, (s + 1) * edge)
                running[rows, :] = potential[rows] * partner[rows, :]

                @pl.when(table[at + 6] == 0)
                def _():
                    running[rows, :] = running[rows, :] + partial(place)[...]

                @pl.when(table[at + 7] == 0)
                def _():
                    partial(place)[...] = running[rows, :]

                @pl.when(table[at + 7] != 0)
                def _():
                    rounded = running[rows, :].astype(jnp.bfloat16).astype(jnp.float32)
                    out[place] = out[place] - damping * rounded

        return carry

    def partial(place):
        return running.at[pl.ds(pl.multiple_of((BATCH + place) * edge, edge), edge)]

    whole = lax.div(count, BATCH)
    left_over = count - whole * BATCH
    small = (left_over > 0) & (left_over <= BATCH // 2)
    batches = whole + ((left_over > 0) & jnp.logical_not(small)).astype(jnp.int32)
    lax.fori_loop(0, batches, batch_step, 0)

    @pl.when(small)
    def _():
        batch_step(whole, 0, BATCH // 2)


    @pl.when(count == 0)
    def _():
        for copy in copies:
            copy.wait()

    mine = jnp.sum(total[...])
    if last:
        lane = lax.broadcasted_iota(jnp.int32, (1, 128), 1)
        row = jnp.where(lane == 0, side[:1], jnp.where(lane == 1, mine, 0.0))
        for device in range(energy.shape[0]):
            energy[device] = row
    else:
        next_boxes, send, sends = rest[0], rest[1], rest[2:-11]
        energy[...] = jnp.full(energy.shape, mine)
        for b in range(own):
            next_boxes[b] = out[b].astype(jnp.bfloat16)
        pack(columns, own, lambda mask: table[WORDS + mask], next_boxes, sends)

        @pl.when(table[1] > 0)
        def _():
            send[0] = next_boxes[table[2]]


def local(orbitals, gradient, offsets, pairs, counts):
    own, edge, plane = orbitals.shape
    columns = lax.axis_size("col")
    devices = lax.axis_size("row") * columns
    owners, slots = pairs.shape[0], pairs.shape[1]
    masks = range(1, columns)
    basis = sine_basis(edge)
    basis_hi, basis_lo = split(jnp.asarray(np.kron(basis, basis), jnp.float32))
    left_hi, left_lo = split(jnp.asarray(np.kron(np.eye(BATCH), basis), jnp.float32))
    gain = jnp.asarray(solve_gain(edge), jnp.float32)
    box_shape = jax.ShapeDtypeStruct((own, edge, plane), jnp.bfloat16)
    send_shapes = [jax.ShapeDtypeStruct((capacity(m, columns), edge, plane), jnp.bfloat16) for m in masks]
    most_extra = sum(max(own - capacity(m, columns), 0) for m in masks)
    pairs = pairs.transpose(1, 2, 0)
    offsets = offsets.T

    one_box = jax.ShapeDtypeStruct((1, edge, plane), jnp.bfloat16)

    def ints(size):
        return jax.ShapeDtypeStruct((size,), jnp.int32)

    need, boxes, *sends = pl.pallas_call(
        functools.partial(need_kernel, (columns, own, slots)),
        out_shape=[ints(columns * columns), box_shape, *send_shapes],
        in_specs=[SMEM, SMEM, VMEM],
        out_specs=[SMEM, VMEM] + [VMEM] * len(send_shapes),
        name="need",
    )(pairs, counts, orbitals)
    table, extra_count, first, extra_mask, extra_box, extra, send = pl.pallas_call(
        functools.partial(plan_kernel, (columns, own, slots)),
        out_shape=[
            ints(WORDS + columns + owners * slots * FIELDS),
            ints(1),
            ints(1),
            ints(most_extra),
            ints(most_extra),
            jax.ShapeDtypeStruct((most_extra, edge, plane), jnp.bfloat16),
            one_box,
        ],
        in_specs=[SMEM] * 4 + [ANY],
        out_specs=[SMEM] * 5 + [ANY, ANY],
        scratch_shapes=[pltpu.SMEM((columns,), jnp.int32), pltpu.SemaphoreType.DMA],
        name="plan",
    )(need, pairs, counts, offsets, boxes)

    def hop(mask, values):
        return lax.ppermute(values, "col", [(c, c ^ mask) for c in range(columns)])

    def exchange(boxes, sends, send, extra):
        got = {m: hop(m, sends[m - 1]) for m in reversed(masks)}
        early = lax.switch(first[0], [lambda box: box] + [functools.partial(hop, m) for m in masks], send)

        def one_more(at, extra):
            box = lax.dynamic_index_in_dim(boxes, extra_box[at], 0, True)
            box = lax.switch(extra_mask[at], [functools.partial(hop, m) for m in masks], box)
            return lax.dynamic_update_slice_in_dim(extra, box, at, 0)

        extra = lax.fori_loop(1, extra_count[0], one_more, extra)
        return [got[m] for m in masks] + [early], extra

    current = orbitals
    side = None
    for round_idx in range(ROUNDS):
        last = round_idx == ROUNDS - 1
        recvs, extra = exchange(boxes, sends, send, extra)
        before = [side] if last else []
        energy_shape = (devices, 1, 128) if last else (8, 128)
        out_shape = [jax.ShapeDtypeStruct((own, edge, plane), jnp.float32), jax.ShapeDtypeStruct(energy_shape, jnp.float32)]
        if not last:
            out_shape += [box_shape, one_box, *send_shapes]
        current, side, *rest = pl.pallas_call(
            functools.partial(pair_kernel, (columns, own, last)),
            out_shape=out_shape,
            in_specs=[SMEM] + [VMEM] * 3 + [ANY] * 6 + [VMEM] * (len(recvs) + len(before)),
            out_specs=[VMEM] * len(out_shape),
            scratch_shapes=[
                pltpu.VMEM((BATCH * edge, plane), jnp.float32),
                pltpu.VMEM((BATCH * edge, plane), jnp.float32),
                pltpu.VMEM((edge, plane), jnp.bfloat16),
                pltpu.VMEM(((BATCH + own) * edge, plane), jnp.float32),
                pltpu.VMEM((8, plane), jnp.float32),
                pltpu.VMEM((plane, plane), jnp.bfloat16),
                pltpu.VMEM((plane, plane), jnp.bfloat16),
                pltpu.VMEM(left_hi.shape, jnp.bfloat16),
                pltpu.VMEM(left_lo.shape, jnp.bfloat16),
                pltpu.VMEM(gain.shape, jnp.float32),
                pltpu.SemaphoreType.DMA((6,)),
            ],
            name="pairs",
        )(table, boxes, current, gradient, left_hi, left_lo, gain, basis_hi, basis_lo, extra, *before, *recvs)
        if not last:
            boxes, send, *sends = rest
    every = lax.all_to_all(side, ("row", "col"), 0, 0, tiled=True)
    energies = jnp.sum(every, (0, 1))[:ROUNDS] / (edge * edge * edge * devices)
    return current, energies


def solution(mesh):
    return jax.shard_map(
        local,
        mesh=mesh,
        in_specs=(
            P(("row", "col"), None, None),
            P(("row", "col"), None, None),
            P(),
            P("row", None, None),
            P("row"),
        ),
        out_specs=(P(("row", "col"), None, None), P()),
        check_vma=False,
    )
```
